512 devices in a mesh: clip: 16 (over x, y), seq: 32 (over z, core).
Axes of the slice: x: 4, y: 4, z: 16, core: 2. Of those that a mesh axis runs over, the one named last changes fastest.
Arguments:
- enc_rows: bfloat16 [65536, 3520], P(('clip', 'seq')), parts along dimension 0, may hold values from -30 to 30
- vis_count: int32 [512], P('clip'), parts along dimension 0, may hold values from 0 to 128, as said below
- vis_dest: int32 [512], P('clip'), parts along dimension 0, may hold values from 0 to 31, as said below
- vis_pos: int32 [65536], P('clip'), parts along dimension 0, may hold values from 0 to 32767, as said below
- kept_pos: int32 [49152], P(('clip', 'seq')), parts along dimension 0, may hold values from 0 to 32767, as said below
- out_weight: bfloat16 [704, 1408], P('seq'), may hold values from -0.21875 to 0.21875
- norm_gain: float32 [1408], replicated, may hold values from 0.1 to 1.9
- bridge_weight: bfloat16 [1408, 512], replicated, may hold values from -0.15625 to 0.15625
- mask_token: bfloat16 [512], replicated, may hold values from -6 to 6
- dec_gain: float32 [512], replicated, may hold values from 0.1 to 1.9
- dec_qkv_weight: bfloat16 [512, 768], replicated, may hold values from -1.1048543 to 1.1048543
- dec_out_weight: bfloat16 [256, 512], replicated, may hold values from -0.375 to 0.375
Outputs:
- enc_out: bfloat16 [32768, 1408], P(('clip', 'seq')), parts along dimension 0
- dec_out: bfloat16 [49152, 512], P(('clip', 'seq')), parts along dimension 0
The draws below stay inside these ranges and needn't reach their ends.
There are 16 independent parts, one for each index of `clip`. The reference program is written for one: setup_inputs(seed, part) draws one part's arguments, and reference() takes and returns one part's arrays. A program takes and returns all parts, laid end to end along the dimension named above; an argument that names none is the same for every part. Nothing has to cross between parts.
Inputs may be any that keep to these rules, and one draw needn't show every extreme that they name: `vis_count`: A device with more than 64 rows is never the last one, and the device after it has none; every device without rows follows such a device; every other device has 32 to 64 rows. `vis_dest`: for a device with more than 64 rows, the next device (index one higher); for other devices the entry is ignored. `vis_pos`: slots of device d hold distinct positions in [d * 1024, (d + 1) * 1024); entries of slots that are not live are ignored. `kept_pos`: device d's entries are distinct positions in [d * 1024, (d + 1) * 1024), none equal to a visible slot's entry.
All inputs are finite; a program needn't handle non-finite values.
Results may differ from the reference program's by a relative error of at most 0.01.
Values may be sent and summed in bfloat16 or wider, within the bound.
No kernel may reach another device: no remote copies, remote signals or barrier semaphores. Data moves between devices by JAX's collectives and lax.ppermute only.
A program may use at most 128 MiB of HBM per device.

```python
import jax
import jax.numpy as jnp
import numpy as np
from jax import lax

MODEL_WIDTH = 1408
HEAD_SIZE = 88
ENC_HEADS = 8
DEC_WIDTH = 512
DEC_HEAD_SIZE = 64
DEC_HEADS = 4
ROW_BLOCK = 64
KEPT_DEV = 96
TOK_DEV = 1024
ENC_INNER = 704
DEC_INNER = 256
N_SEQ = 32


def routing_plan(key):
    base = jax.random.fold_in(key, 7)
    subkeys = jax.random.split(base, 4)
    pair_total = N_SEQ // 2
    linked = jax.random.randint(subkeys[0], (pair_total,), 0, 2)
    pair_ids = jnp.arange(pair_total, dtype=jnp.int32)
    linked = jnp.where(pair_ids == 0, 1, linked)
    linked = jnp.where((pair_ids == N_SEQ // 4 - 1) | (pair_ids == N_SEQ // 4), 0, linked)
    device = jnp.arange(N_SEQ, dtype=jnp.int32)
    is_even = device % 2 == 0
    pair_on = linked[device // 2] == 1
    overflow = is_even & pair_on | (device == N_SEQ // 2 - 1)
    empty_dev = jnp.logical_not(is_even) & pair_on | (device == N_SEQ // 2)
    drawn_count = jax.random.randint(subkeys[1], (N_SEQ,), ROW_BLOCK // 2, ROW_BLOCK + 1)
    full_count = jax.random.randint(subkeys[2], (N_SEQ,), ROW_BLOCK + 1, 2 * ROW_BLOCK + 1)
    counts = jnp.where(overflow, full_count, jnp.where(empty_dev, 0, drawn_count))
    counts = jnp.where(device == 0, 2 * ROW_BLOCK, counts)
    others = jax.random.randint(subkeys[3], (N_SEQ,), 0, N_SEQ)
    others = jnp.where(device == N_SEQ // 2 - 2, N_SEQ - 1, others)
    others = jnp.where(device == N_SEQ // 2 + 1, 0, others)
    target = jnp.where(overflow, device + 1, others)
    return (counts.astype(jnp.int32), target.astype(jnp.int32))


def positions_plan(key):
    base = jax.random.fold_in(key, 19)
    subkeys = jax.random.split(base, N_SEQ)
    orders = jax.vmap(lambda subkey: jax.random.permutation(subkey, TOK_DEV))(subkeys).astype(jnp.int32)
    offsets = jnp.arange(N_SEQ, dtype=jnp.int32)[:, None] * TOK_DEV
    visible = orders[:, :2 * ROW_BLOCK] + offsets
    kept = orders[:, 2 * ROW_BLOCK:2 * ROW_BLOCK + KEPT_DEV] + offsets
    return (visible.reshape(-1), kept.reshape(-1))


def draw_vis_count(key, part):
    return routing_plan(key)[0]


def draw_vis_dest(key, part):
    return routing_plan(key)[1]


def draw_vis_pos(key, part):
    return positions_plan(key)[0]


def draw_kept_pos(key, part):
    return positions_plan(key)[1]


def draw_enc_rows(key, part):
    slots = 2 * ROW_BLOCK * N_SEQ
    inner_width = ENC_HEADS * HEAD_SIZE
    subkeys = jax.random.split(jax.random.fold_in(key, 31), 4)
    queries = 1.7 * jnp.clip(jax.random.normal(subkeys[0], (slots, inner_width), jnp.float32), -6.0, 6.0)
    keyed = 1.7 * jnp.clip(jax.random.normal(subkeys[1], (slots, inner_width), jnp.float32), -6.0, 6.0)
    values = jnp.clip(jax.random.normal(subkeys[2], (slots, inner_width), jnp.float32), -6.0, 6.0)
    inputs = 0.6 * jnp.clip(jax.random.normal(subkeys[3], (slots, MODEL_WIDTH), jnp.float32), -6.0, 6.0)
    return jnp.concatenate([queries, keyed, values, inputs], axis=1).astype(jnp.bfloat16)


def draw_dec_qkv_weight(key, part):
    inner_width = DEC_HEADS * DEC_HEAD_SIZE
    root = DEC_WIDTH ** (-0.5)
    subkeys = jax.random.split(jax.random.fold_in(key, 43), 3)
    query_part = 3.0 * jnp.clip(jax.random.normal(subkeys[0], (DEC_WIDTH, inner_width), jnp.float32), -4.0, 4.0) * root
    key_part = jnp.clip(jax.random.normal(subkeys[1], (DEC_WIDTH, inner_width), jnp.float32), -4.0, 4.0) * root
    value_part = jnp.clip(jax.random.normal(subkeys[2], (DEC_WIDTH, inner_width), jnp.float32), -4.0, 4.0) * root
    return jnp.concatenate([query_part, key_part, value_part], axis=1).astype(jnp.bfloat16)


def steps_of(stream_key, dims, cuts, least, top_value):
    def one(dim, parts):
        draws = jax.random.uniform(jax.random.fold_in(jax.random.fold_in(stream_key, 6), dim), (parts,), jnp.float32, least / len(cuts), top_value / len(cuts))
        return jnp.repeat(jnp.exp(draws), dims[dim] // parts).reshape((-1,) + (1,) * (len(dims) - dim - 1))

    loudness = one(*cuts[0])
    for cut in cuts[1:]:
        loudness = loudness * one(*cut)
    return loudness


def bell_draw(own_key, dims, scale, most, cuts=(), kind=jnp.bfloat16):
    array = jax.random.normal(own_key, dims, jnp.float32) * scale
    if len(cuts) > 0:
        array = steps_of(own_key, dims, cuts, -0.22, 0.18) * array
    return jnp.clip(array, min=-most, max=most).astype(kind)


def setup_inputs(seed: int = 0, part: int = 0) -> dict:
    splits = jax.random.split(jax.random.key(seed), 13)
    part_keys = jax.random.split(jax.random.fold_in(splits[12], part), 13)
    enc_rows = draw_enc_rows(jax.random.fold_in(jax.random.fold_in(splits[12], part), 71), part)
    vis_count = draw_vis_count(jax.random.fold_in(jax.random.fold_in(splits[12], part), 71), part)
    vis_dest = draw_vis_dest(jax.random.fold_in(jax.random.fold_in(splits[12], part), 71), part)
    vis_pos = draw_vis_pos(jax.random.fold_in(jax.random.fold_in(splits[12], part), 71), part)
    kept_pos = draw_kept_pos(jax.random.fold_in(jax.random.fold_in(splits[12], part), 71), part)
    out_weight = bell_draw(splits[5], (ENC_INNER, MODEL_WIDTH), ENC_INNER ** -0.5, 0.21875, ((0, 32),))
    norm_gain = jnp.clip(1.0 + 0.18 * jax.random.normal(splits[6], (MODEL_WIDTH,), jnp.float32), 0.1, 1.9)
    bridge_weight = bell_draw(splits[7], (MODEL_WIDTH, DEC_WIDTH), MODEL_WIDTH ** -0.5, 0.15625)
    mask_token = bell_draw(splits[8], (DEC_WIDTH,), 1.0, 6.0)
    dec_gain = jnp.clip(1.0 + 0.18 * jax.random.normal(splits[9], (DEC_WIDTH,), jnp.float32), 0.1, 1.9)
    dec_qkv_weight = draw_dec_qkv_weight(jax.random.fold_in(splits[12], 71), part)
    dec_out_weight = bell_draw(splits[11], (DEC_INNER, DEC_WIDTH), DEC_INNER ** -0.5, 0.375)
    return dict(enc_rows=enc_rows, vis_count=vis_count, vis_dest=vis_dest, vis_pos=vis_pos, kept_pos=kept_pos, out_weight=out_weight, norm_gain=norm_gain, bridge_weight=bridge_weight, mask_token=mask_token, dec_gain=dec_gain, dec_qkv_weight=dec_qkv_weight, dec_out_weight=dec_out_weight)


NEG_FILL = -1e+30
LN_EPS = 1e-06

def layer_norm(rows_in, gain_row):
    widened = rows_in.astype(jnp.float32)
    centred = widened - lax.optimization_barrier(jnp.mean(widened, axis=-1, keepdims=True))
    spread = lax.optimization_barrier(jnp.mean(centred * centred, axis=-1, keepdims=True))
    return centred * lax.rsqrt(spread + LN_EPS) * gain_row[None, :]

def sinusoid(positions, row_width):
    frequency = jnp.asarray(np.power(10000.0, -np.arange(row_width // 2) * 2.0 / row_width).astype(np.float32))
    angles = positions.astype(jnp.float32)[:, None] * frequency[None, :]
    return jnp.stack([jnp.sin(angles), jnp.cos(angles)], axis=-1).reshape(positions.shape[0], row_width)

def attend_ref(query_block, key_rows, value_rows, usable, head_count, softmax_scale):
    count_q = query_block.shape[0]
    count_k = key_rows.shape[0]
    head_size = query_block.shape[1] // head_count
    query_heads = query_block.reshape(count_q, head_count, head_size).astype(jnp.float32)
    key_heads = key_rows.reshape(count_k, head_count, head_size).astype(jnp.float32)
    value_heads = value_rows.reshape(count_k, head_count, head_size).astype(jnp.float32)
    scores = jnp.einsum('qhd,khd->hqk', query_heads, key_heads, precision=lax.Precision.HIGHEST) * softmax_scale
    scores = jnp.where(usable[None, None, :], scores, NEG_FILL)
    highest = lax.optimization_barrier(jnp.max(scores, axis=-1, keepdims=True))
    weights = jnp.where(usable[None, None, :], jnp.exp(scores - highest), 0.0)
    summed = lax.optimization_barrier(jnp.sum(weights, axis=-1))
    rounded = lax.optimization_barrier(weights.astype(jnp.bfloat16)).astype(jnp.float32)
    mixed = jnp.einsum('hqk,khd->qhd', rounded, value_heads, precision=lax.Precision.HIGHEST)
    mixed = mixed / jnp.transpose(summed)[:, :, None]
    return mixed.reshape(count_q, head_count * head_size).astype(jnp.bfloat16)

def reference(enc_rows, vis_count, vis_dest, vis_pos, kept_pos, out_weight, norm_gain, bridge_weight, mask_token, dec_gain, dec_qkv_weight, dec_out_weight):
    row_block = ROW_BLOCK
    slot_pair = 2 * row_block
    enc_inner = ENC_HEADS * HEAD_SIZE
    dec_inner = DEC_HEADS * DEC_HEAD_SIZE
    slot_total = enc_rows.shape[0]
    ordinal = jnp.arange(slot_total, dtype=jnp.int32)
    home_live = ordinal % slot_pair < vis_count[ordinal // slot_pair]
    queries = enc_rows[:, :enc_inner]
    key_rows = enc_rows[:, enc_inner:2 * enc_inner]
    value_rows = enc_rows[:, 2 * enc_inner:3 * enc_inner]
    residual = enc_rows[:, 3 * enc_inner:]
    enc_scale = HEAD_SIZE ** (-0.5)
    query_blocks = queries.reshape(-1, slot_pair, enc_inner)
    enc_attn = lax.map(lambda query_block: attend_ref(query_block, key_rows, value_rows, home_live, ENC_HEADS, enc_scale), query_blocks)
    enc_attn = enc_attn.reshape(slot_total, enc_inner)
    home_out = (residual.astype(jnp.float32) + jnp.dot(enc_attn, out_weight, preferred_element_type=jnp.float32)).astype(jnp.bfloat16)
    devices_all = jnp.arange(N_SEQ, dtype=jnp.int32)
    matches = (vis_dest[None, :] == devices_all[:, None]) & (vis_count[None, :] > row_block) & (devices_all[None, :] != devices_all[:, None])
    sender = jnp.argmax(matches.astype(jnp.int32), axis=1).astype(jnp.int32)
    has_own = vis_count > 0
    first_row = jnp.where(has_own, devices_all * slot_pair, sender * slot_pair + row_block)
    bal_count = jnp.where(has_own, jnp.minimum(vis_count, row_block), vis_count[sender] - row_block)
    within = jnp.arange(row_block, dtype=jnp.int32)
    bal_rows = (first_row[:, None] + within[None, :]).reshape(-1)
    bal_live = (within[None, :] < bal_count[:, None]).reshape(-1)
    picked = home_out[bal_rows]
    enc_out = jnp.where(bal_live[:, None], picked, jnp.zeros_like(picked))
    vis_normed = layer_norm(home_out, norm_gain).astype(jnp.bfloat16)
    vis_dec = (jnp.dot(vis_normed, bridge_weight, preferred_element_type=jnp.float32) + sinusoid(vis_pos, DEC_WIDTH)).astype(jnp.bfloat16)
    kept_dec = (mask_token.astype(jnp.float32)[None, :] + sinusoid(kept_pos, DEC_WIDTH)).astype(jnp.bfloat16)
    stacked = jnp.concatenate([vis_dec, kept_dec], axis=0)
    dec_normed = layer_norm(stacked, dec_gain).astype(jnp.bfloat16)
    dec_proj = jnp.dot(dec_normed, dec_qkv_weight, preferred_element_type=jnp.float32).astype(jnp.bfloat16)
    kept_total = kept_pos.shape[0]
    dec_live = jnp.concatenate([home_live, jnp.arange(kept_total, dtype=jnp.int32) >= 0], axis=0)
    dec_queries = dec_proj[slot_total:, :dec_inner]
    dec_keys = dec_proj[:, dec_inner:2 * dec_inner]
    dec_values = dec_proj[:, 2 * dec_inner:]
    dec_scale = DEC_HEAD_SIZE ** (-0.5)
    dec_blocks = dec_queries.reshape(-1, KEPT_DEV, dec_inner)
    dec_attn = lax.map(lambda query_block: attend_ref(query_block, dec_keys, dec_values, dec_live, DEC_HEADS, dec_scale), dec_blocks)
    dec_attn = dec_attn.reshape(kept_total, dec_inner)
    dec_out = (kept_dec.astype(jnp.float32) + jnp.dot(dec_attn, dec_out_weight, preferred_element_type=jnp.float32)).astype(jnp.bfloat16)
    return (enc_out, dec_out)
```

```python
import math

import jax
import jax.numpy as jnp
import numpy as np
from jax import lax
from jax.experimental import pallas as pl
from jax.experimental.pallas import tpu as pltpu
from jax.sharding import Mesh
from jax.sharding import PartitionSpec as P

HEAD_SIZE = 88
ENC_HEADS = 8
ENC_INNER = ENC_HEADS * HEAD_SIZE
DEC_WIDTH = 512
DEC_HEAD_SIZE = 64
DEC_HEADS = 4
DEC_INNER = DEC_HEADS * DEC_HEAD_SIZE
ROW_BLOCK = 64
VIS_TAIL = 8
LANES = 128
SEQ = ("z", "core")
CLIP_SEQ = ("clip", "z", "core")
ENC_WINDOW = 768
ENC_SHIFT = ENC_WINDOW - ENC_INNER

NEG_FILL = -1e30
LN_EPS = 1e-06
F32 = jnp.float32
BF16 = jnp.bfloat16


def shifted(shard, axis, by):
    devices = lax.axis_size(axis)
    pairs = [(i, i + by) for i in range(devices) if 0 <= i + by < devices]
    return lax.ppermute(shard, axis, pairs)


def swapped(shard):
    return lax.ppermute(shard, "core", [(0, 1), (1, 0)])


def layer_norm(rows_in, gain_row):
    widened = rows_in.astype(F32)
    centred = widened - jnp.mean(widened, axis=-1, keepdims=True)
    spread = jnp.mean(centred * centred, axis=-1, keepdims=True)
    return centred * lax.rsqrt(spread + LN_EPS) * gain_row


def frequencies():
    half = np.arange(DEC_WIDTH // 2)
    return jnp.asarray(np.power(10000.0, -half * 2.0 / DEC_WIDTH).astype(np.float32))


def sinusoid(positions):
    angles = positions.astype(F32)[:, None] * frequencies()[None, :]
    return jnp.stack([jnp.sin(angles), jnp.cos(angles)], axis=-1).reshape(
        positions.shape[0], DEC_WIDTH
    )


def split_sinusoid(positions):
    angles = positions[:, None] * frequencies()[None, :]
    return jnp.concatenate([jnp.sin(angles), jnp.cos(angles)], axis=-1)


def halves_first(rows):
    apart = rows.reshape(rows.shape[0] // 2, 2, *rows.shape[1:])
    return jnp.concatenate([apart[:, 0], apart[:, 1]], axis=0)


def balance_table(vis_count, row_block):
    left_count = jnp.concatenate([vis_count[:1] * 0, vis_count[:-1]], axis=0)
    return jnp.where(vis_count > 0, jnp.minimum(vis_count, row_block), left_count - row_block)


def nt_dot(left, right):
    return lax.dot_general(left, right, (((1,), (1,)), ((), ())), preferred_element_type=F32)


def head_column(shape, head, size, offset):
    column = lax.broadcasted_iota(jnp.int32, shape, 1) - offset
    return (column >= head * size) & (column < (head + 1) * size)


def per_head(rows, heads, size):
    copies = [
        jnp.where(head_column(rows.shape, h, size, 0), rows, jnp.zeros_like(rows))
        for h in range(heads)
    ]
    return jnp.concatenate(copies, axis=0)


def gathered_heads(stacked, heads, size, offset):
    count = stacked.shape[0] // heads
    shape = (count, stacked.shape[1])
    total = jnp.zeros(shape, F32)
    for h in range(heads):
        mine = head_column(shape, h, size, offset)
        total = jnp.where(mine, stacked[h * count : (h + 1) * count], total)
    return total


def spread_heads(column, heads, size):
    count = column.shape[0] // heads
    shape = (count, heads * size)
    total = jnp.zeros(shape, F32)
    for h in range(heads):
        total = jnp.where(
            head_column(shape, h, size, 0), column[h * count : (h + 1) * count], total
        )
    return total


def encoder_kernel(
    live_ref,
    query_ref,
    kv_ref,
    mask_ref,
    residual_ref,
    weight_ref,
    norm_gain_ref,
    bridge_ref,
    pe_ref,
    dec_gain_ref,
    dec_weight_ref,
    enc_out_ref,
    vis_kv_ref,
):
    scale = 1.0 / math.sqrt(HEAD_SIZE)
    queries = per_head(query_ref[...], ENC_HEADS, HEAD_SIZE)
    scores = nt_dot(queries, kv_ref[:, :ENC_WINDOW]) * scale
    scores = jnp.where(mask_ref[...] > 0.0, scores, NEG_FILL)
    weights = jnp.exp(scores - jnp.max(scores, axis=-1, keepdims=True))
    summed = jnp.sum(weights, axis=-1, keepdims=True)
    mixed = jnp.dot(
        weights.astype(BF16), kv_ref[:, 2 * ENC_INNER - ENC_WINDOW :], preferred_element_type=F32
    )
    attn = gathered_heads(mixed / summed, ENC_HEADS, HEAD_SIZE, ENC_SHIFT).astype(BF16)
    projected = jnp.dot(attn, weight_ref[...], preferred_element_type=F32)
    computed = (residual_ref[...].astype(F32) + projected).astype(BF16)
    slot = lax.broadcasted_iota(jnp.int32, computed.shape, 0)
    enc_out_ref[...] = jnp.where(slot < live_ref[0], computed, jnp.zeros_like(computed))
    normed = layer_norm(computed, norm_gain_ref[...]).astype(BF16)
    bridged = jnp.dot(normed, bridge_ref[...], preferred_element_type=F32) + pe_ref[...]
    dec_normed = layer_norm(bridged.astype(BF16), dec_gain_ref[...]).astype(BF16)
    vis_kv_ref[...] = jnp.dot(dec_normed, dec_weight_ref[...], preferred_element_type=F32).astype(
        BF16
    )


def kept_kernel(kept_ref, gain_ref, weight_ref, query_ref, mixed_ref, peak_ref, sum_ref):
    scale = 1.0 / math.sqrt(DEC_HEAD_SIZE)
    normed = layer_norm(kept_ref[...], gain_ref[...]).astype(BF16)
    pairs = jnp.dot(normed, weight_ref[...], preferred_element_type=F32).astype(BF16)
    queries = per_head(query_ref[...], DEC_HEADS, DEC_HEAD_SIZE)
    scores = nt_dot(queries, pairs[:, :DEC_INNER]) * scale
    peak = jnp.max(scores, axis=-1, keepdims=True)
    weights = jnp.exp(scores - peak)
    sum_ref[...] = jnp.sum(weights, axis=-1, keepdims=True)
    peak_ref[...] = peak
    mixed = jnp.dot(weights.astype(BF16), pairs[:, DEC_INNER:], preferred_element_type=F32)
    mixed_ref[...] = gathered_heads(mixed, DEC_HEADS, DEC_HEAD_SIZE, 0)


def visible_kernel(
    main_ref,
    tail_ref,
    main_mask_ref,
    tail_mask_ref,
    query_ref,
    mixed_ref,
    peak_ref,
    sum_ref,
    own_ref,
    other_ref,
):
    scale = 1.0 / math.sqrt(DEC_HEAD_SIZE)
    queries = per_head(query_ref[...], DEC_HEADS, DEC_HEAD_SIZE)
    main = nt_dot(queries, main_ref[:, :DEC_INNER]) * scale
    main = jnp.where(main_mask_ref[...] > 0.0, main, NEG_FILL)
    tail = nt_dot(queries, tail_ref[:, :DEC_INNER]) * scale
    tail = jnp.where(tail_mask_ref[...] > 0.0, tail, NEG_FILL)
    peak = jnp.maximum(
        jnp.maximum(peak_ref[...], jnp.max(main, axis=-1, keepdims=True)),
        jnp.max(tail, axis=-1, keepdims=True),
    )
    main = jnp.exp(main - peak)
    tail = jnp.exp(tail - peak)
    fade = jnp.exp(peak_ref[...] - peak)
    summed = (
        sum_ref[...] * fade
        + jnp.sum(main, axis=-1, keepdims=True)
        + jnp.sum(tail, axis=-1, keepdims=True)
    )
    mixed = jnp.dot(main.astype(BF16), main_ref[:, DEC_INNER:], preferred_element_type=F32)
    mixed += jnp.dot(tail.astype(BF16), tail_ref[:, DEC_INNER:], preferred_element_type=F32)
    total = gathered_heads(mixed, DEC_HEADS, DEC_HEAD_SIZE, 0)
    total += mixed_ref[...] * spread_heads(fade, DEC_HEADS, DEC_HEAD_SIZE)
    count = total.shape[0]
    lane = lax.broadcasted_iota(jnp.int32, (count, LANES), 1)
    stats = jnp.zeros((count, LANES), F32)
    for h in range(DEC_HEADS):
        stats = jnp.where(lane == h, peak[h * count : (h + 1) * count], stats)
        stats = jnp.where(lane == DEC_HEADS + h, summed[h * count : (h + 1) * count], stats)
    half = count // 2
    own_ref[:, :DEC_INNER] = total[:half]
    own_ref[:, DEC_INNER:] = stats[:half]
    other_ref[:, :DEC_INNER] = total[half:]
    other_ref[:, DEC_INNER:] = stats[half:]


def finish_kernel(own_ref, received_ref, kept_ref, weight_ref, out_ref):
    shape = (own_ref.shape[0], DEC_INNER)
    total = jnp.zeros(shape, F32)
    for h in range(DEC_HEADS):
        own_peak = own_ref[:, DEC_INNER + h : DEC_INNER + h + 1]
        far_peak = received_ref[:, DEC_INNER + h : DEC_INNER + h + 1]
        place = DEC_INNER + DEC_HEADS + h
        peak = jnp.maximum(own_peak, far_peak)
        own_fade = jnp.exp(own_peak - peak)
        far_fade = jnp.exp(far_peak - peak)
        summed = own_fade * own_ref[:, place : place + 1] + far_fade * received_ref[
            :, place : place + 1
        ]
        mixed = (
            own_fade * own_ref[:, :DEC_INNER] + far_fade * received_ref[:, :DEC_INNER]
        ) / summed
        total = jnp.where(head_column(shape, h, DEC_HEAD_SIZE, 0), mixed, total)
    projected = jnp.dot(total.astype(BF16), weight_ref[...], preferred_element_type=F32)
    out_ref[...] = (kept_ref[...].astype(F32) + projected).astype(BF16)


def in_vmem(count):
    return [pl.BlockSpec(memory_space=pltpu.VMEM)] * count


def call(kernel, out_shape, *operands, scalars=0):
    smem = [pl.BlockSpec(memory_space=pltpu.SMEM)] * scalars
    out_specs = jax.tree.map(lambda _: pl.BlockSpec(memory_space=pltpu.VMEM), out_shape)
    return pl.pallas_call(
        kernel,
        out_shape=out_shape,
        in_specs=smem + in_vmem(len(operands) - scalars),
        out_specs=out_specs,
        compiler_params=pltpu.CompilerParams(vmem_limit_bytes=56 * 1024 * 1024),
    )(*operands)


def body(
    enc_rows,
    vis_count,
    vis_dest,
    vis_pos,
    kept_pos,
    out_weight,
    norm_gain,
    bridge_weight,
    mask_token,
    dec_gain,
    dec_qkv_weight,
    dec_out_weight,
):
    row_block = ROW_BLOCK
    shape_of = jax.ShapeDtypeStruct
    myself = lax.axis_index(SEQ)
    core = lax.axis_index("core")
    chips = lax.axis_size("z")
    bal_counts = balance_table(vis_count, row_block)
    has_own = vis_count[myself] > 0

    pair_rows = enc_rows[:, ENC_INNER : 3 * ENC_INNER]
    key_value = jnp.where(has_own, pair_rows[:row_block], shifted(pair_rows[row_block:], SEQ, 1))
    all_kv = lax.all_gather(key_value, SEQ, axis=0, tiled=True)

    kept_f32 = kept_pos.astype(F32)
    coarse = jnp.floor(kept_f32 * (1.0 / 256.0))
    fine = kept_f32 - coarse * 256.0
    coded = jnp.concatenate([coarse, fine]).astype(BF16)
    kept_dev = kept_pos.shape[0]
    coded = jnp.pad(coded, (0, out_weight.shape[1] - coded.shape[0]))
    packet = jnp.concatenate([out_weight, coded[None, :]], axis=0)
    packet, enc_late, _ = lax.optimization_barrier((packet, enc_rows, key_value))
    packets = lax.all_gather(packet, "z", axis=0)
    coded_all = packets[:, -1, : 2 * kept_dev].astype(F32)
    kept_all = (coded_all[:, :kept_dev] * 256.0 + coded_all[:, kept_dev:]).reshape(-1)
    own_weight = packets[:, :-1, :]
    far_weight = swapped(own_weight)
    is_even = core == 0
    weight = jnp.stack(
        [
            jnp.where(is_even, own_weight, far_weight),
            jnp.where(is_even, far_weight, own_weight),
        ],
        axis=1,
    ).reshape(ENC_INNER, -1)
    weight = jnp.pad(weight, ((ENC_SHIFT, 0), (0, 0)))

    rest = jnp.concatenate([enc_late[:, :ENC_INNER], enc_late[:, 3 * ENC_INNER :]], axis=1)
    rest = jnp.where(has_own, rest[:row_block], shifted(rest[row_block:], SEQ, 1))
    queries = jnp.pad(rest[:, :ENC_INNER], ((0, 0), (0, ENC_SHIFT)))
    residual = rest[:, ENC_INNER:]

    kept_in = (mask_token.astype(F32)[None, :] + sinusoid(kept_pos)).astype(BF16)
    own_normed = layer_norm(kept_in, dec_gain[None, :]).astype(BF16)
    asking = jnp.dot(
        own_normed, dec_qkv_weight[:, :DEC_INNER], preferred_element_type=F32
    ).astype(BF16)
    asking = jnp.concatenate([asking, swapped(asking)], axis=0)
    mask_split = halves_first(mask_token)
    kept_split = (mask_split.astype(F32)[None, :] + split_sinusoid(kept_all)).astype(BF16)
    asked = asking.shape[0]
    stat = shape_of((DEC_HEADS * asked, 1), F32)
    kept_state = call(
        kept_kernel,
        (shape_of((asked, DEC_INNER), F32), stat, stat),
        kept_split,
        halves_first(dec_gain)[None, :],
        halves_first(dec_qkv_weight[:, DEC_INNER:]),
        asking,
    )

    first_row = jnp.where(has_own, myself * 2 * row_block, (myself - 1) * 2 * row_block + row_block)
    bal_pos = lax.dynamic_slice_in_dim(vis_pos, first_row, row_block)
    within = jnp.arange(row_block, dtype=jnp.int32)
    live = (within[None, :] < bal_counts[:, None]).astype(F32)
    enc_out, vis_kv = call(
        encoder_kernel,
        (
            shape_of((row_block, residual.shape[1]), BF16),
            shape_of((row_block, 2 * DEC_INNER), BF16),
        ),
        bal_counts[myself][None],
        queries,
        all_kv,
        live.reshape(1, -1),
        residual,
        weight,
        norm_gain[None, :],
        bridge_weight,
        sinusoid(bal_pos),
        dec_gain[None, :],
        dec_qkv_weight[:, DEC_INNER:],
        scalars=1,
    )

    split = row_block - VIS_TAIL
    tails = jnp.broadcast_to(vis_kv[None, split:], (chips, VIS_TAIL, 2 * DEC_INNER))
    vis_tail = lax.all_to_all(tails, "z", 0, 0, tiled=True).reshape(-1, 2 * DEC_INNER)
    vis_main = lax.all_gather(vis_kv[:split], "z", axis=0, tiled=True)
    live_same = lax.dynamic_index_in_dim(
        live.reshape(chips, -1, row_block), core, axis=1, keepdims=False
    )
    half = shape_of((kept_dev, DEC_INNER + LANES), F32)
    own_part, other_part = call(
        visible_kernel,
        (half, half),
        vis_main,
        vis_tail,
        live_same[:, :split].reshape(1, -1),
        live_same[:, split:].reshape(1, -1),
        asking,
        *kept_state,
    )
    dec_out = call(
        finish_kernel,
        shape_of((kept_dev, DEC_WIDTH), BF16),
        own_part,
        swapped(other_part),
        kept_in,
        dec_out_weight,
    )
    return (enc_out, dec_out)


def solution(mesh):
    finer = Mesh(mesh.devices.reshape(mesh.shape["clip"], 16, 2), CLIP_SEQ)
    return jax.shard_map(
        body,
        mesh=finer,
        in_specs=(
            P(CLIP_SEQ, None),
            P("clip"),
            P("clip"),
            P("clip"),
            P(CLIP_SEQ),
            P(SEQ, None),
            P(),
            P(),
            P(),
            P(),
            P(),
            P(),
        ),
        out_specs=(P(CLIP_SEQ, None), P(CLIP_SEQ, None)),
        check_vma=False,
    )
```

```python
import math

import jax
import jax.numpy as jnp
import numpy as np
from jax import lax
from jax.experimental import pallas as pl
from jax.experimental.pallas import tpu as pltpu
from jax.sharding import Mesh
from jax.sharding import PartitionSpec as P

HEAD_SIZE = 88
ENC_HEADS = 8
ENC_INNER = ENC_HEADS * HEAD_SIZE
DEC_WIDTH = 512
DEC_HEAD_SIZE = 64
DEC_HEADS = 4
DEC_INNER = DEC_HEADS * DEC_HEAD_SIZE
ROW_BLOCK = 64
VIS_TAIL = 1
WEIGHT_ROWS = 24
ENC_CHUNKS = 4
LANES = 128
SEQ = ("z", "core")
CLIP_SEQ = ("clip", "z", "core")
ENC_WINDOW = 768
ENC_SHIFT = ENC_WINDOW - ENC_INNER

NEG_FILL = -1e30
LN_EPS = 1e-06
F32 = jnp.float32
BF16 = jnp.bfloat16


def shifted(shard, axis, by):
    devices = lax.axis_size(axis)
    pairs = [(i, i + by) for i in range(devices) if 0 <= i + by < devices]
    return lax.ppermute(shard, axis, pairs)


def swapped(shard):
    return lax.ppermute(shard, "core", [(0, 1), (1, 0)])


def layer_norm(rows_in, gain_row):
    widened = rows_in.astype(F32)
    centred = widened - jnp.mean(widened, axis=-1, keepdims=True)
    spread = jnp.mean(centred * centred, axis=-1, keepdims=True)
    return centred * lax.rsqrt(spread + LN_EPS) * gain_row


def frequencies():
    half = np.arange(DEC_WIDTH // 2)
    return jnp.asarray(np.power(10000.0, -half * 2.0 / DEC_WIDTH).astype(np.float32))


def sinusoid(positions):
    angles = positions.astype(F32)[:, None] * frequencies()[None, :]
    return jnp.stack([jnp.sin(angles), jnp.cos(angles)], axis=-1).reshape(
        positions.shape[0], DEC_WIDTH
    )


def split_sinusoid(positions):
    angles = positions[:, None] * frequencies()[None, :]
    return jnp.concatenate([jnp.sin(angles), jnp.cos(angles)], axis=-1)


def halves_first(rows):
    apart = rows.reshape(rows.shape[0] // 2, 2, *rows.shape[1:])
    return jnp.concatenate([apart[:, 0], apart[:, 1]], axis=0)


def balance_table(vis_count, row_block):
    left_count = jnp.concatenate([vis_count[:1] * 0, vis_count[:-1]], axis=0)
    return jnp.where(vis_count > 0, jnp.minimum(vis_count, row_block), left_count - row_block)


def nt_dot(left, right):
    return lax.dot_general(left, right, (((1,), (1,)), ((), ())), preferred_element_type=F32)


def head_column(shape, head, size, offset):
    column = lax.broadcasted_iota(jnp.int32, shape, 1) - offset
    return (column >= head * size) & (column < (head + 1) * size)


def per_head(rows, heads, size):
    copies = [
        jnp.where(head_column(rows.shape, h, size, 0), rows, jnp.zeros_like(rows))
        for h in range(heads)
    ]
    return jnp.concatenate(copies, axis=0)


def gathered_heads(stacked, heads, size, offset):
    count = stacked.shape[0] // heads
    shape = (count, stacked.shape[1])
    total = jnp.zeros(shape, F32)
    for h in range(heads):
        mine = head_column(shape, h, size, offset)
        total = jnp.where(mine, stacked[h * count : (h + 1) * count], total)
    return total


def spread_heads(column, heads, size):
    count = column.shape[0] // heads
    shape = (count, heads * size)
    total = jnp.zeros(shape, F32)
    for h in range(heads):
        total = jnp.where(
            head_column(shape, h, size, 0), column[h * count : (h + 1) * count], total
        )
    return total


def encoder_kernel(
    live_ref,
    packets_hbm,
    query_ref,
    mask_ref,
    residual_ref,
    spread_ref,
    norm_gain_ref,
    bridge_hbm,
    pe_ref,
    dec_gain_ref,
    dec_weight_hbm,
    enc_out_ref,
    main_ref,
    tail_ref,
    kv_ref,
    weight_ref,
    bridge_ref,
    dec_weight_ref,
    scores_ref,
    kv_sems,
    weight_sems,
    other_sems,
):
    devices = packets_hbm.shape[0]
    kv_copies = [
        pltpu.make_async_copy(
            packets_hbm.at[d, pl.ds(0, ROW_BLOCK)],
            kv_ref.at[pl.ds(d * ROW_BLOCK, ROW_BLOCK)],
            kv_sems.at[d],
        )
        for d in range(devices)
    ]
    weight_copies = [
        pltpu.make_async_copy(
            packets_hbm.at[d, pl.ds(ROW_BLOCK, WEIGHT_ROWS)],
            weight_ref.at[pl.ds(d * WEIGHT_ROWS, WEIGHT_ROWS)],
            weight_sems.at[d],
        )
        for d in range(devices)
    ]
    bridge_copy = pltpu.make_async_copy(bridge_hbm, bridge_ref, other_sems.at[0])
    dec_copy = pltpu.make_async_copy(dec_weight_hbm, dec_weight_ref, other_sems.at[1])
    for copy in kv_copies + weight_copies + [bridge_copy, dec_copy]:
        copy.start()
    scale = 1.0 / math.sqrt(HEAD_SIZE)
    queries = per_head(query_ref[...], ENC_HEADS, HEAD_SIZE)
    per_chunk = devices // ENC_CHUNKS
    width = per_chunk * ROW_BLOCK
    peak = None
    for chunk in range(ENC_CHUNKS):
        for copy in kv_copies[chunk * per_chunk : (chunk + 1) * per_chunk]:
            copy.wait()
        here = slice(chunk * width, (chunk + 1) * width)
        scores = nt_dot(queries, kv_ref[here, :ENC_WINDOW]) * scale
        scores = jnp.where(mask_ref[:, here] > 0.0, scores, NEG_FILL)
        scores_ref[:, here] = scores
        top = jnp.max(scores, axis=-1, keepdims=True)
        peak = top if peak is None else jnp.maximum(peak, top)
    summed = 0.0
    mixed = 0.0
    for chunk in range(ENC_CHUNKS):
        here = slice(chunk * width, (chunk + 1) * width)
        weights = jnp.exp(scores_ref[:, here] - peak)
        summed += jnp.sum(weights, axis=-1, keepdims=True)
        mixed += jnp.dot(
            weights.astype(BF16),
            kv_ref[here, 2 * ENC_INNER - ENC_WINDOW :],
            preferred_element_type=F32,
        )
    attn = gathered_heads(mixed / summed, ENC_HEADS, HEAD_SIZE, ENC_SHIFT).astype(BF16)
    attn = jnp.dot(attn, spread_ref[...], preferred_element_type=F32).astype(BF16)
    for copy in weight_copies:
        copy.wait()
    projected = jnp.dot(attn, weight_ref[...], preferred_element_type=F32)
    computed = (residual_ref[...].astype(F32) + projected).astype(BF16)
    slot = lax.broadcasted_iota(jnp.int32, computed.shape, 0)
    enc_out_ref[...] = jnp.where(slot < live_ref[0], computed, jnp.zeros_like(computed))
    normed = layer_norm(computed, norm_gain_ref[...]).astype(BF16)
    bridge_copy.wait()
    bridged = jnp.dot(normed, bridge_ref[...], preferred_element_type=F32) + pe_ref[...]
    dec_normed = layer_norm(bridged.astype(BF16), dec_gain_ref[...]).astype(BF16)
    dec_copy.wait()
    pairs = jnp.dot(dec_normed, dec_weight_ref[...], preferred_element_type=F32)
    main_ref[...] = pairs[: main_ref.shape[0]].astype(BF16)
    last = pairs[main_ref.shape[0] :]
    tail_ref[...] = jnp.broadcast_to(last, tail_ref.shape).astype(BF16)


def kept_kernel(kept_ref, gain_ref, weight_ref, query_ref, mixed_ref, peak_ref, sum_ref):
    scale = 1.0 / math.sqrt(DEC_HEAD_SIZE)
    normed = layer_norm(kept_ref[...], gain_ref[...]).astype(BF16)
    pairs = jnp.dot(normed, weight_ref[...], preferred_element_type=F32).astype(BF16)
    queries = per_head(query_ref[...], DEC_HEADS, DEC_HEAD_SIZE)
    scores = nt_dot(queries, pairs[:, :DEC_INNER]) * scale
    peak = jnp.max(scores, axis=-1, keepdims=True)
    weights = jnp.exp(scores - peak)
    sum_ref[...] = jnp.sum(weights, axis=-1, keepdims=True)
    peak_ref[...] = peak
    mixed = jnp.dot(weights.astype(BF16), pairs[:, DEC_INNER:], preferred_element_type=F32)
    mixed_ref[...] = gathered_heads(mixed, DEC_HEADS, DEC_HEAD_SIZE, 0)


def visible_kernel(
    main_ref,
    tail_ref,
    main_mask_ref,
    tail_mask_ref,
    query_ref,
    mixed_ref,
    peak_ref,
    sum_ref,
    own_ref,
    other_ref,
    rows_ref,
):
    rows_ref[...] = jnp.zeros_like(rows_ref)
    for z in range(main_ref.shape[0]):
        rows_ref[z, : main_ref.shape[1]] = main_ref[z]
    main_rows = rows_ref[...].reshape(-1, 2 * DEC_INNER)
    scale = 1.0 / math.sqrt(DEC_HEAD_SIZE)
    queries = per_head(query_ref[...], DEC_HEADS, DEC_HEAD_SIZE)
    main = nt_dot(queries, main_rows[:, :DEC_INNER]) * scale
    main = jnp.where(main_mask_ref[...] > 0.0, main, NEG_FILL)
    tail = nt_dot(queries, tail_ref[:, :DEC_INNER]) * scale
    tail = jnp.where(tail_mask_ref[...] > 0.0, tail, NEG_FILL)
    peak = jnp.maximum(
        jnp.maximum(peak_ref[...], jnp.max(main, axis=-1, keepdims=True)),
        jnp.max(tail, axis=-1, keepdims=True),
    )
    main = jnp.exp(main - peak)
    tail = jnp.exp(tail - peak)
    fade = jnp.exp(peak_ref[...] - peak)
    summed = (
        sum_ref[...] * fade
        + jnp.sum(main, axis=-1, keepdims=True)
        + jnp.sum(tail, axis=-1, keepdims=True)
    )
    mixed = jnp.dot(main.astype(BF16), main_rows[:, DEC_INNER:], preferred_element_type=F32)
    mixed += jnp.dot(tail.astype(BF16), tail_ref[:, DEC_INNER:], preferred_element_type=F32)
    total = gathered_heads(mixed, DEC_HEADS, DEC_HEAD_SIZE, 0)
    total += mixed_ref[...] * spread_heads(fade, DEC_HEADS, DEC_HEAD_SIZE)
    count = total.shape[0]
    lane = lax.broadcasted_iota(jnp.int32, (count, LANES), 1)
    stats = jnp.zeros((count, LANES), F32)
    for h in range(DEC_HEADS):
        stats = jnp.where(lane == h, peak[h * count : (h + 1) * count], stats)
        stats = jnp.where(lane == DEC_HEADS + h, summed[h * count : (h + 1) * count], stats)
    half = count // 2
    own_ref[:, :DEC_INNER] = total[:half]
    own_ref[:, DEC_INNER:] = stats[:half]
    other_ref[:, :DEC_INNER] = total[half:]
    other_ref[:, DEC_INNER:] = stats[half:]


def finish_kernel(own_ref, received_ref, kept_ref, weight_ref, out_ref):
    shape = (own_ref.shape[0], DEC_INNER)
    total = jnp.zeros(shape, F32)
    for h in range(DEC_HEADS):
        own_peak = own_ref[:, DEC_INNER + h : DEC_INNER + h + 1]
        far_peak = received_ref[:, DEC_INNER + h : DEC_INNER + h + 1]
        place = DEC_INNER + DEC_HEADS + h
        peak = jnp.maximum(own_peak, far_peak)
        own_fade = jnp.exp(own_peak - peak)
        far_fade = jnp.exp(far_peak - peak)
        summed = own_fade * own_ref[:, place : place + 1] + far_fade * received_ref[
            :, place : place + 1
        ]
        mixed = (
            own_fade * own_ref[:, :DEC_INNER] + far_fade * received_ref[:, :DEC_INNER]
        ) / summed
        total = jnp.where(head_column(shape, h, DEC_HEAD_SIZE, 0), mixed, total)
    projected = jnp.dot(total.astype(BF16), weight_ref[...], preferred_element_type=F32)
    out_ref[...] = (kept_ref[...].astype(F32) + projected).astype(BF16)


def call(kernel, out_shape, *operands, scalars=0, in_hbm=(), scratch=()):
    in_vmem = pl.BlockSpec(memory_space=pltpu.VMEM)
    specs = [in_vmem] * len(operands)
    for k in range(scalars):
        specs[k] = pl.BlockSpec(memory_space=pltpu.SMEM)
    for k in in_hbm:
        specs[k] = pl.BlockSpec(memory_space=pl.ANY)
    return pl.pallas_call(
        kernel,
        out_shape=out_shape,
        in_specs=specs,
        out_specs=jax.tree.map(lambda _: in_vmem, out_shape),
        scratch_shapes=list(scratch),
        compiler_params=pltpu.CompilerParams(vmem_limit_bytes=56 * 1024 * 1024),
    )(*operands)


def body(
    enc_rows,
    vis_count,
    vis_dest,
    vis_pos,
    kept_pos,
    out_weight,
    norm_gain,
    bridge_weight,
    mask_token,
    dec_gain,
    dec_qkv_weight,
    dec_out_weight,
):
    row_block = ROW_BLOCK
    shape_of = jax.ShapeDtypeStruct
    myself = lax.axis_index(SEQ)
    core = lax.axis_index("core")
    chips = lax.axis_size("z")
    bal_counts = balance_table(vis_count, row_block)
    has_own = vis_count[myself] > 0

    pair_rows = enc_rows[:, ENC_INNER : 3 * ENC_INNER]
    key_value = jnp.where(has_own, pair_rows[:row_block], shifted(pair_rows[row_block:], SEQ, 1))
    seq_devices = lax.axis_size(SEQ)
    weight_rows = out_weight.shape[0]
    padded_weight = jnp.pad(out_weight, ((0, WEIGHT_ROWS - weight_rows), (0, 0)))
    packet = jnp.concatenate([key_value, padded_weight], axis=0)
    packets = lax.all_gather(packet, SEQ, axis=0, tiled=True).reshape(seq_devices, -1, packet.shape[1])
    enc_late, kept_pos, _ = lax.optimization_barrier((enc_rows, kept_pos, key_value))

    kept_dev = kept_pos.shape[0]
    kept_all = lax.all_to_all(
        jnp.broadcast_to(kept_pos[None, :], (chips, kept_dev)), "z", 0, 0, tiled=True
    )
    kept_all = kept_all.reshape(-1).astype(F32)

    rest = jnp.concatenate([enc_late[:, :ENC_INNER], enc_late[:, 3 * ENC_INNER :]], axis=1)
    rest = jnp.where(has_own, rest[:row_block], shifted(rest[row_block:], SEQ, 1))
    queries = jnp.pad(rest[:, :ENC_INNER], ((0, 0), (0, ENC_SHIFT)))
    residual = rest[:, ENC_INNER:]

    kept_in = (mask_token.astype(F32)[None, :] + sinusoid(kept_pos)).astype(BF16)
    own_normed = layer_norm(kept_in, dec_gain[None, :]).astype(BF16)
    asking = jnp.dot(
        own_normed, dec_qkv_weight[:, :DEC_INNER], preferred_element_type=F32
    ).astype(BF16)
    asking = jnp.concatenate([asking, swapped(asking)], axis=0)
    mask_split = halves_first(mask_token)
    kept_split = (mask_split.astype(F32)[None, :] + split_sinusoid(kept_all)).astype(BF16)
    asked = asking.shape[0]
    stat = shape_of((DEC_HEADS * asked, 1), F32)
    kept_state = call(
        kept_kernel,
        (shape_of((asked, DEC_INNER), F32), stat, stat),
        kept_split,
        halves_first(dec_gain)[None, :],
        halves_first(dec_qkv_weight[:, DEC_INNER:]),
        asking,
    )

    packets, kept_state = lax.optimization_barrier((packets, kept_state))

    first_row = jnp.where(has_own, myself * 2 * row_block, (myself - 1) * 2 * row_block + row_block)
    bal_pos = lax.dynamic_slice_in_dim(vis_pos, first_row, row_block)
    within = jnp.arange(row_block, dtype=jnp.int32)
    live = (within[None, :] < bal_counts[:, None]).astype(F32)
    source = jnp.arange(ENC_WINDOW, dtype=jnp.int32)[:, None] - ENC_SHIFT
    place = jnp.arange(seq_devices * WEIGHT_ROWS, dtype=jnp.int32)[None, :]
    block = place // WEIGHT_ROWS
    inside = place - block * WEIGHT_ROWS
    spread = ((source == block * weight_rows + inside) & (inside < weight_rows)).astype(BF16)
    split = row_block - VIS_TAIL
    pair_width = 2 * DEC_INNER
    model_width = residual.shape[1]
    slots = seq_devices * row_block
    enc_out, vis_main, vis_tail = call(
        encoder_kernel,
        (
            shape_of((row_block, model_width), BF16),
            shape_of((split, pair_width), BF16),
            shape_of((chips, pair_width), BF16),
        ),
        bal_counts[myself][None],
        packets,
        queries,
        live.reshape(1, -1),
        residual,
        spread,
        norm_gain[None, :],
        bridge_weight,
        sinusoid(bal_pos),
        dec_gain[None, :],
        dec_qkv_weight[:, DEC_INNER:],
        scalars=1,
        in_hbm=(1, 7, 10),
        scratch=(
            pltpu.VMEM((slots, 2 * ENC_INNER), BF16),
            pltpu.VMEM((seq_devices * WEIGHT_ROWS, model_width), BF16),
            pltpu.VMEM(bridge_weight.shape, BF16),
            pltpu.VMEM((DEC_WIDTH, pair_width), BF16),
            pltpu.VMEM((ENC_HEADS * row_block, slots), F32),
            pltpu.SemaphoreType.DMA((seq_devices,)),
            pltpu.SemaphoreType.DMA((seq_devices,)),
            pltpu.SemaphoreType.DMA((2,)),
        ),
    )

    vis_tail = lax.all_to_all(vis_tail, "z", 0, 0, tiled=True)
    vis_main = lax.all_gather(vis_main, "z", axis=0)
    live_same = lax.dynamic_index_in_dim(
        live.reshape(chips, -1, row_block), core, axis=1, keepdims=False
    )
    half = shape_of((kept_dev, DEC_INNER + LANES), F32)
    own_part, other_part = call(
        visible_kernel,
        (half, half),
        vis_main,
        vis_tail,
        jnp.where(within[None, :] < split, live_same, 0.0).reshape(1, -1),
        live_same[:, split:].reshape(1, -1),
        asking,
        *kept_state,
        scratch=(pltpu.VMEM((chips, row_block, pair_width), BF16),),
    )
    dec_out = call(
        finish_kernel,
        shape_of((kept_dev, DEC_WIDTH), BF16),
        own_part,
        swapped(other_part),
        kept_in,
        dec_out_weight,
    )
    return (enc_out, dec_out)


def solution(mesh):
    finer = Mesh(mesh.devices.reshape(mesh.shape["clip"], 16, 2), CLIP_SEQ)
    return jax.shard_map(
        body,
        mesh=finer,
        in_specs=(
            P(CLIP_SEQ, None),
            P("clip"),
            P("clip"),
            P("clip"),
            P(CLIP_SEQ),
            P(SEQ, None),
            P(),
            P(),
            P(),
            P(),
            P(),
            P(),
        ),
        out_specs=(P(CLIP_SEQ, None), P(CLIP_SEQ, None)),
        check_vma=False,
    )
```

```python
import math

import jax
import jax.numpy as jnp
import numpy as np
from jax import lax
from jax.experimental import pallas as pl
from jax.experimental.pallas import tpu as pltpu
from jax.sharding import Mesh
from jax.sharding import PartitionSpec as P

HEAD_SIZE = 88
ENC_HEADS = 8
ENC_INNER = ENC_HEADS * HEAD_SIZE
DEC_WIDTH = 512
DEC_HEAD_SIZE = 64
DEC_HEADS = 4
DEC_INNER = DEC_HEADS * DEC_HEAD_SIZE
ROW_BLOCK = 64
WEIGHT_ROWS = 24
ENC_CHUNKS = 4
LANES = 128
SEQ = ("far", "chip", "core")
NEAR = ("chip", "core")
CLIP_SEQ = ("clip", "far", "chip", "core")
NEAR_CHIPS = 2
ENC_WINDOW = 768
ENC_SHIFT = ENC_WINDOW - ENC_INNER

LOG2_E = math.log2(math.e)
NEG_FILL = -1e30
LN_EPS = 1e-06
F32 = jnp.float32
BF16 = jnp.bfloat16


def shifted(shard, axis, by):
    devices = lax.axis_size(axis)
    pairs = [(i, i + by) for i in range(devices) if 0 <= i + by < devices]
    return lax.ppermute(shard, axis, pairs)


def layer_norm(rows_in, gain_row):
    widened = rows_in.astype(F32)
    centred = widened - jnp.mean(widened, axis=-1, keepdims=True)
    spread = jnp.mean(centred * centred, axis=-1, keepdims=True)
    return centred * lax.rsqrt(spread + LN_EPS) * gain_row


def frequencies():
    half = np.arange(DEC_WIDTH // 2)
    return jnp.asarray(np.power(10000.0, -half * 2.0 / DEC_WIDTH).astype(np.float32))


def sinusoid(positions):
    angles = positions.astype(F32)[:, None] * frequencies()[None, :]
    return jnp.stack([jnp.sin(angles), jnp.cos(angles)], axis=-1).reshape(
        positions.shape[0], DEC_WIDTH
    )


def split_sinusoid(positions):
    angles = positions[:, None] * frequencies()[None, :]
    return jnp.concatenate([jnp.sin(angles), jnp.cos(angles)], axis=-1)


def halves_first(rows):
    apart = rows.reshape(rows.shape[0] // 2, 2, *rows.shape[1:])
    return jnp.concatenate([apart[:, 0], apart[:, 1]], axis=0)


def balance_table(vis_count, row_block):
    left_count = jnp.concatenate([vis_count[:1] * 0, vis_count[:-1]], axis=0)
    return jnp.where(vis_count > 0, jnp.minimum(vis_count, row_block), left_count - row_block)


def nt_dot(left, right):
    return lax.dot_general(left, right, (((1,), (1,)), ((), ())), preferred_element_type=F32)


def head_column(shape, head, size, offset):
    column = lax.broadcasted_iota(jnp.int32, shape, 1) - offset
    return (column >= head * size) & (column < (head + 1) * size)


def per_head(rows, heads, size):
    copies = [
        jnp.where(head_column(rows.shape, h, size, 0), rows, jnp.zeros_like(rows))
        for h in range(heads)
    ]
    return jnp.concatenate(copies, axis=0)


def gathered_heads(stacked, heads, size, offset):
    count = stacked.shape[0] // heads
    shape = (count, stacked.shape[1])
    total = jnp.zeros(shape, F32)
    for h in range(heads):
        mine = head_column(shape, h, size, offset)
        total = jnp.where(mine, stacked[h * count : (h + 1) * count], total)
    return total


def spread_heads(column, heads, size):
    count = column.shape[0] // heads
    shape = (count, heads * size)
    total = jnp.zeros(shape, F32)
    for h in range(heads):
        total = jnp.where(
            head_column(shape, h, size, 0), column[h * count : (h + 1) * count], total
        )
    return total


def encoder_kernel(
    live_ref,
    packets_hbm,
    query_ref,
    mask_ref,
    residual_ref,
    spread_ref,
    norm_gain_ref,
    bridge_hbm,
    pe_ref,
    dec_gain_ref,
    dec_weight_hbm,
    enc_out_ref,
    vis_ref,
    kv_ref,
    weight_ref,
    bridge_ref,
    dec_weight_ref,
    scores_ref,
    kv_sems,
    weight_sems,
    other_sems,
):
    devices = packets_hbm.shape[0]
    kv_copies = [
        pltpu.make_async_copy(
            packets_hbm.at[d, pl.ds(0, ROW_BLOCK)],
            kv_ref.at[pl.ds(d * ROW_BLOCK, ROW_BLOCK)],
            kv_sems.at[d],
        )
        for d in range(devices)
    ]
    weight_copies = [
        pltpu.make_async_copy(
            packets_hbm.at[d, pl.ds(ROW_BLOCK, WEIGHT_ROWS)],
            weight_ref.at[pl.ds(d * WEIGHT_ROWS, WEIGHT_ROWS)],
            weight_sems.at[d],
        )
        for d in range(devices)
    ]
    bridge_copy = pltpu.make_async_copy(bridge_hbm, bridge_ref, other_sems.at[0])
    dec_copy = pltpu.make_async_copy(dec_weight_hbm, dec_weight_ref, other_sems.at[1])
    for copy in kv_copies + weight_copies + [bridge_copy, dec_copy]:
        copy.start()
    scale = LOG2_E / math.sqrt(HEAD_SIZE)
    queries = per_head(query_ref[...], ENC_HEADS, HEAD_SIZE)
    per_chunk = devices // ENC_CHUNKS
    width = per_chunk * ROW_BLOCK
    peak = None
    for chunk in range(ENC_CHUNKS):
        for copy in kv_copies[chunk * per_chunk : (chunk + 1) * per_chunk]:
            copy.wait()
        here = slice(chunk * width, (chunk + 1) * width)
        scores = nt_dot(queries, kv_ref[here, :ENC_WINDOW])
        scores = jnp.where(mask_ref[:, here] > 0.0, scores, NEG_FILL)
        scores_ref[:, here] = scores
        top = jnp.max(scores, axis=-1, keepdims=True)
        peak = top if peak is None else jnp.maximum(peak, top)
    summed = 0.0
    mixed = 0.0
    for chunk in range(ENC_CHUNKS):
        here = slice(chunk * width, (chunk + 1) * width)
        weights = jnp.exp2((scores_ref[:, here] - peak) * scale)
        summed += jnp.sum(weights, axis=-1, keepdims=True)
        mixed += jnp.dot(
            weights.astype(BF16),
            kv_ref[here, 2 * ENC_INNER - ENC_WINDOW :],
            preferred_element_type=F32,
        )
    attn = gathered_heads(mixed / summed, ENC_HEADS, HEAD_SIZE, ENC_SHIFT).astype(BF16)
    attn = jnp.dot(attn, spread_ref[...], preferred_element_type=F32).astype(BF16)
    for copy in weight_copies:
        copy.wait()
    projected = jnp.dot(attn, weight_ref[...], preferred_element_type=F32)
    computed = (residual_ref[...].astype(F32) + projected).astype(BF16)
    slot = lax.broadcasted_iota(jnp.int32, computed.shape, 0)
    enc_out_ref[...] = jnp.where(slot < live_ref[0], computed, jnp.zeros_like(computed))
    normed = layer_norm(computed, norm_gain_ref[...]).astype(BF16)
    bridge_copy.wait()
    bridged = jnp.dot(normed, bridge_ref[...], preferred_element_type=F32) + pe_ref[...]
    dec_normed = layer_norm(bridged.astype(BF16), dec_gain_ref[...]).astype(BF16)
    dec_copy.wait()
    pairs = jnp.dot(dec_normed, dec_weight_ref[...], preferred_element_type=F32)
    vis_ref[...] = pairs.astype(BF16)


def kept_kernel(kept_ref, gain_ref, weight_ref, query_ref, mixed_ref, peak_ref, sum_ref):
    scale = LOG2_E / math.sqrt(DEC_HEAD_SIZE)
    normed = layer_norm(kept_ref[...], gain_ref[...]).astype(BF16)
    pairs = jnp.dot(normed, weight_ref[...], preferred_element_type=F32).astype(BF16)
    queries = per_head(query_ref[...], DEC_HEADS, DEC_HEAD_SIZE)
    scores = nt_dot(queries, pairs[:, :DEC_INNER])
    peak = jnp.max(scores, axis=-1, keepdims=True)
    weights = jnp.exp2((scores - peak) * scale)
    sum_ref[...] = jnp.sum(weights, axis=-1, keepdims=True)
    peak_ref[...] = peak
    mixed = jnp.dot(weights.astype(BF16), pairs[:, DEC_INNER:], preferred_element_type=F32)
    mixed_ref[...] = gathered_heads(mixed, DEC_HEADS, DEC_HEAD_SIZE, 0)


def visible_kernel(vis_ref, mask_ref, query_ref, mixed_ref, peak_ref, sum_ref, out_ref):
    scale = LOG2_E / math.sqrt(DEC_HEAD_SIZE)
    queries = per_head(query_ref[...], DEC_HEADS, DEC_HEAD_SIZE)
    scores = nt_dot(queries, vis_ref[:, :DEC_INNER])
    scores = jnp.where(mask_ref[...] > 0.0, scores, NEG_FILL)
    peak = jnp.maximum(peak_ref[...], jnp.max(scores, axis=-1, keepdims=True))
    weights = jnp.exp2((scores - peak) * scale)
    fade = jnp.exp2((peak_ref[...] - peak) * scale)
    summed = sum_ref[...] * fade + jnp.sum(weights, axis=-1, keepdims=True)
    mixed = jnp.dot(weights.astype(BF16), vis_ref[:, DEC_INNER:], preferred_element_type=F32)
    total = gathered_heads(mixed, DEC_HEADS, DEC_HEAD_SIZE, 0)
    total += mixed_ref[...] * spread_heads(fade, DEC_HEADS, DEC_HEAD_SIZE)
    count = total.shape[0]
    lane = lax.broadcasted_iota(jnp.int32, (count, LANES), 1)
    stats = jnp.zeros((count, LANES), F32)
    for h in range(DEC_HEADS):
        stats = jnp.where(lane == h, peak[h * count : (h + 1) * count], stats)
        stats = jnp.where(lane == DEC_HEADS + h, summed[h * count : (h + 1) * count], stats)
    near, rows = out_ref.shape[:2]
    for k in range(near):
        out_ref[k, :, :DEC_INNER] = total[k * rows : (k + 1) * rows]
        out_ref[k, :, DEC_INNER:] = stats[k * rows : (k + 1) * rows]


def finish_kernel(parts_ref, kept_ref, weight_ref, out_ref):
    scale = LOG2_E / math.sqrt(DEC_HEAD_SIZE)
    near, rows = parts_ref.shape[:2]
    shape = (rows, DEC_INNER)
    stats = [parts_ref[k, :, DEC_INNER:] for k in range(near)]
    peak = stats[0]
    for k in range(1, near):
        peak = jnp.maximum(peak, stats[k])
    fades = [jnp.exp2((stats[k] - peak) * scale) for k in range(near)]
    total = jnp.zeros(shape, F32)
    summed = jnp.ones(shape, F32)
    for h in range(DEC_HEADS):
        place = DEC_HEADS + h
        mixed = 0.0
        weight = 0.0
        for k in range(near):
            fade = fades[k][:, h : h + 1]
            mixed += fade * parts_ref[k, :, :DEC_INNER]
            weight += fade * stats[k][:, place : place + 1]
        mine = head_column(shape, h, DEC_HEAD_SIZE, 0)
        total = jnp.where(mine, mixed, total)
        summed = jnp.where(mine, weight, summed)
    attn = (total / summed).astype(BF16)
    projected = jnp.dot(attn, weight_ref[...], preferred_element_type=F32)
    out_ref[...] = (kept_ref[...].astype(F32) + projected).astype(BF16)


def call(kernel, out_shape, *operands, scalars=0, in_hbm=(), scratch=()):
    in_vmem = pl.BlockSpec(memory_space=pltpu.VMEM)
    specs = [in_vmem] * len(operands)
    for k in range(scalars):
        specs[k] = pl.BlockSpec(memory_space=pltpu.SMEM)
    for k in in_hbm:
        specs[k] = pl.BlockSpec(memory_space=pl.ANY)
    return pl.pallas_call(
        kernel,
        out_shape=out_shape,
        in_specs=specs,
        out_specs=jax.tree.map(lambda _: in_vmem, out_shape),
        scratch_shapes=list(scratch),
        compiler_params=pltpu.CompilerParams(vmem_limit_bytes=56 * 1024 * 1024),
    )(*operands)


def body(
    enc_rows,
    vis_count,
    vis_dest,
    vis_pos,
    kept_pos,
    out_weight,
    norm_gain,
    bridge_weight,
    mask_token,
    dec_gain,
    dec_qkv_weight,
    dec_out_weight,
):
    row_block = ROW_BLOCK
    shape_of = jax.ShapeDtypeStruct
    myself = lax.axis_index(SEQ)
    near = lax.axis_size(NEAR)
    far = lax.axis_size("far")
    bal_counts = balance_table(vis_count, row_block)
    has_own = vis_count[myself] > 0

    pair_rows = enc_rows[:, ENC_INNER : 3 * ENC_INNER]
    key_value = jnp.where(has_own, pair_rows[:row_block], shifted(pair_rows[row_block:], SEQ, 1))
    seq_devices = lax.axis_size(SEQ)
    weight_rows = out_weight.shape[0]
    padded_weight = jnp.pad(out_weight, ((0, WEIGHT_ROWS - weight_rows), (0, 0)))
    packet = jnp.concatenate([key_value, padded_weight], axis=0)
    packets = lax.all_gather(packet, SEQ, axis=0, tiled=True).reshape(seq_devices, -1, packet.shape[1])
    enc_late, kept_pos, _ = lax.optimization_barrier((enc_rows, kept_pos, key_value))

    kept_dev = kept_pos.shape[0]
    kept_all = lax.all_to_all(
        jnp.broadcast_to(kept_pos[None, :], (far, kept_dev)), "far", 0, 0, tiled=True
    )
    kept_all = kept_all.reshape(-1).astype(F32)

    rest = jnp.concatenate([enc_late[:, :ENC_INNER], enc_late[:, 3 * ENC_INNER :]], axis=1)
    rest = jnp.where(has_own, rest[:row_block], shifted(rest[row_block:], SEQ, 1))
    queries = jnp.pad(rest[:, :ENC_INNER], ((0, 0), (0, ENC_SHIFT)))
    residual = rest[:, ENC_INNER:]

    kept_in = (mask_token.astype(F32)[None, :] + sinusoid(kept_pos)).astype(BF16)
    own_normed = layer_norm(kept_in, dec_gain[None, :]).astype(BF16)
    asking = jnp.dot(
        own_normed, dec_qkv_weight[:, :DEC_INNER], preferred_element_type=F32
    ).astype(BF16)
    asking = lax.all_gather(asking, NEAR, axis=0, tiled=True)
    mask_split = halves_first(mask_token)
    kept_split = (mask_split.astype(F32)[None, :] + split_sinusoid(kept_all)).astype(BF16)
    asked = asking.shape[0]
    stat = shape_of((DEC_HEADS * asked, 1), F32)
    kept_state = call(
        kept_kernel,
        (shape_of((asked, DEC_INNER), F32), stat, stat),
        kept_split,
        halves_first(dec_gain)[None, :],
        halves_first(dec_qkv_weight[:, DEC_INNER:]),
        asking,
    )

    packets, kept_state = lax.optimization_barrier((packets, kept_state))

    first_row = jnp.where(has_own, myself * 2 * row_block, (myself - 1) * 2 * row_block + row_block)
    bal_pos = lax.dynamic_slice_in_dim(vis_pos, first_row, row_block)
    within = jnp.arange(row_block, dtype=jnp.int32)
    live = (within[None, :] < bal_counts[:, None]).astype(F32)
    source = jnp.arange(ENC_WINDOW, dtype=jnp.int32)[:, None] - ENC_SHIFT
    place = jnp.arange(seq_devices * WEIGHT_ROWS, dtype=jnp.int32)[None, :]
    block = place // WEIGHT_ROWS
    inside = place - block * WEIGHT_ROWS
    spread = ((source == block * weight_rows + inside) & (inside < weight_rows)).astype(BF16)
    pair_width = 2 * DEC_INNER
    model_width = residual.shape[1]
    slots = seq_devices * row_block
    enc_out, vis_kv = call(
        encoder_kernel,
        (
            shape_of((row_block, model_width), BF16),
            shape_of((row_block, pair_width), BF16),
        ),
        bal_counts[myself][None],
        packets,
        queries,
        live.reshape(1, -1),
        residual,
        spread,
        norm_gain[None, :],
        bridge_weight,
        sinusoid(bal_pos),
        dec_gain[None, :],
        dec_qkv_weight[:, DEC_INNER:],
        scalars=1,
        in_hbm=(1, 7, 10),
        scratch=(
            pltpu.VMEM((slots, 2 * ENC_INNER), BF16),
            pltpu.VMEM((seq_devices * WEIGHT_ROWS, model_width), BF16),
            pltpu.VMEM(bridge_weight.shape, BF16),
            pltpu.VMEM((DEC_WIDTH, pair_width), BF16),
            pltpu.VMEM((ENC_HEADS * row_block, slots), F32),
            pltpu.SemaphoreType.DMA((seq_devices,)),
            pltpu.SemaphoreType.DMA((seq_devices,)),
            pltpu.SemaphoreType.DMA((2,)),
        ),
    )

    vis_all = lax.all_gather(vis_kv, "far", axis=0, tiled=True)
    live_same = lax.dynamic_index_in_dim(
        live.reshape(far, near, row_block), lax.axis_index(NEAR), axis=1, keepdims=False
    )
    parts = call(
        visible_kernel,
        shape_of((near, kept_dev, DEC_INNER + LANES), F32),
        vis_all,
        live_same.reshape(1, -1),
        asking,
        *kept_state,
    )
    parts = lax.all_to_all(parts, NEAR, 0, 0, tiled=True)
    dec_out = call(
        finish_kernel,
        shape_of((kept_dev, DEC_WIDTH), BF16),
        parts,
        kept_in,
        dec_out_weight,
    )
    return (enc_out, dec_out)


def solution(mesh):
    grid = (mesh.shape["clip"], mesh.shape["seq"] // (2 * NEAR_CHIPS), NEAR_CHIPS, 2)
    finer = Mesh(mesh.devices.reshape(grid), CLIP_SEQ)
    return jax.shard_map(
        body,
        mesh=finer,
        in_specs=(
            P(CLIP_SEQ, None),
            P("clip"),
            P("clip"),
            P("clip"),
            P(CLIP_SEQ),
            P(SEQ, None),
            P(),
            P(),
            P(),
            P(),
            P(),
            P(),
        ),
        out_specs=(P(CLIP_SEQ, None), P(CLIP_SEQ, None)),
        check_vma=False,
    )
```

```python
import math

import jax
import jax.numpy as jnp
import numpy as np
from jax import lax
from jax.experimental import pallas as pl
from jax.experimental.pallas import tpu as pltpu
from jax.sharding import Mesh
from jax.sharding import PartitionSpec as P

HEAD_SIZE = 88
ENC_HEADS = 8
ENC_INNER = ENC_HEADS * HEAD_SIZE
DEC_WIDTH = 512
DEC_HEAD_SIZE = 64
DEC_HEADS = 4
DEC_INNER = DEC_HEADS * DEC_HEAD_SIZE
ROW_BLOCK = 64
WEIGHT_ROWS = 24
ENC_CHUNKS = 2
LANES = 128
SEQ = ("far", "chip", "core")
NEAR = ("chip", "core")
CLIP_SEQ = ("clip", "far", "chip", "core")
NEAR_CHIPS = 2
ENC_WINDOW = 768
ENC_SHIFT = ENC_WINDOW - ENC_INNER
HEAD_PAIRS = ENC_HEADS // 2
PAIR_SIZE = 2 * HEAD_SIZE

LOG2_E = math.log2(math.e)
NEG_FILL = -1e30
LN_EPS = 1e-06
F32 = jnp.float32
BF16 = jnp.bfloat16


def shifted(shard, axis, by):
    devices = lax.axis_size(axis)
    pairs = [(i, i + by) for i in range(devices) if 0 <= i + by < devices]
    return lax.ppermute(shard, axis, pairs)


def layer_norm(rows_in, gain_row):
    widened = rows_in.astype(F32)
    centred = widened - jnp.mean(widened, axis=-1, keepdims=True)
    spread = jnp.mean(centred * centred, axis=-1, keepdims=True)
    return centred * lax.rsqrt(spread + LN_EPS) * gain_row


def frequencies():
    half = np.arange(DEC_WIDTH // 2)
    return jnp.asarray(np.power(10000.0, -half * 2.0 / DEC_WIDTH).astype(np.float32))


def sinusoid(positions):
    angles = positions.astype(F32)[:, None] * frequencies()[None, :]
    return jnp.stack([jnp.sin(angles), jnp.cos(angles)], axis=-1).reshape(
        positions.shape[0], DEC_WIDTH
    )


def split_sinusoid(positions):
    angles = positions[:, None] * frequencies()[None, :]
    return jnp.concatenate([jnp.sin(angles), jnp.cos(angles)], axis=-1)


def halves_first(rows):
    apart = rows.reshape(rows.shape[0] // 2, 2, *rows.shape[1:])
    return jnp.concatenate([apart[:, 0], apart[:, 1]], axis=0)


def balance_table(vis_count, row_block):
    left_count = jnp.concatenate([vis_count[:1] * 0, vis_count[:-1]], axis=0)
    return jnp.where(vis_count > 0, jnp.minimum(vis_count, row_block), left_count - row_block)


def nt_dot(left, right):
    return lax.dot_general(left, right, (((1,), (1,)), ((), ())), preferred_element_type=F32)


def head_column(shape, head, size, offset):
    column = lax.broadcasted_iota(jnp.int32, shape, 1) - offset
    return (column >= head * size) & (column < (head + 1) * size)


def lane_window(start, size):
    first = start // LANES * LANES
    return first, -(-(start + size - first) // LANES) * LANES


def encoder_kernel(
    live_ref,
    packets_hbm,
    query_ref,
    mask_ref,
    residual_ref,
    spread_hbm,
    norm_gain_ref,
    bridge_hbm,
    pe_ref,
    dec_gain_ref,
    dec_weight_hbm,
    enc_out_hbm,
    vis_ref,
    kv_ref,
    weight_ref,
    bridge_ref,
    dec_weight_ref,
    spread_ref,
    attn_ref,
    enc_out_ref,
    kv_sems,
    weight_sems,
    other_sems,
):
    devices = packets_hbm.shape[0]
    kv_copies = [
        pltpu.make_async_copy(
            packets_hbm.at[d, pl.ds(0, ROW_BLOCK)],
            kv_ref.at[pl.ds(d * ROW_BLOCK, ROW_BLOCK)],
            kv_sems.at[d],
        )
        for d in range(devices)
    ]
    weight_copies = [
        pltpu.make_async_copy(
            packets_hbm.at[d, pl.ds(ROW_BLOCK, WEIGHT_ROWS)],
            weight_ref.at[pl.ds(d * WEIGHT_ROWS, WEIGHT_ROWS)],
            weight_sems.at[d],
        )
        for d in range(devices)
    ]
    bridge_copy = pltpu.make_async_copy(bridge_hbm, bridge_ref, other_sems.at[0])
    dec_copy = pltpu.make_async_copy(dec_weight_hbm, dec_weight_ref, other_sems.at[1])
    spread_copy = pltpu.make_async_copy(spread_hbm, spread_ref, other_sems.at[2])
    for copy in kv_copies + [spread_copy] + weight_copies + [bridge_copy, dec_copy]:
        copy.start()
    scale = LOG2_E / math.sqrt(HEAD_SIZE)
    value_base = 2 * ENC_INNER - ENC_WINDOW
    queries = []
    for pair in range(HEAD_PAIRS):
        first, width = lane_window(pair * PAIR_SIZE, PAIR_SIZE)
        part = query_ref[:, first : first + width]
        copies = [
            jnp.where(
                head_column(part.shape, 2 * pair + k, HEAD_SIZE, -first), part, jnp.zeros_like(part)
            )
            for k in range(2)
        ]
        queries.append(jnp.concatenate(copies, axis=0))
    per_chunk = devices // ENC_CHUNKS
    length = per_chunk * ROW_BLOCK
    peaks = [None] * HEAD_PAIRS
    sums = [0.0] * HEAD_PAIRS
    mixes = [0.0] * HEAD_PAIRS
    for chunk in range(ENC_CHUNKS):
        for copy in kv_copies[chunk * per_chunk : (chunk + 1) * per_chunk]:
            copy.wait()
        here = slice(chunk * length, (chunk + 1) * length)
        usable = mask_ref[:, here] > 0.0
        for pair in range(HEAD_PAIRS):
            first, width = lane_window(pair * PAIR_SIZE, PAIR_SIZE)
            scores = nt_dot(queries[pair], kv_ref[here, first : first + width])
            scores = jnp.where(usable, scores, NEG_FILL)
            peak = jnp.max(scores, axis=-1, keepdims=True)
            if chunk > 0:
                peak = jnp.maximum(peaks[pair], peak)
                fade = jnp.exp2((peaks[pair] - peak) * scale)
                sums[pair] *= fade
                mixes[pair] *= fade
            peaks[pair] = peak
            weights = jnp.exp2((scores - peak) * scale)
            sums[pair] += jnp.sum(weights, axis=-1, keepdims=True)
            first, width = lane_window(ENC_SHIFT + pair * PAIR_SIZE, PAIR_SIZE)
            first += value_base
            mixes[pair] += jnp.dot(
                weights.astype(BF16), kv_ref[here, first : first + width], preferred_element_type=F32
            )
    attn_ref[...] = jnp.zeros_like(attn_ref)
    for pair in range(HEAD_PAIRS):
        first, width = lane_window(ENC_SHIFT + pair * PAIR_SIZE, PAIR_SIZE)
        mixed = mixes[pair] / sums[pair]
        part = attn_ref[:, first : first + width]
        for k in range(2):
            mine = head_column(part.shape, 2 * pair + k, HEAD_SIZE, ENC_SHIFT - first)
            part = jnp.where(mine, mixed[k * ROW_BLOCK : (k + 1) * ROW_BLOCK], part)
        attn_ref[:, first : first + width] = part
    attn = attn_ref[...].astype(BF16)
    spread_copy.wait()
    attn = jnp.dot(attn, spread_ref[...], preferred_element_type=F32).astype(BF16)
    for copy in weight_copies:
        copy.wait()
    projected = jnp.dot(attn, weight_ref[...], preferred_element_type=F32)
    computed = (residual_ref[...].astype(F32) + projected).astype(BF16)
    slot = lax.broadcasted_iota(jnp.int32, computed.shape, 0)
    enc_out_ref[...] = jnp.where(slot < live_ref[0], computed, jnp.zeros_like(computed))
    out_copy = pltpu.make_async_copy(enc_out_ref, enc_out_hbm, other_sems.at[3])
    out_copy.start()
    normed = layer_norm(computed, norm_gain_ref[...]).astype(BF16)
    bridge_copy.wait()
    bridged = jnp.dot(normed, bridge_ref[...], preferred_element_type=F32) + pe_ref[...]
    dec_normed = layer_norm(bridged.astype(BF16), dec_gain_ref[...]).astype(BF16)
    dec_copy.wait()
    pairs = jnp.dot(dec_normed, dec_weight_ref[...], preferred_element_type=F32)
    vis_ref[...] = pairs.astype(BF16)
    out_copy.wait()


def head_stats(stats, head, peak, summed):
    lane = lax.broadcasted_iota(jnp.int32, stats.shape, 1)
    stats = jnp.where(lane == head, peak, stats)
    return jnp.where(lane == DEC_HEADS + head, summed, stats)


def coded_stats(stats):
    group = 2 * DEC_HEADS
    high = stats.astype(BF16).astype(F32)
    middle = (stats - high).astype(BF16).astype(F32)
    low = stats - high - middle
    return (high + pltpu.roll(middle, group, 1) + pltpu.roll(low, 2 * group, 1)).astype(BF16)


def decoded_stats(coded):
    group = 2 * DEC_HEADS
    widened = coded.astype(F32)
    middle = pltpu.roll(widened, LANES - group, 1)
    low = pltpu.roll(widened, LANES - 2 * group, 1)
    return widened + (middle + low)


def kept_kernel(kept_ref, gain_ref, weight_ref, query_ref, state_ref):
    scale = LOG2_E / math.sqrt(DEC_HEAD_SIZE)
    normed = layer_norm(kept_ref[...], gain_ref[...]).astype(BF16)
    pairs = jnp.dot(normed, weight_ref[...], preferred_element_type=F32).astype(BF16)
    queries = query_ref[...]
    total = jnp.zeros(queries.shape, F32)
    stats = jnp.zeros((queries.shape[0], LANES), F32)
    for h in range(DEC_HEADS):
        mine = head_column(queries.shape, h, DEC_HEAD_SIZE, 0)
        scores = nt_dot(jnp.where(mine, queries, jnp.zeros_like(queries)), pairs[:, :DEC_INNER])
        peak = jnp.max(scores, axis=-1, keepdims=True)
        weights = jnp.exp2((scores - peak) * scale)
        stats = head_stats(stats, h, peak, jnp.sum(weights, axis=-1, keepdims=True))
        mixed = jnp.dot(weights.astype(BF16), pairs[:, DEC_INNER:], preferred_element_type=F32)
        total = jnp.where(mine, mixed, total)
    state_ref[:, :DEC_INNER] = total
    state_ref[:, DEC_INNER:] = stats


def visible_kernel(vis_ref, mask_ref, query_ref, state_ref, out_ref):
    scale = LOG2_E / math.sqrt(DEC_HEAD_SIZE)
    usable = mask_ref[...] > 0.0
    queries = query_ref[...]
    total = jnp.zeros(queries.shape, F32)
    stats = jnp.zeros((queries.shape[0], LANES), F32)
    for h in range(DEC_HEADS):
        place = DEC_INNER + h
        kept_peak = state_ref[:, place : place + 1]
        kept_sum = state_ref[:, place + DEC_HEADS : place + DEC_HEADS + 1]
        mine = head_column(queries.shape, h, DEC_HEAD_SIZE, 0)
        scores = nt_dot(jnp.where(mine, queries, jnp.zeros_like(queries)), vis_ref[:, :DEC_INNER])
        scores = jnp.where(usable, scores, NEG_FILL)
        peak = jnp.maximum(kept_peak, jnp.max(scores, axis=-1, keepdims=True))
        weights = jnp.exp2((scores - peak) * scale)
        fade = jnp.exp2((kept_peak - peak) * scale)
        summed = kept_sum * fade + jnp.sum(weights, axis=-1, keepdims=True)
        stats = head_stats(stats, h, peak, summed)
        mixed = jnp.dot(weights.astype(BF16), vis_ref[:, DEC_INNER:], preferred_element_type=F32)
        total = jnp.where(mine, mixed + fade * state_ref[:, :DEC_INNER], total)
    near, rows = out_ref.shape[:2]
    for k in range(near):
        out_ref[k, :, :DEC_INNER] = total[k * rows : (k + 1) * rows].astype(BF16)
        out_ref[k, :, DEC_INNER:] = coded_stats(stats[k * rows : (k + 1) * rows])


def finish_kernel(parts_ref, kept_ref, weight_ref, out_ref):
    scale = LOG2_E / math.sqrt(DEC_HEAD_SIZE)
    near, rows = parts_ref.shape[:2]
    shape = (rows, DEC_INNER)
    stats = [decoded_stats(parts_ref[k, :, DEC_INNER:]) for k in range(near)]
    mixes = [parts_ref[k, :, :DEC_INNER].astype(F32) for k in range(near)]
    peak = stats[0]
    for k in range(1, near):
        peak = jnp.maximum(peak, stats[k])
    fades = [jnp.exp2((stats[k] - peak) * scale) for k in range(near)]
    total = jnp.zeros(shape, F32)
    summed = jnp.ones(shape, F32)
    for h in range(DEC_HEADS):
        place = DEC_HEADS + h
        mixed = 0.0
        weight = 0.0
        for k in range(near):
            fade = fades[k][:, h : h + 1]
            mixed += fade * mixes[k]
            weight += fade * stats[k][:, place : place + 1]
        mine = head_column(shape, h, DEC_HEAD_SIZE, 0)
        total = jnp.where(mine, mixed, total)
        summed = jnp.where(mine, weight, summed)
    attn = (total / summed).astype(BF16)
    projected = jnp.dot(attn, weight_ref[...], preferred_element_type=F32)
    out_ref[...] = (kept_ref[...].astype(F32) + projected).astype(BF16)


def call(kernel, out_shape, *operands, scalars=0, in_hbm=(), out_hbm=(), scratch=()):
    in_vmem = pl.BlockSpec(memory_space=pltpu.VMEM)
    specs = [in_vmem] * len(operands)
    for k in range(scalars):
        specs[k] = pl.BlockSpec(memory_space=pltpu.SMEM)
    for k in in_hbm:
        specs[k] = pl.BlockSpec(memory_space=pl.ANY)
    out_specs = jax.tree.map(lambda _: in_vmem, out_shape)
    for k in out_hbm:
        out_specs = out_specs[:k] + (pl.BlockSpec(memory_space=pl.ANY),) + out_specs[k + 1 :]
    return pl.pallas_call(
        kernel,
        out_shape=out_shape,
        in_specs=specs,
        out_specs=out_specs,
        scratch_shapes=list(scratch),
        compiler_params=pltpu.CompilerParams(vmem_limit_bytes=56 * 1024 * 1024),
    )(*operands)


def body(
    enc_rows,
    vis_count,
    vis_dest,
    vis_pos,
    kept_pos,
    out_weight,
    norm_gain,
    bridge_weight,
    mask_token,
    dec_gain,
    dec_qkv_weight,
    dec_out_weight,
):
    row_block = ROW_BLOCK
    shape_of = jax.ShapeDtypeStruct
    myself = lax.axis_index(SEQ)
    near = lax.axis_size(NEAR)
    far = lax.axis_size("far")
    bal_counts = balance_table(vis_count, row_block)
    has_own = vis_count[myself] > 0

    pair_rows = enc_rows[:, ENC_INNER : 3 * ENC_INNER]
    key_value = jnp.where(has_own, pair_rows[:row_block], shifted(pair_rows[row_block:], SEQ, 1))
    seq_devices = lax.axis_size(SEQ)
    weight_rows = out_weight.shape[0]
    padded_weight = jnp.pad(out_weight, ((0, WEIGHT_ROWS - weight_rows), (0, 0)))
    packet = jnp.concatenate([key_value, padded_weight], axis=0)
    packets = lax.all_gather(packet, SEQ, axis=0, tiled=True).reshape(seq_devices, -1, packet.shape[1])
    enc_late, kept_pos, _ = lax.optimization_barrier((enc_rows, kept_pos, key_value))

    kept_dev = kept_pos.shape[0]
    kept_all = lax.all_to_all(
        jnp.broadcast_to(kept_pos[None, :], (far, kept_dev)), "far", 0, 0, tiled=True
    )
    kept_all = kept_all.reshape(-1).astype(F32)

    rest = jnp.concatenate([enc_late[:, :ENC_INNER], enc_late[:, 3 * ENC_INNER :]], axis=1)
    rest = jnp.where(has_own, rest[:row_block], shifted(rest[row_block:], SEQ, 1))
    queries = jnp.pad(rest[:, :ENC_INNER], ((0, 0), (0, ENC_SHIFT)))
    residual = rest[:, ENC_INNER:]

    kept_in = (mask_token.astype(F32)[None, :] + sinusoid(kept_pos)).astype(BF16)
    own_normed = layer_norm(kept_in, dec_gain[None, :]).astype(BF16)
    asking = jnp.dot(
        own_normed, dec_qkv_weight[:, :DEC_INNER], preferred_element_type=F32
    ).astype(BF16)
    asking = lax.all_gather(asking, NEAR, axis=0, tiled=True)
    mask_split = halves_first(mask_token)
    kept_split = (mask_split.astype(F32)[None, :] + split_sinusoid(kept_all)).astype(BF16)
    asked = asking.shape[0]
    kept_state = call(
        kept_kernel,
        shape_of((asked, DEC_INNER + LANES), F32),
        kept_split,
        halves_first(dec_gain)[None, :],
        halves_first(dec_qkv_weight[:, DEC_INNER:]),
        asking,
    )

    packets, kept_state = lax.optimization_barrier((packets, kept_state))

    first_row = jnp.where(has_own, myself * 2 * row_block, (myself - 1) * 2 * row_block + row_block)
    bal_pos = lax.dynamic_slice_in_dim(vis_pos, first_row, row_block)
    within = jnp.arange(row_block, dtype=jnp.int32)
    live = (within[None, :] < bal_counts[:, None]).astype(F32)
    source = jnp.arange(ENC_WINDOW, dtype=jnp.int32)[:, None] - ENC_SHIFT
    place = jnp.arange(seq_devices * WEIGHT_ROWS, dtype=jnp.int32)[None, :]
    block = place // WEIGHT_ROWS
    inside = place - block * WEIGHT_ROWS
    spread = ((source == block * weight_rows + inside) & (inside < weight_rows)).astype(BF16)
    pair_width = 2 * DEC_INNER
    model_width = residual.shape[1]
    slots = seq_devices * row_block
    enc_out, vis_kv = call(
        encoder_kernel,
        (
            shape_of((row_block, model_width), BF16),
            shape_of((row_block, pair_width), BF16),
        ),
        bal_counts[myself][None],
        packets,
        queries,
        live.reshape(1, -1),
        residual,
        spread,
        norm_gain[None, :],
        bridge_weight,
        sinusoid(bal_pos),
        dec_gain[None, :],
        dec_qkv_weight[:, DEC_INNER:],
        scalars=1,
        in_hbm=(1, 5, 7, 10),
        out_hbm=(0,),
        scratch=(
            pltpu.VMEM((slots, 2 * ENC_INNER), BF16),
            pltpu.VMEM((seq_devices * WEIGHT_ROWS, model_width), BF16),
            pltpu.VMEM(bridge_weight.shape, BF16),
            pltpu.VMEM((DEC_WIDTH, pair_width), BF16),
            pltpu.VMEM(spread.shape, BF16),
            pltpu.VMEM((row_block, ENC_WINDOW), F32),
            pltpu.VMEM((row_block, model_width), BF16),
            pltpu.SemaphoreType.DMA((seq_devices,)),
            pltpu.SemaphoreType.DMA((seq_devices,)),
            pltpu.SemaphoreType.DMA((4,)),
        ),
    )

    vis_all = lax.all_gather(vis_kv, "far", axis=0, tiled=True)
    live_same = lax.dynamic_index_in_dim(
        live.reshape(far, near, row_block), lax.axis_index(NEAR), axis=1, keepdims=False
    )
    parts = call(
        visible_kernel,
        shape_of((near, kept_dev, DEC_INNER + LANES), BF16),
        vis_all,
        live_same.reshape(1, -1),
        asking,
        kept_state,
    )
    parts = lax.all_to_all(parts, NEAR, 0, 0, tiled=True)
    dec_out = call(
        finish_kernel,
        shape_of((kept_dev, DEC_WIDTH), BF16),
        parts,
        kept_in,
        dec_out_weight,
    )
    return (enc_out, dec_out)


def solution(mesh):
    grid = (mesh.shape["clip"], mesh.shape["seq"] // (2 * NEAR_CHIPS), NEAR_CHIPS, 2)
    finer = Mesh(mesh.devices.reshape(grid), CLIP_SEQ)
    return jax.shard_map(
        body,
        mesh=finer,
        in_specs=(
            P(CLIP_SEQ, None),
            P("clip"),
            P("clip"),
            P("clip"),
            P(CLIP_SEQ),
            P(SEQ, None),
            P(),
            P(),
            P(),
            P(),
            P(),
            P(),
        ),
        out_specs=(P(CLIP_SEQ, None), P(CLIP_SEQ, None)),
        check_vma=False,
    )
```

```python
import math

import jax
import jax.numpy as jnp
import numpy as np
from jax import lax
from jax.experimental import pallas as pl
from jax.experimental.pallas import tpu as pltpu
from jax.sharding import Mesh
from jax.sharding import PartitionSpec as P

HEAD_SIZE = 88
ENC_HEADS = 8
ENC_INNER = ENC_HEADS * HEAD_SIZE
DEC_WIDTH = 512
DEC_HEAD_SIZE = 64
DEC_HEADS = 4
DEC_INNER = DEC_HEADS * DEC_HEAD_SIZE
ROW_BLOCK = 64
WEIGHT_ROWS = 24
ENC_CHUNKS = 2
LANES = 128
SEQ = ("far", "chip", "core")
CHIPS = ("far", "chip")
NEAR = ("chip", "core")
CLIP_SEQ = ("clip", "far", "chip", "core")
NEAR_CHIPS = 2
ENC_WINDOW = 768
ENC_SHIFT = ENC_WINDOW - ENC_INNER
HEAD_PAIRS = ENC_HEADS // 2
PAIR_SIZE = 2 * HEAD_SIZE

LOG2_E = math.log2(math.e)
NEG_FILL = -1e30
LN_EPS = 1e-06
F32 = jnp.float32
BF16 = jnp.bfloat16


def shifted(shard, axis, by):
    devices = lax.axis_size(axis)
    pairs = [(i, i + by) for i in range(devices) if 0 <= i + by < devices]
    return lax.ppermute(shard, axis, pairs)


def swapped(shard):
    return lax.ppermute(shard, "core", [(0, 1), (1, 0)])


def layer_norm(rows_in, gain_row):
    widened = rows_in.astype(F32)
    centred = widened - jnp.mean(widened, axis=-1, keepdims=True)
    spread = jnp.mean(centred * centred, axis=-1, keepdims=True)
    return centred * lax.rsqrt(spread + LN_EPS) * gain_row


def frequencies():
    half = np.arange(DEC_WIDTH // 2)
    return jnp.asarray(np.power(10000.0, -half * 2.0 / DEC_WIDTH).astype(np.float32))


def sinusoid(positions):
    angles = positions.astype(F32)[:, None] * frequencies()[None, :]
    return jnp.stack([jnp.sin(angles), jnp.cos(angles)], axis=-1).reshape(
        positions.shape[0], DEC_WIDTH
    )


def split_sinusoid(positions):
    angles = positions[:, None] * frequencies()[None, :]
    return jnp.concatenate([jnp.sin(angles), jnp.cos(angles)], axis=-1)


def halves_first(rows):
    apart = rows.reshape(rows.shape[0] // 2, 2, *rows.shape[1:])
    return jnp.concatenate([apart[:, 0], apart[:, 1]], axis=0)


def balance_table(vis_count, row_block):
    left_count = jnp.concatenate([vis_count[:1] * 0, vis_count[:-1]], axis=0)
    return jnp.where(vis_count > 0, jnp.minimum(vis_count, row_block), left_count - row_block)


def nt_dot(left, right):
    return lax.dot_general(left, right, (((1,), (1,)), ((), ())), preferred_element_type=F32)


def head_column(shape, head, size, offset):
    column = lax.broadcasted_iota(jnp.int32, shape, 1) - offset
    return (column >= head * size) & (column < (head + 1) * size)


def lane_window(start, size):
    first = start // LANES * LANES
    return first, -(-(start + size - first) // LANES) * LANES


def encoder_kernel(packets_hbm, query_ref, mask_ref, own_ref, other_ref, kv_ref, sems):
    chips = packets_hbm.shape[0]
    per_chunk = chips // ENC_CHUNKS
    copies = []
    for chunk in range(ENC_CHUNKS):
        part = pl.ds(chunk * per_chunk, per_chunk)
        copies.append(
            pltpu.make_async_copy(
                packets_hbm.at[part, pl.ds(0, ROW_BLOCK)], kv_ref.at[part], sems.at[chunk]
            )
        )
        copies[-1].start()
    scale = LOG2_E / math.sqrt(HEAD_SIZE)
    value_base = 2 * ENC_INNER - ENC_WINDOW
    asked = query_ref.shape[0]
    queries = []
    for pair in range(HEAD_PAIRS):
        first, width = lane_window(pair * PAIR_SIZE, PAIR_SIZE)
        part = query_ref[:, first : first + width]
        repeats = [
            jnp.where(
                head_column(part.shape, 2 * pair + k, HEAD_SIZE, -first), part, jnp.zeros_like(part)
            )
            for k in range(2)
        ]
        queries.append(jnp.concatenate(repeats, axis=0))
    length = per_chunk * ROW_BLOCK
    peaks = [None] * HEAD_PAIRS
    sums = [0.0] * HEAD_PAIRS
    mixes = [0.0] * HEAD_PAIRS
    for chunk in range(ENC_CHUNKS):
        copies[chunk].wait()
        those = slice(chunk * per_chunk, (chunk + 1) * per_chunk)
        usable = mask_ref[:, chunk * length : (chunk + 1) * length] > 0.0
        for pair in range(HEAD_PAIRS):
            first, width = lane_window(pair * PAIR_SIZE, PAIR_SIZE)
            keys = kv_ref[those, :, first : first + width].reshape(length, width)
            scores = nt_dot(queries[pair], keys)
            scores = jnp.where(usable, scores, NEG_FILL)
            peak = jnp.max(scores, axis=-1, keepdims=True)
            if chunk > 0:
                peak = jnp.maximum(peaks[pair], peak)
                fade = jnp.exp2((peaks[pair] - peak) * scale)
                sums[pair] *= fade
                mixes[pair] *= fade
            peaks[pair] = peak
            weights = jnp.exp2((scores - peak) * scale)
            sums[pair] += jnp.sum(weights, axis=-1, keepdims=True)
            first, width = lane_window(ENC_SHIFT + pair * PAIR_SIZE, PAIR_SIZE)
            first += value_base
            values = kv_ref[those, :, first : first + width].reshape(length, width)
            mixes[pair] += jnp.dot(weights.astype(BF16), values, preferred_element_type=F32)
    half = asked // 2
    for out_ref, base in ((own_ref, 0), (other_ref, half)):
        out_ref[...] = jnp.zeros_like(out_ref)
        stats = jnp.zeros((half, LANES), F32)
        for pair in range(HEAD_PAIRS):
            first, width = lane_window(ENC_SHIFT + pair * PAIR_SIZE, PAIR_SIZE)
            part = out_ref[:, first : first + width]
            for k in range(2):
                head = 2 * pair + k
                rows = slice(k * asked + base, k * asked + base + half)
                mine = head_column(part.shape, head, HEAD_SIZE, ENC_SHIFT - first)
                part = jnp.where(mine, mixes[pair][rows], part)
                stats = head_stats(stats, head, ENC_HEADS, peaks[pair][rows], sums[pair][rows])
            out_ref[:, first : first + width] = part
        out_ref[:, ENC_WINDOW:] = stats


def project_kernel(
    live_ref,
    packets_hbm,
    own_ref,
    far_ref,
    residual_ref,
    spread_hbm,
    norm_gain_ref,
    bridge_hbm,
    pe_ref,
    dec_gain_ref,
    dec_weight_hbm,
    enc_out_hbm,
    vis_ref,
    weight_ref,
    bridge_ref,
    dec_weight_ref,
    spread_ref,
    enc_out_ref,
    sems,
):
    rows_in = packets_hbm.at[pl.ds(0, packets_hbm.shape[0]), pl.ds(ROW_BLOCK, 2 * WEIGHT_ROWS)]
    spread_copy = pltpu.make_async_copy(spread_hbm, spread_ref, sems.at[0])
    weight_copy = pltpu.make_async_copy(rows_in, weight_ref, sems.at[1])
    bridge_copy = pltpu.make_async_copy(bridge_hbm, bridge_ref, sems.at[2])
    dec_copy = pltpu.make_async_copy(dec_weight_hbm, dec_weight_ref, sems.at[3])
    for copy in (spread_copy, weight_copy, bridge_copy, dec_copy):
        copy.start()
    scale = LOG2_E / math.sqrt(HEAD_SIZE)
    own_stats = own_ref[:, ENC_WINDOW:]
    far_stats = far_ref[:, ENC_WINDOW:]
    peak = jnp.maximum(own_stats, far_stats)
    own_fade = jnp.exp2((own_stats - peak) * scale)
    far_fade = jnp.exp2((far_stats - peak) * scale)
    shape = (own_ref.shape[0], ENC_WINDOW)
    own_factor = jnp.zeros(shape, F32)
    far_factor = jnp.zeros(shape, F32)
    for head in range(ENC_HEADS):
        here = slice(head, head + 1)
        there = slice(ENC_HEADS + head, ENC_HEADS + head + 1)
        summed = own_fade[:, here] * own_stats[:, there] + far_fade[:, here] * far_stats[:, there]
        mine = head_column(shape, head, HEAD_SIZE, ENC_SHIFT)
        own_factor = jnp.where(mine, own_fade[:, here] / summed, own_factor)
        far_factor = jnp.where(mine, far_fade[:, here] / summed, far_factor)
    attn = own_ref[:, :ENC_WINDOW] * own_factor + far_ref[:, :ENC_WINDOW] * far_factor
    spread_copy.wait()
    attn = jnp.dot(attn.astype(BF16), spread_ref[...], preferred_element_type=F32).astype(BF16)
    weight_copy.wait()
    weight = weight_ref[...].reshape(-1, weight_ref.shape[-1])
    projected = jnp.dot(attn, weight, preferred_element_type=F32)
    computed = (residual_ref[...].astype(F32) + projected).astype(BF16)
    slot = lax.broadcasted_iota(jnp.int32, computed.shape, 0)
    enc_out_ref[...] = jnp.where(slot < live_ref[0], computed, jnp.zeros_like(computed))
    out_copy = pltpu.make_async_copy(enc_out_ref, enc_out_hbm, sems.at[4])
    out_copy.start()
    normed = layer_norm(computed, norm_gain_ref[...]).astype(BF16)
    bridge_copy.wait()
    bridged = jnp.dot(normed, bridge_ref[...], preferred_element_type=F32) + pe_ref[...]
    dec_normed = layer_norm(bridged.astype(BF16), dec_gain_ref[...]).astype(BF16)
    dec_copy.wait()
    pairs = jnp.dot(dec_normed, dec_weight_ref[...], preferred_element_type=F32)
    vis_ref[...] = pairs.astype(BF16)
    out_copy.wait()


def head_stats(stats, head, heads, peak, summed):
    lane = lax.broadcasted_iota(jnp.int32, stats.shape, 1)
    stats = jnp.where(lane == head, peak, stats)
    return jnp.where(lane == heads + head, summed, stats)


def coded_stats(stats):
    group = 2 * DEC_HEADS
    high = stats.astype(BF16).astype(F32)
    middle = (stats - high).astype(BF16).astype(F32)
    low = stats - high - middle
    return (high + pltpu.roll(middle, group, 1) + pltpu.roll(low, 2 * group, 1)).astype(BF16)


def decoded_stats(coded):
    group = 2 * DEC_HEADS
    widened = coded.astype(F32)
    middle = pltpu.roll(widened, LANES - group, 1)
    low = pltpu.roll(widened, LANES - 2 * group, 1)
    return widened + (middle + low)


def kept_kernel(kept_ref, gain_ref, weight_ref, query_ref, state_ref):
    scale = LOG2_E / math.sqrt(DEC_HEAD_SIZE)
    normed = layer_norm(kept_ref[...], gain_ref[...]).astype(BF16)
    pairs = jnp.dot(normed, weight_ref[...], preferred_element_type=F32).astype(BF16)
    queries = query_ref[...]
    total = jnp.zeros(queries.shape, F32)
    stats = jnp.zeros((queries.shape[0], LANES), F32)
    for h in range(DEC_HEADS):
        mine = head_column(queries.shape, h, DEC_HEAD_SIZE, 0)
        scores = nt_dot(jnp.where(mine, queries, jnp.zeros_like(queries)), pairs[:, :DEC_INNER])
        peak = jnp.max(scores, axis=-1, keepdims=True)
        weights = jnp.exp2((scores - peak) * scale)
        stats = head_stats(stats, h, DEC_HEADS, peak, jnp.sum(weights, axis=-1, keepdims=True))
        mixed = jnp.dot(weights.astype(BF16), pairs[:, DEC_INNER:], preferred_element_type=F32)
        total = jnp.where(mine, mixed, total)
    state_ref[:, :DEC_INNER] = total
    state_ref[:, DEC_INNER:] = stats


def visible_kernel(vis_ref, mask_ref, query_ref, state_ref, out_ref):
    scale = LOG2_E / math.sqrt(DEC_HEAD_SIZE)
    usable = mask_ref[...] > 0.0
    queries = query_ref[...]
    total = jnp.zeros(queries.shape, F32)
    stats = jnp.zeros((queries.shape[0], LANES), F32)
    for h in range(DEC_HEADS):
        place = DEC_INNER + h
        kept_peak = state_ref[:, place : place + 1]
        kept_sum = state_ref[:, place + DEC_HEADS : place + DEC_HEADS + 1]
        mine = head_column(queries.shape, h, DEC_HEAD_SIZE, 0)
        scores = nt_dot(jnp.where(mine, queries, jnp.zeros_like(queries)), vis_ref[:, :DEC_INNER])
        scores = jnp.where(usable, scores, NEG_FILL)
        peak = jnp.maximum(kept_peak, jnp.max(scores, axis=-1, keepdims=True))
        weights = jnp.exp2((scores - peak) * scale)
        fade = jnp.exp2((kept_peak - peak) * scale)
        summed = kept_sum * fade + jnp.sum(weights, axis=-1, keepdims=True)
        stats = head_stats(stats, h, DEC_HEADS, peak, summed)
        mixed = jnp.dot(weights.astype(BF16), vis_ref[:, DEC_INNER:], preferred_element_type=F32)
        total = jnp.where(mine, mixed + fade * state_ref[:, :DEC_INNER], total)
    near, rows = out_ref.shape[:2]
    for k in range(near):
        out_ref[k, :, :DEC_INNER] = total[k * rows : (k + 1) * rows].astype(BF16)
        out_ref[k, :, DEC_INNER:] = coded_stats(stats[k * rows : (k + 1) * rows])


def finish_kernel(parts_ref, kept_ref, weight_ref, out_ref):
    scale = LOG2_E / math.sqrt(DEC_HEAD_SIZE)
    near, rows = parts_ref.shape[:2]
    shape = (rows, DEC_INNER)
    stats = [decoded_stats(parts_ref[k, :, DEC_INNER:]) for k in range(near)]
    mixes = [parts_ref[k, :, :DEC_INNER].astype(F32) for k in range(near)]
    peak = stats[0]
    for k in range(1, near):
        peak = jnp.maximum(peak, stats[k])
    fades = [jnp.exp2((stats[k] - peak) * scale) for k in range(near)]
    total = jnp.zeros(shape, F32)
    summed = jnp.ones(shape, F32)
    for h in range(DEC_HEADS):
        place = DEC_HEADS + h
        mixed = 0.0
        weight = 0.0
        for k in range(near):
            fade = fades[k][:, h : h + 1]
            mixed += fade * mixes[k]
            weight += fade * stats[k][:, place : place + 1]
        mine = head_column(shape, h, DEC_HEAD_SIZE, 0)
        total = jnp.where(mine, mixed, total)
        summed = jnp.where(mine, weight, summed)
    attn = (total / summed).astype(BF16)
    projected = jnp.dot(attn, weight_ref[...], preferred_element_type=F32)
    out_ref[...] = (kept_ref[...].astype(F32) + projected).astype(BF16)


def call(kernel, out_shape, *operands, scalars=0, in_hbm=(), out_hbm=(), scratch=()):
    in_vmem = pl.BlockSpec(memory_space=pltpu.VMEM)
    specs = [in_vmem] * len(operands)
    for k in range(scalars):
        specs[k] = pl.BlockSpec(memory_space=pltpu.SMEM)
    for k in in_hbm:
        specs[k] = pl.BlockSpec(memory_space=pl.ANY)
    out_specs = jax.tree.map(lambda _: in_vmem, out_shape)
    for k in out_hbm:
        out_specs = out_specs[:k] + (pl.BlockSpec(memory_space=pl.ANY),) + out_specs[k + 1 :]
    return pl.pallas_call(
        kernel,
        out_shape=out_shape,
        in_specs=specs,
        out_specs=out_specs,
        scratch_shapes=list(scratch),
        compiler_params=pltpu.CompilerParams(vmem_limit_bytes=56 * 1024 * 1024),
    )(*operands)


def body(
    enc_rows,
    vis_count,
    vis_dest,
    vis_pos,
    kept_pos,
    out_weight,
    norm_gain,
    bridge_weight,
    mask_token,
    dec_gain,
    dec_qkv_weight,
    dec_out_weight,
):
    row_block = ROW_BLOCK
    shape_of = jax.ShapeDtypeStruct
    myself = lax.axis_index(SEQ)
    near = lax.axis_size(NEAR)
    far = lax.axis_size("far")
    bal_counts = balance_table(vis_count, row_block)
    has_own = vis_count[myself] > 0

    pair_rows = enc_rows[:, ENC_INNER : 3 * ENC_INNER]
    key_value = jnp.where(has_own, pair_rows[:row_block], shifted(pair_rows[row_block:], SEQ, 1))
    seq_devices = lax.axis_size(SEQ)
    chips = lax.axis_size(CHIPS)
    core = lax.axis_index("core")
    weight_rows = out_weight.shape[0]
    own_weight = jnp.pad(out_weight, ((0, WEIGHT_ROWS - weight_rows), (0, 0)))
    far_weight = swapped(own_weight)
    packet = jnp.concatenate(
        [
            key_value,
            jnp.where(core == 0, own_weight, far_weight),
            jnp.where(core == 0, far_weight, own_weight),
        ],
        axis=0,
    )
    packets = lax.all_gather(packet, CHIPS, axis=0, tiled=True).reshape(chips, *packet.shape)
    enc_late, kept_pos, _ = lax.optimization_barrier((enc_rows, kept_pos, key_value))

    kept_dev = kept_pos.shape[0]
    kept_all = lax.all_to_all(
        jnp.broadcast_to(kept_pos[None, :], (far, kept_dev)), "far", 0, 0, tiled=True
    )
    kept_all = kept_all.reshape(-1).astype(F32)

    rest = jnp.concatenate([enc_late[:, :ENC_INNER], enc_late[:, 3 * ENC_INNER :]], axis=1)
    rest = jnp.where(has_own, rest[:row_block], shifted(rest[row_block:], SEQ, 1))
    queries = jnp.pad(rest[:, :ENC_INNER], ((0, 0), (0, ENC_SHIFT)))
    queries = jnp.concatenate([queries, swapped(queries)], axis=0)
    residual = rest[:, ENC_INNER:]

    kept_in = (mask_token.astype(F32)[None, :] + sinusoid(kept_pos)).astype(BF16)
    own_normed = layer_norm(kept_in, dec_gain[None, :]).astype(BF16)
    asking = jnp.dot(
        own_normed, dec_qkv_weight[:, :DEC_INNER], preferred_element_type=F32
    ).astype(BF16)
    asking = lax.all_gather(asking, NEAR, axis=0, tiled=True)
    mask_split = halves_first(mask_token)
    kept_split = (mask_split.astype(F32)[None, :] + split_sinusoid(kept_all)).astype(BF16)
    asked = asking.shape[0]
    kept_state = call(
        kept_kernel,
        shape_of((asked, DEC_INNER + LANES), F32),
        kept_split,
        halves_first(dec_gain)[None, :],
        halves_first(dec_qkv_weight[:, DEC_INNER:]),
        asking,
    )

    packets, kept_state = lax.optimization_barrier((packets, kept_state))

    first_row = jnp.where(has_own, myself * 2 * row_block, (myself - 1) * 2 * row_block + row_block)
    bal_pos = lax.dynamic_slice_in_dim(vis_pos, first_row, row_block)
    within = jnp.arange(row_block, dtype=jnp.int32)
    live = (within[None, :] < bal_counts[:, None]).astype(F32)
    source = jnp.arange(ENC_WINDOW, dtype=jnp.int32)[:, None] - ENC_SHIFT
    place = jnp.arange(seq_devices * WEIGHT_ROWS, dtype=jnp.int32)[None, :]
    block = place // WEIGHT_ROWS
    inside = place - block * WEIGHT_ROWS
    spread = ((source == block * weight_rows + inside) & (inside < weight_rows)).astype(BF16)
    pair_width = 2 * DEC_INNER
    model_width = residual.shape[1]
    live_core = lax.dynamic_index_in_dim(
        live.reshape(chips, -1, row_block), core, axis=1, keepdims=False
    )
    state = shape_of((row_block, ENC_WINDOW + LANES), F32)
    own_state, other_state = call(
        encoder_kernel,
        (state, state),
        packets,
        queries,
        live_core.reshape(1, -1),
        in_hbm=(0,),
        scratch=(
            pltpu.VMEM((chips, row_block, 2 * ENC_INNER), BF16),
            pltpu.SemaphoreType.DMA((ENC_CHUNKS,)),
        ),
    )
    enc_out, vis_kv = call(
        project_kernel,
        (
            shape_of((row_block, model_width), BF16),
            shape_of((row_block, pair_width), BF16),
        ),
        bal_counts[myself][None],
        packets,
        own_state,
        swapped(other_state),
        residual,
        spread,
        norm_gain[None, :],
        bridge_weight,
        sinusoid(bal_pos),
        dec_gain[None, :],
        dec_qkv_weight[:, DEC_INNER:],
        scalars=1,
        in_hbm=(1, 5, 7, 10),
        out_hbm=(0,),
        scratch=(
            pltpu.VMEM((chips, 2 * WEIGHT_ROWS, model_width), BF16),
            pltpu.VMEM(bridge_weight.shape, BF16),
            pltpu.VMEM((DEC_WIDTH, pair_width), BF16),
            pltpu.VMEM(spread.shape, BF16),
            pltpu.VMEM((row_block, model_width), BF16),
            pltpu.SemaphoreType.DMA((5,)),
        ),
    )

    vis_all = lax.all_gather(vis_kv, "far", axis=0, tiled=True)
    live_same = lax.dynamic_index_in_dim(
        live.reshape(far, near, row_block), lax.axis_index(NEAR), axis=1, keepdims=False
    )
    parts = call(
        visible_kernel,
        shape_of((near, kept_dev, DEC_INNER + LANES), BF16),
        vis_all,
        live_same.reshape(1, -1),
        asking,
        kept_state,
    )
    parts = lax.all_to_all(parts, NEAR, 0, 0, tiled=True)
    dec_out = call(
        finish_kernel,
        shape_of((kept_dev, DEC_WIDTH), BF16),
        parts,
        kept_in,
        dec_out_weight,
    )
    return (enc_out, dec_out)


def solution(mesh):
    grid = (mesh.shape["clip"], mesh.shape["seq"] // (2 * NEAR_CHIPS), NEAR_CHIPS, 2)
    finer = Mesh(mesh.devices.reshape(grid), CLIP_SEQ)
    return jax.shard_map(
        body,
        mesh=finer,
        in_specs=(
            P(CLIP_SEQ, None),
            P("clip"),
            P("clip"),
            P("clip"),
            P(CLIP_SEQ),
            P(SEQ, None),
            P(),
            P(),
            P(),
            P(),
            P(),
            P(),
        ),
        out_specs=(P(CLIP_SEQ, None), P(CLIP_SEQ, None)),
        check_vma=False,
    )
```

```python
import math

import jax
import jax.numpy as jnp
import numpy as np
from jax import lax
from jax.experimental import pallas as pl
from jax.experimental.pallas import tpu as pltpu
from jax.sharding import Mesh
from jax.sharding import PartitionSpec as P

HEAD_SIZE = 88
ENC_HEADS = 8
ENC_INNER = ENC_HEADS * HEAD_SIZE
DEC_WIDTH = 512
DEC_HEAD_SIZE = 64
DEC_HEADS = 4
DEC_INNER = DEC_HEADS * DEC_HEAD_SIZE
ROW_BLOCK = 64
WEIGHT_ROWS = 24
STAT_ROWS = 24
ENC_CHUNKS = 2
LANES = 128
SEQ = ("far", "chip", "core")
NEAR = ("chip", "core")
CLIP_SEQ = ("clip", "far", "chip", "core")
NEAR_CHIPS = 4
ENC_WINDOW = 768
ENC_SHIFT = ENC_WINDOW - ENC_INNER
HEAD_PAIRS = ENC_HEADS // 2
PAIR_SIZE = 2 * HEAD_SIZE

LOG2_E = math.log2(math.e)
NEG_FILL = -1e30
LN_EPS = 1e-06
F32 = jnp.float32
BF16 = jnp.bfloat16


def shifted(shard, axis, by):
    devices = lax.axis_size(axis)
    pairs = [(i, i + by) for i in range(devices) if 0 <= i + by < devices]
    return lax.ppermute(shard, axis, pairs)


def layer_norm(rows_in, gain_row):
    widened = rows_in.astype(F32)
    centred = widened - jnp.mean(widened, axis=-1, keepdims=True)
    spread = jnp.mean(centred * centred, axis=-1, keepdims=True)
    return centred * lax.rsqrt(spread + LN_EPS) * gain_row


def frequencies():
    half = np.arange(DEC_WIDTH // 2)
    return jnp.asarray(np.power(10000.0, -half * 2.0 / DEC_WIDTH).astype(np.float32))


def sinusoid(positions):
    angles = positions.astype(F32)[:, None] * frequencies()[None, :]
    return jnp.stack([jnp.sin(angles), jnp.cos(angles)], axis=-1).reshape(
        positions.shape[0], DEC_WIDTH
    )


def split_sinusoid(positions):
    angles = positions[:, None] * frequencies()[None, :]
    return jnp.concatenate([jnp.sin(angles), jnp.cos(angles)], axis=-1)


def halves_first(rows):
    apart = rows.reshape(rows.shape[0] // 2, 2, *rows.shape[1:])
    return jnp.concatenate([apart[:, 0], apart[:, 1]], axis=0)


def balance_table(vis_count, row_block):
    left_count = jnp.concatenate([vis_count[:1] * 0, vis_count[:-1]], axis=0)
    return jnp.where(vis_count > 0, jnp.minimum(vis_count, row_block), left_count - row_block)


def nt_dot(left, right):
    return lax.dot_general(left, right, (((1,), (1,)), ((), ())), preferred_element_type=F32)


def head_column(shape, head, size, offset):
    column = lax.broadcasted_iota(jnp.int32, shape, 1) - offset
    return (column >= head * size) & (column < (head + 1) * size)


def lane_window(start, size):
    first = start // LANES * LANES
    return first, -(-(start + size - first) // LANES) * LANES


def encoder_kernel(
    live_ref,
    packets_hbm,
    query_ref,
    mask_ref,
    residual_ref,
    spread_hbm,
    norm_gain_ref,
    bridge_hbm,
    pe_ref,
    dec_gain_ref,
    dec_weight_hbm,
    enc_out_hbm,
    vis_ref,
    kv_ref,
    weight_ref,
    bridge_ref,
    dec_weight_ref,
    spread_ref,
    attn_ref,
    enc_out_ref,
    kv_sems,
    other_sems,
):
    devices = packets_hbm.shape[0]
    per_chunk = devices // ENC_CHUNKS
    kv_copies = []
    for chunk in range(ENC_CHUNKS):
        part = pl.ds(chunk * per_chunk, per_chunk)
        kv_copies.append(
            pltpu.make_async_copy(
                packets_hbm.at[part, pl.ds(0, ROW_BLOCK)], kv_ref.at[part], kv_sems.at[chunk]
            )
        )
    weight_copy = pltpu.make_async_copy(
        packets_hbm.at[pl.ds(0, devices), pl.ds(ROW_BLOCK, WEIGHT_ROWS)], weight_ref, other_sems.at[4]
    )
    spread_copy = pltpu.make_async_copy(spread_hbm, spread_ref, other_sems.at[2])
    bridge_copy = pltpu.make_async_copy(bridge_hbm, bridge_ref, other_sems.at[0])
    dec_copy = pltpu.make_async_copy(dec_weight_hbm, dec_weight_ref, other_sems.at[1])
    for copy in kv_copies + [spread_copy, weight_copy, bridge_copy, dec_copy]:
        copy.start()
    scale = LOG2_E / math.sqrt(HEAD_SIZE)
    value_base = 2 * ENC_INNER - ENC_WINDOW
    queries = []
    for pair in range(HEAD_PAIRS):
        first, width = lane_window(pair * PAIR_SIZE, PAIR_SIZE)
        part = query_ref[:, first : first + width]
        copies = [
            jnp.where(
                head_column(part.shape, 2 * pair + k, HEAD_SIZE, -first), part, jnp.zeros_like(part)
            )
            for k in range(2)
        ]
        queries.append(jnp.concatenate(copies, axis=0))
    length = per_chunk * ROW_BLOCK
    peaks = [None] * HEAD_PAIRS
    sums = [0.0] * HEAD_PAIRS
    mixes = [0.0] * HEAD_PAIRS
    for chunk in range(ENC_CHUNKS):
        kv_copies[chunk].wait()
        those = slice(chunk * per_chunk, (chunk + 1) * per_chunk)
        usable = mask_ref[:, chunk * length : (chunk + 1) * length] > 0.0
        for pair in range(HEAD_PAIRS):
            first, width = lane_window(pair * PAIR_SIZE, PAIR_SIZE)
            keys = kv_ref[those, :, first : first + width].reshape(length, width)
            scores = nt_dot(queries[pair], keys)
            scores = jnp.where(usable, scores, NEG_FILL)
            peak = jnp.max(scores, axis=-1, keepdims=True)
            if chunk > 0:
                peak = jnp.maximum(peaks[pair], peak)
                fade = jnp.exp2((peaks[pair] - peak) * scale)
                sums[pair] *= fade
                mixes[pair] *= fade
            peaks[pair] = peak
            weights = jnp.exp2((scores - peak) * scale)
            sums[pair] += jnp.sum(weights, axis=-1, keepdims=True)
            first, width = lane_window(ENC_SHIFT + pair * PAIR_SIZE, PAIR_SIZE)
            first += value_base
            values = kv_ref[those, :, first : first + width].reshape(length, width)
            mixes[pair] += jnp.dot(weights.astype(BF16), values, preferred_element_type=F32)
    attn_ref[...] = jnp.zeros_like(attn_ref)
    for pair in range(HEAD_PAIRS):
        first, width = lane_window(ENC_SHIFT + pair * PAIR_SIZE, PAIR_SIZE)
        mixed = mixes[pair] / sums[pair]
        part = attn_ref[:, first : first + width]
        for k in range(2):
            mine = head_column(part.shape, 2 * pair + k, HEAD_SIZE, ENC_SHIFT - first)
            part = jnp.where(mine, mixed[k * ROW_BLOCK : (k + 1) * ROW_BLOCK], part)
        attn_ref[:, first : first + width] = part
    attn = attn_ref[...].astype(BF16)
    spread_copy.wait()
    attn = jnp.dot(attn, spread_ref[...], preferred_element_type=F32).astype(BF16)
    weight_copy.wait()
    weight = weight_ref[...].reshape(-1, weight_ref.shape[-1])
    projected = jnp.dot(attn, weight, preferred_element_type=F32)
    computed = (residual_ref[...].astype(F32) + projected).astype(BF16)
    slot = lax.broadcasted_iota(jnp.int32, computed.shape, 0)
    enc_out_ref[...] = jnp.where(slot < live_ref[0], computed, jnp.zeros_like(computed))
    out_copy = pltpu.make_async_copy(enc_out_ref, enc_out_hbm, other_sems.at[3])
    out_copy.start()
    normed = layer_norm(computed, norm_gain_ref[...]).astype(BF16)
    bridge_copy.wait()
    bridged = jnp.dot(normed, bridge_ref[...], preferred_element_type=F32) + pe_ref[...]
    dec_normed = layer_norm(bridged.astype(BF16), dec_gain_ref[...]).astype(BF16)
    dec_copy.wait()
    pairs = jnp.dot(dec_normed, dec_weight_ref[...], preferred_element_type=F32)
    vis_ref[...] = pairs.astype(BF16)
    out_copy.wait()


def head_stats(stats, head, peak, summed):
    lane = lax.broadcasted_iota(jnp.int32, stats.shape, 1)
    stats = jnp.where(lane == head, peak, stats)
    return jnp.where(lane == DEC_HEADS + head, summed, stats)


def unit_rows(count, width):
    row = lax.broadcasted_iota(jnp.int32, (count, width), 0)
    column = lax.broadcasted_iota(jnp.int32, (count, width), 1)
    return jnp.where(row == column, 1.0, 0.0).astype(BF16)


def three_parts(numbers):
    high = numbers.astype(BF16).astype(F32)
    middle = (numbers - high).astype(BF16).astype(F32)
    return high, middle, numbers - high - middle


def coded_stats(stats):
    group = 2 * DEC_HEADS
    high, middle, low = three_parts(stats)
    lanes = high + pltpu.roll(middle, group, 1) + pltpu.roll(low, 2 * group, 1)
    return nt_dot(unit_rows(STAT_ROWS, LANES), lanes.astype(BF16)).astype(BF16)


def decoded_stats(coded):
    group = 2 * DEC_HEADS
    widened = coded.astype(F32)
    return widened[:group] + (widened[group : 2 * group] + widened[2 * group :])


def kept_kernel(kept_ref, gain_ref, weight_ref, query_ref, state_ref):
    scale = LOG2_E / math.sqrt(DEC_HEAD_SIZE)
    normed = layer_norm(kept_ref[...], gain_ref[...]).astype(BF16)
    pairs = jnp.dot(normed, weight_ref[...], preferred_element_type=F32).astype(BF16)
    queries = query_ref[...]
    total = jnp.zeros(queries.shape, F32)
    stats = jnp.zeros((queries.shape[0], LANES), F32)
    for h in range(DEC_HEADS):
        mine = head_column(queries.shape, h, DEC_HEAD_SIZE, 0)
        scores = nt_dot(jnp.where(mine, queries, jnp.zeros_like(queries)), pairs[:, :DEC_INNER])
        peak = jnp.max(scores, axis=-1, keepdims=True)
        weights = jnp.exp2((scores - peak) * scale)
        stats = head_stats(stats, h, peak, jnp.sum(weights, axis=-1, keepdims=True))
        mixed = jnp.dot(weights.astype(BF16), pairs[:, DEC_INNER:], preferred_element_type=F32)
        total = jnp.where(mine, mixed, total)
    state_ref[:, :DEC_INNER] = total
    state_ref[:, DEC_INNER:] = stats


def visible_kernel(vis_ref, mask_ref, query_ref, state_ref, out_ref):
    scale = LOG2_E / math.sqrt(DEC_HEAD_SIZE)
    usable = mask_ref[...] > 0.0
    queries = query_ref[...]
    total = jnp.zeros(queries.shape, F32)
    stats = jnp.zeros((queries.shape[0], LANES), F32)
    for h in range(DEC_HEADS):
        place = DEC_INNER + h
        kept_peak = state_ref[:, place : place + 1]
        kept_sum = state_ref[:, place + DEC_HEADS : place + DEC_HEADS + 1]
        mine = head_column(queries.shape, h, DEC_HEAD_SIZE, 0)
        scores = nt_dot(jnp.where(mine, queries, jnp.zeros_like(queries)), vis_ref[:, :DEC_INNER])
        scores = jnp.where(usable, scores, NEG_FILL)
        peak = jnp.maximum(kept_peak, jnp.max(scores, axis=-1, keepdims=True))
        weights = jnp.exp2((scores - peak) * scale)
        fade = jnp.exp2((kept_peak - peak) * scale)
        summed = kept_sum * fade + jnp.sum(weights, axis=-1, keepdims=True)
        stats = head_stats(stats, h, peak, summed)
        mixed = jnp.dot(weights.astype(BF16), vis_ref[:, DEC_INNER:], preferred_element_type=F32)
        total = jnp.where(mine, mixed + fade * state_ref[:, :DEC_INNER], total)
    near = out_ref.shape[0]
    rows = out_ref.shape[1] - STAT_ROWS
    for k in range(near):
        those = slice(k * rows, (k + 1) * rows)
        out_ref[k, :rows] = total[those].astype(BF16)
        out_ref[k, rows:] = jnp.zeros((STAT_ROWS, DEC_INNER), BF16)
        out_ref[k, rows:, :rows] = coded_stats(stats[those])


def finish_kernel(parts_ref, kept_ref, weight_ref, out_ref):
    scale = LOG2_E / math.sqrt(DEC_HEAD_SIZE)
    near = parts_ref.shape[0]
    rows = parts_ref.shape[1] - STAT_ROWS
    stats = [decoded_stats(parts_ref[k, rows:, :rows]) for k in range(near)]
    peak = stats[0]
    for k in range(1, near):
        peak = jnp.maximum(peak, stats[k])
    fades = [jnp.exp2((stats[k] - peak) * scale) for k in range(near)]
    summed = 0.0
    for k in range(near):
        summed += pltpu.roll(fades[k], DEC_HEADS, 0) * stats[k]
    summed = pltpu.roll(summed, DEC_HEADS, 0)
    group = 2 * DEC_HEADS
    row = lax.broadcasted_iota(jnp.int32, (STAT_ROWS, DEC_INNER), 0)
    column = lax.broadcasted_iota(jnp.int32, (STAT_ROWS, DEC_INNER), 1)
    within = row - row // group * group
    over_heads = jnp.where(within == column // DEC_HEAD_SIZE, 1.0, 0.0).astype(BF16)
    turn = unit_rows(rows, rows)
    is_head = lax.broadcasted_iota(jnp.int32, summed.shape, 0) < DEC_HEADS
    total = jnp.zeros((rows, DEC_INNER), F32)
    for k in range(near):
        factor = jnp.where(is_head, fades[k] / summed, 0.0)
        factor = jnp.concatenate(three_parts(factor), axis=0).astype(BF16)
        factor = nt_dot(turn, factor).astype(BF16)
        factor = jnp.dot(factor, over_heads, preferred_element_type=F32)
        total += parts_ref[k, :rows].astype(F32) * factor
    attn = total.astype(BF16)
    projected = jnp.dot(attn, weight_ref[...], preferred_element_type=F32)
    out_ref[...] = (kept_ref[...].astype(F32) + projected).astype(BF16)


def call(kernel, out_shape, *operands, scalars=0, in_hbm=(), out_hbm=(), scratch=()):
    in_vmem = pl.BlockSpec(memory_space=pltpu.VMEM)
    specs = [in_vmem] * len(operands)
    for k in range(scalars):
        specs[k] = pl.BlockSpec(memory_space=pltpu.SMEM)
    for k in in_hbm:
        specs[k] = pl.BlockSpec(memory_space=pl.ANY)
    out_specs = jax.tree.map(lambda _: in_vmem, out_shape)
    for k in out_hbm:
        out_specs = out_specs[:k] + (pl.BlockSpec(memory_space=pl.ANY),) + out_specs[k + 1 :]
    return pl.pallas_call(
        kernel,
        out_shape=out_shape,
        in_specs=specs,
        out_specs=out_specs,
        scratch_shapes=list(scratch),
        compiler_params=pltpu.CompilerParams(vmem_limit_bytes=56 * 1024 * 1024),
    )(*operands)


def body(
    enc_rows,
    vis_count,
    vis_dest,
    vis_pos,
    kept_pos,
    out_weight,
    norm_gain,
    bridge_weight,
    mask_token,
    dec_gain,
    dec_qkv_weight,
    dec_out_weight,
):
    row_block = ROW_BLOCK
    shape_of = jax.ShapeDtypeStruct
    myself = lax.axis_index(SEQ)
    near = lax.axis_size(NEAR)
    far = lax.axis_size("far")
    bal_counts = balance_table(vis_count, row_block)
    has_own = vis_count[myself] > 0

    pair_rows = enc_rows[:, ENC_INNER : 3 * ENC_INNER]
    key_value = jnp.where(has_own, pair_rows[:row_block], shifted(pair_rows[row_block:], SEQ, 1))
    seq_devices = lax.axis_size(SEQ)
    weight_rows = out_weight.shape[0]
    padded_weight = jnp.pad(out_weight, ((0, WEIGHT_ROWS - weight_rows), (0, 0)))
    packet = jnp.concatenate([key_value, padded_weight], axis=0)
    packets = lax.all_gather(packet, SEQ, axis=0, tiled=True).reshape(seq_devices, -1, packet.shape[1])
    enc_late, kept_pos, _ = lax.optimization_barrier((enc_rows, kept_pos, key_value))

    kept_dev = kept_pos.shape[0]
    kept_all = lax.all_to_all(
        jnp.broadcast_to(kept_pos[None, :], (far, kept_dev)), "far", 0, 0, tiled=True
    )
    kept_all = kept_all.reshape(-1).astype(F32)

    rest = jnp.concatenate([enc_late[:, :ENC_INNER], enc_late[:, 3 * ENC_INNER :]], axis=1)
    rest = jnp.where(has_own, rest[:row_block], shifted(rest[row_block:], SEQ, 1))
    queries = jnp.pad(rest[:, :ENC_INNER], ((0, 0), (0, ENC_SHIFT)))
    residual = rest[:, ENC_INNER:]

    kept_in = (mask_token.astype(F32)[None, :] + sinusoid(kept_pos)).astype(BF16)
    own_normed = layer_norm(kept_in, dec_gain[None, :]).astype(BF16)
    asking = jnp.dot(
        own_normed, dec_qkv_weight[:, :DEC_INNER], preferred_element_type=F32
    ).astype(BF16)
    asking = lax.all_gather(asking, NEAR, axis=0, tiled=True)
    mask_split = halves_first(mask_token)
    kept_split = (mask_split.astype(F32)[None, :] + split_sinusoid(kept_all)).astype(BF16)
    asked = asking.shape[0]
    kept_state = call(
        kept_kernel,
        shape_of((asked, DEC_INNER + LANES), F32),
        kept_split,
        halves_first(dec_gain)[None, :],
        halves_first(dec_qkv_weight[:, DEC_INNER:]),
        asking,
    )

    packets, kept_state = lax.optimization_barrier((packets, kept_state))

    first_row = jnp.where(has_own, myself * 2 * row_block, (myself - 1) * 2 * row_block + row_block)
    bal_pos = lax.dynamic_slice_in_dim(vis_pos, first_row, row_block)
    within = jnp.arange(row_block, dtype=jnp.int32)
    live = (within[None, :] < bal_counts[:, None]).astype(F32)
    source = jnp.arange(ENC_WINDOW, dtype=jnp.int32)[:, None] - ENC_SHIFT
    place = jnp.arange(seq_devices * WEIGHT_ROWS, dtype=jnp.int32)[None, :]
    block = place // WEIGHT_ROWS
    inside = place - block * WEIGHT_ROWS
    spread = ((source == block * weight_rows + inside) & (inside < weight_rows)).astype(BF16)
    pair_width = 2 * DEC_INNER
    model_width = residual.shape[1]
    enc_out, vis_kv = call(
        encoder_kernel,
        (
            shape_of((row_block, model_width), BF16),
            shape_of((row_block, pair_width), BF16),
        ),
        bal_counts[myself][None],
        packets,
        queries,
        live.reshape(1, -1),
        residual,
        spread,
        norm_gain[None, :],
        bridge_weight,
        sinusoid(bal_pos),
        dec_gain[None, :],
        dec_qkv_weight[:, DEC_INNER:],
        scalars=1,
        in_hbm=(1, 5, 7, 10),
        out_hbm=(0,),
        scratch=(
            pltpu.VMEM((seq_devices, row_block, 2 * ENC_INNER), BF16),
            pltpu.VMEM((seq_devices, WEIGHT_ROWS, model_width), BF16),
            pltpu.VMEM(bridge_weight.shape, BF16),
            pltpu.VMEM((DEC_WIDTH, pair_width), BF16),
            pltpu.VMEM(spread.shape, BF16),
            pltpu.VMEM((row_block, ENC_WINDOW), F32),
            pltpu.VMEM((row_block, model_width), BF16),
            pltpu.SemaphoreType.DMA((ENC_CHUNKS,)),
            pltpu.SemaphoreType.DMA((5,)),
        ),
    )

    vis_all = lax.all_gather(vis_kv, "far", axis=0, tiled=True)
    live_same = lax.dynamic_index_in_dim(
        live.reshape(far, near, row_block), lax.axis_index(NEAR), axis=1, keepdims=False
    )
    parts = call(
        visible_kernel,
        shape_of((near, kept_dev + STAT_ROWS, DEC_INNER), BF16),
        vis_all,
        live_same.reshape(1, -1),
        asking,
        kept_state,
    )
    parts = lax.all_to_all(parts, NEAR, 0, 0, tiled=True)
    dec_out = call(
        finish_kernel,
        shape_of((kept_dev, DEC_WIDTH), BF16),
        parts,
        kept_in,
        dec_out_weight,
    )
    return (enc_out, dec_out)


def solution(mesh):
    grid = (mesh.shape["clip"], mesh.shape["seq"] // (2 * NEAR_CHIPS), NEAR_CHIPS, 2)
    finer = Mesh(mesh.devices.reshape(grid), CLIP_SEQ)
    return jax.shard_map(
        body,
        mesh=finer,
        in_specs=(
            P(CLIP_SEQ, None),
            P("clip"),
            P("clip"),
            P("clip"),
            P(CLIP_SEQ),
            P(SEQ, None),
            P(),
            P(),
            P(),
            P(),
            P(),
            P(),
        ),
        out_specs=(P(CLIP_SEQ, None), P(CLIP_SEQ, None)),
        check_vma=False,
    )
```

```python
import math

import jax
import jax.numpy as jnp
import numpy as np
from jax import lax
from jax.experimental import pallas as pl
from jax.experimental.pallas import tpu as pltpu
from jax.sharding import Mesh
from jax.sharding import PartitionSpec as P

HEAD_SIZE = 88
ENC_HEADS = 8
ENC_INNER = ENC_HEADS * HEAD_SIZE
DEC_WIDTH = 512
DEC_HEAD_SIZE = 64
DEC_HEADS = 4
DEC_INNER = DEC_HEADS * DEC_HEAD_SIZE
ROW_BLOCK = 64
WEIGHT_ROWS = 24
STAT_ROWS = 24
ENC_CHUNKS = 2
ENC_COPIES = 8
WEIGHT_COPIES = 4
LANES = 128
SEQ = ("far", "chip", "core")
NEAR = ("chip", "core")
CLIP_SEQ = ("clip", "far", "chip", "core")
NEAR_CHIPS = 2
ENC_WINDOW = 768
ENC_SHIFT = ENC_WINDOW - ENC_INNER
HEAD_PAIRS = ENC_HEADS // 2
PAIR_SIZE = 2 * HEAD_SIZE

LOG2_E = math.log2(math.e)
NEG_FILL = -1e30
LN_EPS = 1e-06
F32 = jnp.float32
BF16 = jnp.bfloat16


def shifted(shard, axis, by):
    devices = lax.axis_size(axis)
    pairs = [(i, i + by) for i in range(devices) if 0 <= i + by < devices]
    return lax.ppermute(shard, axis, pairs)


def layer_norm(rows_in, gain_row):
    widened = rows_in.astype(F32)
    centred = widened - jnp.mean(widened, axis=-1, keepdims=True)
    spread = jnp.mean(centred * centred, axis=-1, keepdims=True)
    return centred * lax.rsqrt(spread + LN_EPS) * gain_row


def frequencies():
    half = np.arange(DEC_WIDTH // 2)
    return jnp.asarray(np.power(10000.0, -half * 2.0 / DEC_WIDTH).astype(np.float32))


def sinusoid(positions):
    angles = positions.astype(F32)[:, None] * frequencies()[None, :]
    return jnp.stack([jnp.sin(angles), jnp.cos(angles)], axis=-1).reshape(
        positions.shape[0], DEC_WIDTH
    )


def split_sinusoid(positions):
    angles = positions[:, None] * frequencies()[None, :]
    return jnp.concatenate([jnp.sin(angles), jnp.cos(angles)], axis=-1)


def halves_first(rows):
    apart = rows.reshape(rows.shape[0] // 2, 2, *rows.shape[1:])
    return jnp.concatenate([apart[:, 0], apart[:, 1]], axis=0)


def balance_table(vis_count, row_block):
    left_count = jnp.concatenate([vis_count[:1] * 0, vis_count[:-1]], axis=0)
    return jnp.where(vis_count > 0, jnp.minimum(vis_count, row_block), left_count - row_block)


def nt_dot(left, right):
    return lax.dot_general(left, right, (((1,), (1,)), ((), ())), preferred_element_type=F32)


def head_column(shape, head, size, offset):
    column = lax.broadcasted_iota(jnp.int32, shape, 1) - offset
    return (column >= head * size) & (column < (head + 1) * size)


def lane_window(start, size):
    first = start // LANES * LANES
    return first, -(-(start + size - first) // LANES) * LANES


def encoder_kernel(
    live_ref,
    packets_hbm,
    query_ref,
    mask_ref,
    residual_ref,
    norm_gain_ref,
    bridge_hbm,
    pe_ref,
    dec_gain_ref,
    dec_weight_hbm,
    enc_out_hbm,
    vis_ref,
    kv_ref,
    weight_ref,
    bridge_ref,
    dec_weight_ref,
    spread_ref,
    attn_ref,
    enc_out_ref,
    kv_sems,
    weight_sems,
    other_sems,
):
    devices = packets_hbm.shape[0]
    per_chunk = devices // ENC_CHUNKS
    kv_copies = []
    for k in range(ENC_COPIES):
        part = pl.ds(k * (devices // ENC_COPIES), devices // ENC_COPIES)
        kv_copies.append(
            pltpu.make_async_copy(
                packets_hbm.at[part, pl.ds(0, ROW_BLOCK)], kv_ref.at[part], kv_sems.at[k]
            )
        )
    weight_copies = []
    for k in range(WEIGHT_COPIES):
        part = pl.ds(k * (devices // WEIGHT_COPIES), devices // WEIGHT_COPIES)
        weight_copies.append(
            pltpu.make_async_copy(
                packets_hbm.at[part, pl.ds(ROW_BLOCK, WEIGHT_ROWS)],
                weight_ref.at[part],
                weight_sems.at[k],
            )
        )
    bridge_copy = pltpu.make_async_copy(bridge_hbm, bridge_ref, other_sems.at[0])
    dec_copy = pltpu.make_async_copy(dec_weight_hbm, dec_weight_ref, other_sems.at[1])
    for copy in kv_copies + weight_copies + [bridge_copy, dec_copy]:
        copy.start()
    source = lax.broadcasted_iota(jnp.int32, spread_ref.shape, 0) - ENC_SHIFT
    place = lax.broadcasted_iota(jnp.int32, spread_ref.shape, 1)
    block = (place * 2731) >> 16
    inside = place - block * WEIGHT_ROWS
    used = ENC_INNER // devices
    spread = jnp.where((source == block * used + inside) & (inside < used), 1.0, 0.0)
    spread_ref[...] = spread.astype(BF16)
    scale = LOG2_E / math.sqrt(HEAD_SIZE)
    value_base = 2 * ENC_INNER - ENC_WINDOW
    queries = []
    for pair in range(HEAD_PAIRS):
        first, width = lane_window(pair * PAIR_SIZE, PAIR_SIZE)
        part = query_ref[:, first : first + width]
        copies = [
            jnp.where(
                head_column(part.shape, 2 * pair + k, HEAD_SIZE, -first), part, jnp.zeros_like(part)
            )
            for k in range(2)
        ]
        queries.append(jnp.concatenate(copies, axis=0))
    length = per_chunk * ROW_BLOCK
    peaks = [None] * HEAD_PAIRS
    sums = [0.0] * HEAD_PAIRS
    mixes = [0.0] * HEAD_PAIRS
    for chunk in range(ENC_CHUNKS):
        each = ENC_COPIES // ENC_CHUNKS
        for copy in kv_copies[chunk * each : (chunk + 1) * each]:
            copy.wait()
        those = slice(chunk * per_chunk, (chunk + 1) * per_chunk)
        usable = mask_ref[:, chunk * length : (chunk + 1) * length] > 0.0
        for pair in range(HEAD_PAIRS):
            first, width = lane_window(pair * PAIR_SIZE, PAIR_SIZE)
            keys = kv_ref[those, :, first : first + width].reshape(length, width)
            scores = nt_dot(queries[pair], keys)
            scores = jnp.where(usable, scores, NEG_FILL)
            peak = jnp.max(scores, axis=-1, keepdims=True)
            if chunk > 0:
                peak = jnp.maximum(peaks[pair], peak)
                fade = jnp.exp2((peaks[pair] - peak) * scale)
                sums[pair] *= fade
                mixes[pair] *= fade
            peaks[pair] = peak
            weights = jnp.exp2((scores - peak) * scale)
            sums[pair] += jnp.sum(weights, axis=-1, keepdims=True)
            first, width = lane_window(ENC_SHIFT + pair * PAIR_SIZE, PAIR_SIZE)
            first += value_base
            values = kv_ref[those, :, first : first + width].reshape(length, width)
            mixes[pair] += jnp.dot(weights.astype(BF16), values, preferred_element_type=F32)
    attn_ref[...] = jnp.zeros_like(attn_ref)
    for pair in range(HEAD_PAIRS):
        first, width = lane_window(ENC_SHIFT + pair * PAIR_SIZE, PAIR_SIZE)
        mixed = mixes[pair] / sums[pair]
        part = attn_ref[:, first : first + width]
        for k in range(2):
            mine = head_column(part.shape, 2 * pair + k, HEAD_SIZE, ENC_SHIFT - first)
            part = jnp.where(mine, mixed[k * ROW_BLOCK : (k + 1) * ROW_BLOCK], part)
        attn_ref[:, first : first + width] = part
    attn = attn_ref[...].astype(BF16)
    attn = jnp.dot(attn, spread_ref[...], preferred_element_type=F32).astype(BF16)
    for copy in weight_copies:
        copy.wait()
    weight = weight_ref[...].reshape(-1, weight_ref.shape[-1])
    projected = jnp.dot(attn, weight, preferred_element_type=F32)
    computed = (residual_ref[...].astype(F32) + projected).astype(BF16)
    slot = lax.broadcasted_iota(jnp.int32, computed.shape, 0)
    enc_out_ref[...] = jnp.where(slot < live_ref[0], computed, jnp.zeros_like(computed))
    out_copy = pltpu.make_async_copy(enc_out_ref, enc_out_hbm, other_sems.at[2])
    out_copy.start()
    normed = layer_norm(computed, norm_gain_ref[...]).astype(BF16)
    bridge_copy.wait()
    bridged = jnp.dot(normed, bridge_ref[...], preferred_element_type=F32) + pe_ref[...]
    dec_normed = layer_norm(bridged.astype(BF16), dec_gain_ref[...]).astype(BF16)
    dec_copy.wait()
    pairs = jnp.dot(dec_normed, dec_weight_ref[...], preferred_element_type=F32)
    vis_ref[...] = pairs.astype(BF16)
    out_copy.wait()


def head_stats(stats, head, peak, summed):
    lane = lax.broadcasted_iota(jnp.int32, stats.shape, 1)
    stats = jnp.where(lane == head, peak, stats)
    return jnp.where(lane == DEC_HEADS + head, summed, stats)


def unit_rows(count, width):
    row = lax.broadcasted_iota(jnp.int32, (count, width), 0)
    column = lax.broadcasted_iota(jnp.int32, (count, width), 1)
    return jnp.where(row == column, 1.0, 0.0).astype(BF16)


def three_parts(numbers):
    high = numbers.astype(BF16).astype(F32)
    middle = (numbers - high).astype(BF16).astype(F32)
    return high, middle, numbers - high - middle


def coded_stats(stats):
    group = 2 * DEC_HEADS
    high, middle, low = three_parts(stats)
    lanes = high + pltpu.roll(middle, group, 1) + pltpu.roll(low, 2 * group, 1)
    return nt_dot(unit_rows(STAT_ROWS, LANES), lanes.astype(BF16)).astype(BF16)


def decoded_stats(coded):
    group = 2 * DEC_HEADS
    widened = coded.astype(F32)
    return widened[:group] + (widened[group : 2 * group] + widened[2 * group :])


def kept_kernel(kept_ref, gain_ref, weight_ref, query_ref, state_ref):
    scale = LOG2_E / math.sqrt(DEC_HEAD_SIZE)
    normed = layer_norm(kept_ref[...], gain_ref[...]).astype(BF16)
    pairs = jnp.dot(normed, weight_ref[...], preferred_element_type=F32).astype(BF16)
    queries = query_ref[...]
    total = jnp.zeros(queries.shape, F32)
    stats = jnp.zeros((queries.shape[0], LANES), F32)
    for h in range(DEC_HEADS):
        mine = head_column(queries.shape, h, DEC_HEAD_SIZE, 0)
        scores = nt_dot(jnp.where(mine, queries, jnp.zeros_like(queries)), pairs[:, :DEC_INNER])
        peak = jnp.max(scores, axis=-1, keepdims=True)
        weights = jnp.exp2((scores - peak) * scale)
        stats = head_stats(stats, h, peak, jnp.sum(weights, axis=-1, keepdims=True))
        mixed = jnp.dot(weights.astype(BF16), pairs[:, DEC_INNER:], preferred_element_type=F32)
        total = jnp.where(mine, mixed, total)
    state_ref[:, :DEC_INNER] = total
    state_ref[:, DEC_INNER:] = stats


def visible_kernel(vis_ref, mask_ref, query_ref, state_ref, out_ref):
    scale = LOG2_E / math.sqrt(DEC_HEAD_SIZE)
    usable = mask_ref[...] > 0.0
    queries = query_ref[...]
    total = jnp.zeros(queries.shape, F32)
    stats = jnp.zeros((queries.shape[0], LANES), F32)
    for h in range(DEC_HEADS):
        place = DEC_INNER + h
        kept_peak = state_ref[:, place : place + 1]
        kept_sum = state_ref[:, place + DEC_HEADS : place + DEC_HEADS + 1]
        mine = head_column(queries.shape, h, DEC_HEAD_SIZE, 0)
        scores = nt_dot(jnp.where(mine, queries, jnp.zeros_like(queries)), vis_ref[:, :DEC_INNER])
        scores = jnp.where(usable, scores, NEG_FILL)
        peak = jnp.maximum(kept_peak, jnp.max(scores, axis=-1, keepdims=True))
        weights = jnp.exp2((scores - peak) * scale)
        fade = jnp.exp2((kept_peak - peak) * scale)
        summed = kept_sum * fade + jnp.sum(weights, axis=-1, keepdims=True)
        stats = head_stats(stats, h, peak, summed)
        mixed = jnp.dot(weights.astype(BF16), vis_ref[:, DEC_INNER:], preferred_element_type=F32)
        total = jnp.where(mine, mixed + fade * state_ref[:, :DEC_INNER], total)
    near = out_ref.shape[0]
    rows = out_ref.shape[1] - STAT_ROWS
    for k in range(near):
        those = slice(k * rows, (k + 1) * rows)
        out_ref[k, :rows] = total[those].astype(BF16)
        out_ref[k, rows:] = jnp.zeros((STAT_ROWS, DEC_INNER), BF16)
        out_ref[k, rows:, :rows] = coded_stats(stats[those])


def finish_kernel(parts_ref, kept_ref, weight_ref, out_ref):
    scale = LOG2_E / math.sqrt(DEC_HEAD_SIZE)
    near = parts_ref.shape[0]
    rows = parts_ref.shape[1] - STAT_ROWS
    stats = [decoded_stats(parts_ref[k, rows:, :rows]) for k in range(near)]
    peak = stats[0]
    for k in range(1, near):
        peak = jnp.maximum(peak, stats[k])
    fades = [jnp.exp2((stats[k] - peak) * scale) for k in range(near)]
    summed = 0.0
    for k in range(near):
        summed += pltpu.roll(fades[k], DEC_HEADS, 0) * stats[k]
    summed = pltpu.roll(summed, DEC_HEADS, 0)
    group = 2 * DEC_HEADS
    row = lax.broadcasted_iota(jnp.int32, (STAT_ROWS, DEC_INNER), 0)
    column = lax.broadcasted_iota(jnp.int32, (STAT_ROWS, DEC_INNER), 1)
    within = row - row // group * group
    over_heads = jnp.where(within == column // DEC_HEAD_SIZE, 1.0, 0.0).astype(BF16)
    turn = unit_rows(rows, rows)
    is_head = lax.broadcasted_iota(jnp.int32, summed.shape, 0) < DEC_HEADS
    total = jnp.zeros((rows, DEC_INNER), F32)
    for k in range(near):
        factor = jnp.where(is_head, fades[k] / summed, 0.0)
        factor = jnp.concatenate(three_parts(factor), axis=0).astype(BF16)
        factor = nt_dot(turn, factor).astype(BF16)
        factor = jnp.dot(factor, over_heads, preferred_element_type=F32)
        total += parts_ref[k, :rows].astype(F32) * factor
    attn = total.astype(BF16)
    projected = jnp.dot(attn, weight_ref[...], preferred_element_type=F32)
    out_ref[...] = (kept_ref[...].astype(F32) + projected).astype(BF16)


def call(kernel, out_shape, *operands, scalars=0, in_hbm=(), out_hbm=(), scratch=()):
    in_vmem = pl.BlockSpec(memory_space=pltpu.VMEM)
    specs = [in_vmem] * len(operands)
    for k in range(scalars):
        specs[k] = pl.BlockSpec(memory_space=pltpu.SMEM)
    for k in in_hbm:
        specs[k] = pl.BlockSpec(memory_space=pl.ANY)
    out_specs = jax.tree.map(lambda _: in_vmem, out_shape)
    for k in out_hbm:
        out_specs = out_specs[:k] + (pl.BlockSpec(memory_space=pl.ANY),) + out_specs[k + 1 :]
    return pl.pallas_call(
        kernel,
        out_shape=out_shape,
        in_specs=specs,
        out_specs=out_specs,
        scratch_shapes=list(scratch),
        compiler_params=pltpu.CompilerParams(vmem_limit_bytes=56 * 1024 * 1024),
    )(*operands)


def body(
    enc_rows,
    vis_count,
    vis_dest,
    vis_pos,
    kept_pos,
    out_weight,
    norm_gain,
    bridge_weight,
    mask_token,
    dec_gain,
    dec_qkv_weight,
    dec_out_weight,
):
    row_block = ROW_BLOCK
    shape_of = jax.ShapeDtypeStruct
    myself = lax.axis_index(SEQ)
    near = lax.axis_size(NEAR)
    far = lax.axis_size("far")
    bal_counts = balance_table(vis_count, row_block)
    has_own = vis_count[myself] > 0

    pair_rows = enc_rows[:, ENC_INNER : 3 * ENC_INNER]
    key_value = jnp.where(has_own, pair_rows[:row_block], shifted(pair_rows[row_block:], SEQ, 1))
    seq_devices = lax.axis_size(SEQ)
    weight_rows = out_weight.shape[0]
    padded_weight = jnp.pad(out_weight, ((0, WEIGHT_ROWS - weight_rows), (0, 0)))
    packet = jnp.concatenate([key_value, padded_weight], axis=0)
    packets = lax.all_gather(packet, SEQ, axis=0, tiled=True).reshape(seq_devices, -1, packet.shape[1])
    enc_late, kept_pos, _ = lax.optimization_barrier((enc_rows, kept_pos, key_value))

    kept_dev = kept_pos.shape[0]
    kept_all = lax.all_to_all(
        jnp.broadcast_to(kept_pos[None, :], (far, kept_dev)), "far", 0, 0, tiled=True
    )
    kept_all = kept_all.reshape(-1).astype(F32)

    rest = jnp.concatenate([enc_late[:, :ENC_INNER], enc_late[:, 3 * ENC_INNER :]], axis=1)
    rest = jnp.where(has_own, rest[:row_block], shifted(rest[row_block:], SEQ, 1))
    queries = jnp.pad(rest[:, :ENC_INNER], ((0, 0), (0, ENC_SHIFT)))
    residual = rest[:, ENC_INNER:]

    kept_in = (mask_token.astype(F32)[None, :] + sinusoid(kept_pos)).astype(BF16)
    own_normed = layer_norm(kept_in, dec_gain[None, :]).astype(BF16)
    asking = jnp.dot(
        own_normed, dec_qkv_weight[:, :DEC_INNER], preferred_element_type=F32
    ).astype(BF16)
    asking = lax.all_gather(asking, NEAR, axis=0, tiled=True)
    mask_split = halves_first(mask_token)
    kept_split = (mask_split.astype(F32)[None, :] + split_sinusoid(kept_all)).astype(BF16)
    asked = asking.shape[0]
    kept_state = call(
        kept_kernel,
        shape_of((asked, DEC_INNER + LANES), F32),
        kept_split,
        halves_first(dec_gain)[None, :],
        halves_first(dec_qkv_weight[:, DEC_INNER:]),
        asking,
    )

    packets, kept_state = lax.optimization_barrier((packets, kept_state))

    first_row = jnp.where(has_own, myself * 2 * row_block, (myself - 1) * 2 * row_block + row_block)
    bal_pos = lax.dynamic_slice_in_dim(vis_pos, first_row, row_block)
    within = jnp.arange(row_block, dtype=jnp.int32)
    live = (within[None, :] < bal_counts[:, None]).astype(F32)
    pair_width = 2 * DEC_INNER
    model_width = residual.shape[1]
    enc_out, vis_kv = call(
        encoder_kernel,
        (
            shape_of((row_block, model_width), BF16),
            shape_of((row_block, pair_width), BF16),
        ),
        bal_counts[myself][None],
        packets,
        queries,
        live.reshape(1, -1),
        residual,
        norm_gain[None, :],
        bridge_weight,
        sinusoid(bal_pos),
        dec_gain[None, :],
        dec_qkv_weight[:, DEC_INNER:],
        scalars=1,
        in_hbm=(1, 6, 9),
        out_hbm=(0,),
        scratch=(
            pltpu.VMEM((seq_devices, row_block, 2 * ENC_INNER), BF16),
            pltpu.VMEM((seq_devices, WEIGHT_ROWS, model_width), BF16),
            pltpu.VMEM(bridge_weight.shape, BF16),
            pltpu.VMEM((DEC_WIDTH, pair_width), BF16),
            pltpu.VMEM((ENC_WINDOW, seq_devices * WEIGHT_ROWS), BF16),
            pltpu.VMEM((row_block, ENC_WINDOW), F32),
            pltpu.VMEM((row_block, model_width), BF16),
            pltpu.SemaphoreType.DMA((ENC_COPIES,)),
            pltpu.SemaphoreType.DMA((WEIGHT_COPIES,)),
            pltpu.SemaphoreType.DMA((3,)),
        ),
    )

    vis_all = lax.all_gather(vis_kv, "far", axis=0, tiled=True)
    live_same = lax.dynamic_index_in_dim(
        live.reshape(far, near, row_block), lax.axis_index(NEAR), axis=1, keepdims=False
    )
    parts = call(
        visible_kernel,
        shape_of((near, kept_dev + STAT_ROWS, DEC_INNER), BF16),
        vis_all,
        live_same.reshape(1, -1),
        asking,
        kept_state,
    )
    parts = lax.all_to_all(parts, NEAR, 0, 0, tiled=True)
    dec_out = call(
        finish_kernel,
        shape_of((kept_dev, DEC_WIDTH), BF16),
        parts,
        kept_in,
        dec_out_weight,
    )
    return (enc_out, dec_out)


def solution(mesh):
    grid = (mesh.shape["clip"], mesh.shape["seq"] // (2 * NEAR_CHIPS), NEAR_CHIPS, 2)
    finer = Mesh(mesh.devices.reshape(grid), CLIP_SEQ)
    return jax.shard_map(
        body,
        mesh=finer,
        in_specs=(
            P(CLIP_SEQ, None),
            P("clip"),
            P("clip"),
            P("clip"),
            P(CLIP_SEQ),
            P(SEQ, None),
            P(),
            P(),
            P(),
            P(),
            P(),
            P(),
        ),
        out_specs=(P(CLIP_SEQ, None), P(CLIP_SEQ, None)),
        check_vma=False,
    )
```

```python
import math

import jax
import jax.numpy as jnp
import numpy as np
from jax import lax
from jax.experimental import pallas as pl
from jax.experimental.pallas import tpu as pltpu
from jax.sharding import Mesh
from jax.sharding import PartitionSpec as P

HEAD_SIZE = 88
ENC_HEADS = 8
ENC_INNER = ENC_HEADS * HEAD_SIZE
DEC_WIDTH = 512
DEC_HEAD_SIZE = 64
DEC_HEADS = 4
DEC_INNER = DEC_HEADS * DEC_HEAD_SIZE
ROW_BLOCK = 64
WEIGHT_ROWS = 24
STAT_ROWS = 24
ENC_CHUNKS = 2
ENC_COPIES = 8
WEIGHT_COPIES = 4
LANES = 128
SEQ = ("far", "chip", "core")
NEAR = "chip"
FAR = ("far", "core")
CLIP_SEQ = ("clip", "far", "chip", "core")
NEAR_CHIPS = 4
ENC_WINDOW = 768
ENC_SHIFT = ENC_WINDOW - ENC_INNER
HEAD_PAIRS = ENC_HEADS // 2
PAIR_SIZE = 2 * HEAD_SIZE

LOG2_E = math.log2(math.e)
NEG_FILL = -1e30
LN_EPS = 1e-06
F32 = jnp.float32
BF16 = jnp.bfloat16


def shifted(shard, axis, by):
    devices = lax.axis_size(axis)
    pairs = [(i, i + by) for i in range(devices) if 0 <= i + by < devices]
    return lax.ppermute(shard, axis, pairs)


def layer_norm(rows_in, gain_row):
    widened = rows_in.astype(F32)
    centred = widened - jnp.mean(widened, axis=-1, keepdims=True)
    spread = jnp.mean(centred * centred, axis=-1, keepdims=True)
    return centred * lax.rsqrt(spread + LN_EPS) * gain_row


def frequencies():
    half = np.arange(DEC_WIDTH // 2)
    return jnp.asarray(np.power(10000.0, -half * 2.0 / DEC_WIDTH).astype(np.float32))


def sinusoid(positions):
    angles = positions.astype(F32)[:, None] * frequencies()[None, :]
    return jnp.stack([jnp.sin(angles), jnp.cos(angles)], axis=-1).reshape(
        positions.shape[0], DEC_WIDTH
    )


def split_sinusoid(positions):
    angles = positions[:, None] * frequencies()[None, :]
    return jnp.concatenate([jnp.sin(angles), jnp.cos(angles)], axis=-1)


def halves_first(rows):
    apart = rows.reshape(rows.shape[0] // 2, 2, *rows.shape[1:])
    return jnp.concatenate([apart[:, 0], apart[:, 1]], axis=0)


def balance_table(vis_count, row_block):
    left_count = jnp.concatenate([vis_count[:1] * 0, vis_count[:-1]], axis=0)
    return jnp.where(vis_count > 0, jnp.minimum(vis_count, row_block), left_count - row_block)


def nt_dot(left, right):
    return lax.dot_general(left, right, (((1,), (1,)), ((), ())), preferred_element_type=F32)


def head_column(shape, head, size, offset):
    column = lax.broadcasted_iota(jnp.int32, shape, 1) - offset
    return (column >= head * size) & (column < (head + 1) * size)


def lane_window(start, size):
    first = start // LANES * LANES
    return first, -(-(start + size - first) // LANES) * LANES


def encoder_kernel(
    live_ref,
    packets_hbm,
    query_ref,
    mask_ref,
    residual_ref,
    norm_gain_ref,
    bridge_hbm,
    pe_ref,
    dec_gain_ref,
    dec_weight_hbm,
    enc_out_hbm,
    vis_ref,
    kv_ref,
    weight_ref,
    bridge_ref,
    dec_weight_ref,
    spread_ref,
    attn_ref,
    enc_out_ref,
    kv_sems,
    weight_sems,
    other_sems,
):
    devices = packets_hbm.shape[0]
    per_chunk = devices // ENC_CHUNKS
    kv_copies = []
    for k in range(ENC_COPIES):
        part = pl.ds(k * (devices // ENC_COPIES), devices // ENC_COPIES)
        kv_copies.append(
            pltpu.make_async_copy(
                packets_hbm.at[part, pl.ds(0, ROW_BLOCK)], kv_ref.at[part], kv_sems.at[k]
            )
        )
    weight_copies = []
    for k in range(WEIGHT_COPIES):
        part = pl.ds(k * (devices // WEIGHT_COPIES), devices // WEIGHT_COPIES)
        weight_copies.append(
            pltpu.make_async_copy(
                packets_hbm.at[part, pl.ds(ROW_BLOCK, WEIGHT_ROWS)],
                weight_ref.at[part],
                weight_sems.at[k],
            )
        )
    bridge_copy = pltpu.make_async_copy(bridge_hbm, bridge_ref, other_sems.at[0])
    dec_copy = pltpu.make_async_copy(dec_weight_hbm, dec_weight_ref, other_sems.at[1])
    for copy in kv_copies + weight_copies + [bridge_copy, dec_copy]:
        copy.start()
    source = lax.broadcasted_iota(jnp.int32, spread_ref.shape, 0) - ENC_SHIFT
    place = lax.broadcasted_iota(jnp.int32, spread_ref.shape, 1)
    block = (place * 2731) >> 16
    inside = place - block * WEIGHT_ROWS
    used = ENC_INNER // devices
    spread = jnp.where((source == block * used + inside) & (inside < used), 1.0, 0.0)
    spread_ref[...] = spread.astype(BF16)
    scale = LOG2_E / math.sqrt(HEAD_SIZE)
    value_base = 2 * ENC_INNER - ENC_WINDOW
    queries = []
    for pair in range(HEAD_PAIRS):
        first, width = lane_window(pair * PAIR_SIZE, PAIR_SIZE)
        part = query_ref[:, first : first + width]
        copies = [
            jnp.where(
                head_column(part.shape, 2 * pair + k, HEAD_SIZE, -first), part, jnp.zeros_like(part)
            )
            for k in range(2)
        ]
        queries.append(jnp.concatenate(copies, axis=0))
    length = per_chunk * ROW_BLOCK
    peaks = [None] * HEAD_PAIRS
    sums = [0.0] * HEAD_PAIRS
    mixes = [0.0] * HEAD_PAIRS
    for chunk in range(ENC_CHUNKS):
        each = ENC_COPIES // ENC_CHUNKS
        for copy in kv_copies[chunk * each : (chunk + 1) * each]:
            copy.wait()
        those = slice(chunk * per_chunk, (chunk + 1) * per_chunk)
        usable = mask_ref[:, chunk * length : (chunk + 1) * length] > 0.0
        for pair in range(HEAD_PAIRS):
            first, width = lane_window(pair * PAIR_SIZE, PAIR_SIZE)
            keys = kv_ref[those, :, first : first + width].reshape(length, width)
            scores = nt_dot(queries[pair], keys)
            scores = jnp.where(usable, scores, NEG_FILL)
            peak = jnp.max(scores, axis=-1, keepdims=True)
            if chunk > 0:
                peak = jnp.maximum(peaks[pair], peak)
                fade = jnp.exp2((peaks[pair] - peak) * scale)
                sums[pair] *= fade
                mixes[pair] *= fade
            peaks[pair] = peak
            weights = jnp.exp2((scores - peak) * scale)
            sums[pair] += jnp.sum(weights, axis=-1, keepdims=True)
            first, width = lane_window(ENC_SHIFT + pair * PAIR_SIZE, PAIR_SIZE)
            first += value_base
            values = kv_ref[those, :, first : first + width].reshape(length, width)
            mixes[pair] += jnp.dot(weights.astype(BF16), values, preferred_element_type=F32)
    attn_ref[...] = jnp.zeros_like(attn_ref)
    for pair in range(HEAD_PAIRS):
        first, width = lane_window(ENC_SHIFT + pair * PAIR_SIZE, PAIR_SIZE)
        mixed = mixes[pair] / sums[pair]
        part = attn_ref[:, first : first + width]
        for k in range(2):
            mine = head_column(part.shape, 2 * pair + k, HEAD_SIZE, ENC_SHIFT - first)
            part = jnp.where(mine, mixed[k * ROW_BLOCK : (k + 1) * ROW_BLOCK], part)
        attn_ref[:, first : first + width] = part
    attn = attn_ref[...].astype(BF16)
    attn = jnp.dot(attn, spread_ref[...], preferred_element_type=F32).astype(BF16)
    for copy in weight_copies:
        copy.wait()
    weight = weight_ref[...].reshape(-1, weight_ref.shape[-1])
    projected = jnp.dot(attn, weight, preferred_element_type=F32)
    computed = (residual_ref[...].astype(F32) + projected).astype(BF16)
    slot = lax.broadcasted_iota(jnp.int32, computed.shape, 0)
    enc_out_ref[...] = jnp.where(slot < live_ref[0], computed, jnp.zeros_like(computed))
    out_copy = pltpu.make_async_copy(enc_out_ref, enc_out_hbm, other_sems.at[2])
    out_copy.start()
    normed = layer_norm(computed, norm_gain_ref[...]).astype(BF16)
    bridge_copy.wait()
    bridged = jnp.dot(normed, bridge_ref[...], preferred_element_type=F32) + pe_ref[...]
    dec_normed = layer_norm(bridged.astype(BF16), dec_gain_ref[...]).astype(BF16)
    dec_copy.wait()
    pairs = jnp.dot(dec_normed, dec_weight_ref[...], preferred_element_type=F32)
    vis_ref[...] = pairs.astype(BF16)
    out_copy.wait()


def head_stats(stats, head, peak, summed):
    lane = lax.broadcasted_iota(jnp.int32, stats.shape, 1)
    stats = jnp.where(lane == head, peak, stats)
    return jnp.where(lane == DEC_HEADS + head, summed, stats)


def unit_rows(count, width):
    row = lax.broadcasted_iota(jnp.int32, (count, width), 0)
    column = lax.broadcasted_iota(jnp.int32, (count, width), 1)
    return jnp.where(row == column, 1.0, 0.0).astype(BF16)


def three_parts(numbers):
    high = numbers.astype(BF16).astype(F32)
    middle = (numbers - high).astype(BF16).astype(F32)
    return high, middle, numbers - high - middle


def coded_stats(stats):
    group = 2 * DEC_HEADS
    high, middle, low = three_parts(stats)
    lanes = high + pltpu.roll(middle, group, 1) + pltpu.roll(low, 2 * group, 1)
    return nt_dot(unit_rows(STAT_ROWS, LANES), lanes.astype(BF16)).astype(BF16)


def decoded_stats(coded):
    group = 2 * DEC_HEADS
    widened = coded.astype(F32)
    return widened[:group] + (widened[group : 2 * group] + widened[2 * group :])


def kept_kernel(kept_ref, gain_ref, weight_ref, query_ref, state_ref):
    scale = LOG2_E / math.sqrt(DEC_HEAD_SIZE)
    normed = layer_norm(kept_ref[...], gain_ref[...]).astype(BF16)
    pairs = jnp.dot(normed, weight_ref[...], preferred_element_type=F32).astype(BF16)
    queries = query_ref[...]
    total = jnp.zeros(queries.shape, F32)
    stats = jnp.zeros((queries.shape[0], LANES), F32)
    for h in range(DEC_HEADS):
        mine = head_column(queries.shape, h, DEC_HEAD_SIZE, 0)
        scores = nt_dot(jnp.where(mine, queries, jnp.zeros_like(queries)), pairs[:, :DEC_INNER])
        peak = jnp.max(scores, axis=-1, keepdims=True)
        weights = jnp.exp2((scores - peak) * scale)
        stats = head_stats(stats, h, peak, jnp.sum(weights, axis=-1, keepdims=True))
        mixed = jnp.dot(weights.astype(BF16), pairs[:, DEC_INNER:], preferred_element_type=F32)
        total = jnp.where(mine, mixed, total)
    state_ref[:, :DEC_INNER] = total
    state_ref[:, DEC_INNER:] = stats


def visible_kernel(vis_ref, mask_ref, query_ref, state_ref, out_ref):
    scale = LOG2_E / math.sqrt(DEC_HEAD_SIZE)
    usable = mask_ref[...] > 0.0
    queries = query_ref[...]
    total = jnp.zeros(queries.shape, F32)
    stats = jnp.zeros((queries.shape[0], LANES), F32)
    for h in range(DEC_HEADS):
        place = DEC_INNER + h
        kept_peak = state_ref[:, place : place + 1]
        kept_sum = state_ref[:, place + DEC_HEADS : place + DEC_HEADS + 1]
        mine = head_column(queries.shape, h, DEC_HEAD_SIZE, 0)
        scores = nt_dot(jnp.where(mine, queries, jnp.zeros_like(queries)), vis_ref[:, :DEC_INNER])
        scores = jnp.where(usable, scores, NEG_FILL)
        peak = jnp.maximum(kept_peak, jnp.max(scores, axis=-1, keepdims=True))
        weights = jnp.exp2((scores - peak) * scale)
        fade = jnp.exp2((kept_peak - peak) * scale)
        summed = kept_sum * fade + jnp.sum(weights, axis=-1, keepdims=True)
        stats = head_stats(stats, h, peak, summed)
        mixed = jnp.dot(weights.astype(BF16), vis_ref[:, DEC_INNER:], preferred_element_type=F32)
        total = jnp.where(mine, mixed + fade * state_ref[:, :DEC_INNER], total)
    near = out_ref.shape[0]
    rows = out_ref.shape[1] - STAT_ROWS
    for k in range(near):
        those = slice(k * rows, (k + 1) * rows)
        out_ref[k, :rows] = total[those].astype(BF16)
        out_ref[k, rows:] = jnp.zeros((STAT_ROWS, DEC_INNER), BF16)
        out_ref[k, rows:, :rows] = coded_stats(stats[those])


def finish_kernel(parts_ref, kept_ref, weight_ref, out_ref):
    scale = LOG2_E / math.sqrt(DEC_HEAD_SIZE)
    near = parts_ref.shape[0]
    rows = parts_ref.shape[1] - STAT_ROWS
    stats = [decoded_stats(parts_ref[k, rows:, :rows]) for k in range(near)]
    peak = stats[0]
    for k in range(1, near):
        peak = jnp.maximum(peak, stats[k])
    fades = [jnp.exp2((stats[k] - peak) * scale) for k in range(near)]
    summed = 0.0
    for k in range(near):
        summed += pltpu.roll(fades[k], DEC_HEADS, 0) * stats[k]
    summed = pltpu.roll(summed, DEC_HEADS, 0)
    group = 2 * DEC_HEADS
    row = lax.broadcasted_iota(jnp.int32, (STAT_ROWS, DEC_INNER), 0)
    column = lax.broadcasted_iota(jnp.int32, (STAT_ROWS, DEC_INNER), 1)
    within = row - row // group * group
    over_heads = jnp.where(within == column // DEC_HEAD_SIZE, 1.0, 0.0).astype(BF16)
    turn = unit_rows(rows, rows)
    is_head = lax.broadcasted_iota(jnp.int32, summed.shape, 0) < DEC_HEADS
    total = jnp.zeros((rows, DEC_INNER), F32)
    for k in range(near):
        factor = jnp.where(is_head, fades[k] / summed, 0.0)
        factor = jnp.concatenate(three_parts(factor), axis=0).astype(BF16)
        factor = nt_dot(turn, factor).astype(BF16)
        factor = jnp.dot(factor, over_heads, preferred_element_type=F32)
        total += parts_ref[k, :rows].astype(F32) * factor
    attn = total.astype(BF16)
    projected = jnp.dot(attn, weight_ref[...], preferred_element_type=F32)
    out_ref[...] = (kept_ref[...].astype(F32) + projected).astype(BF16)


def call(kernel, out_shape, *operands, scalars=0, in_hbm=(), out_hbm=(), scratch=()):
    in_vmem = pl.BlockSpec(memory_space=pltpu.VMEM)
    specs = [in_vmem] * len(operands)
    for k in range(scalars):
        specs[k] = pl.BlockSpec(memory_space=pltpu.SMEM)
    for k in in_hbm:
        specs[k] = pl.BlockSpec(memory_space=pl.ANY)
    out_specs = jax.tree.map(lambda _: in_vmem, out_shape)
    for k in out_hbm:
        out_specs = out_specs[:k] + (pl.BlockSpec(memory_space=pl.ANY),) + out_specs[k + 1 :]
    return pl.pallas_call(
        kernel,
        out_shape=out_shape,
        in_specs=specs,
        out_specs=out_specs,
        scratch_shapes=list(scratch),
        compiler_params=pltpu.CompilerParams(vmem_limit_bytes=56 * 1024 * 1024),
    )(*operands)


def body(
    enc_rows,
    vis_count,
    vis_dest,
    vis_pos,
    kept_pos,
    out_weight,
    norm_gain,
    bridge_weight,
    mask_token,
    dec_gain,
    dec_qkv_weight,
    dec_out_weight,
):
    row_block = ROW_BLOCK
    shape_of = jax.ShapeDtypeStruct
    myself = lax.axis_index(SEQ)
    near = lax.axis_size(NEAR)
    far = lax.axis_size(FAR)
    bal_counts = balance_table(vis_count, row_block)
    has_own = vis_count[myself] > 0

    pair_rows = enc_rows[:, ENC_INNER : 3 * ENC_INNER]
    key_value = jnp.where(has_own, pair_rows[:row_block], shifted(pair_rows[row_block:], SEQ, 1))
    seq_devices = lax.axis_size(SEQ)
    weight_rows = out_weight.shape[0]
    padded_weight = jnp.pad(out_weight, ((0, WEIGHT_ROWS - weight_rows), (0, 0)))
    packet = jnp.concatenate([key_value, padded_weight], axis=0)
    packets = lax.all_gather(packet, SEQ, axis=0, tiled=True).reshape(seq_devices, -1, packet.shape[1])
    enc_late, kept_pos, _ = lax.optimization_barrier((enc_rows, kept_pos, key_value))

    kept_dev = kept_pos.shape[0]
    kept_all = lax.all_to_all(
        jnp.broadcast_to(kept_pos[None, :], (far, kept_dev)), FAR, 0, 0, tiled=True
    )
    kept_all = kept_all.reshape(-1).astype(F32)

    rest = jnp.concatenate([enc_late[:, :ENC_INNER], enc_late[:, 3 * ENC_INNER :]], axis=1)
    rest = jnp.where(has_own, rest[:row_block], shifted(rest[row_block:], SEQ, 1))
    queries = jnp.pad(rest[:, :ENC_INNER], ((0, 0), (0, ENC_SHIFT)))
    residual = rest[:, ENC_INNER:]

    kept_in = (mask_token.astype(F32)[None, :] + sinusoid(kept_pos)).astype(BF16)
    own_normed = layer_norm(kept_in, dec_gain[None, :]).astype(BF16)
    asking = jnp.dot(
        own_normed, dec_qkv_weight[:, :DEC_INNER], preferred_element_type=F32
    ).astype(BF16)
    asking = lax.all_gather(asking, NEAR, axis=0, tiled=True)
    mask_split = halves_first(mask_token)
    kept_split = (mask_split.astype(F32)[None, :] + split_sinusoid(kept_all)).astype(BF16)
    asked = asking.shape[0]
    kept_state = call(
        kept_kernel,
        shape_of((asked, DEC_INNER + LANES), F32),
        kept_split,
        halves_first(dec_gain)[None, :],
        halves_first(dec_qkv_weight[:, DEC_INNER:]),
        asking,
    )

    packets, kept_state = lax.optimization_barrier((packets, kept_state))

    first_row = jnp.where(has_own, myself * 2 * row_block, (myself - 1) * 2 * row_block + row_block)
    bal_pos = lax.dynamic_slice_in_dim(vis_pos, first_row, row_block)
    within = jnp.arange(row_block, dtype=jnp.int32)
    live = (within[None, :] < bal_counts[:, None]).astype(F32)
    pair_width = 2 * DEC_INNER
    model_width = residual.shape[1]
    enc_out, vis_kv = call(
        encoder_kernel,
        (
            shape_of((row_block, model_width), BF16),
            shape_of((row_block, pair_width), BF16),
        ),
        bal_counts[myself][None],
        packets,
        queries,
        live.reshape(1, -1),
        residual,
        norm_gain[None, :],
        bridge_weight,
        sinusoid(bal_pos),
        dec_gain[None, :],
        dec_qkv_weight[:, DEC_INNER:],
        scalars=1,
        in_hbm=(1, 6, 9),
        out_hbm=(0,),
        scratch=(
            pltpu.VMEM((seq_devices, row_block, 2 * ENC_INNER), BF16),
            pltpu.VMEM((seq_devices, WEIGHT_ROWS, model_width), BF16),
            pltpu.VMEM(bridge_weight.shape, BF16),
            pltpu.VMEM((DEC_WIDTH, pair_width), BF16),
            pltpu.VMEM((ENC_WINDOW, seq_devices * WEIGHT_ROWS), BF16),
            pltpu.VMEM((row_block, ENC_WINDOW), F32),
            pltpu.VMEM((row_block, model_width), BF16),
            pltpu.SemaphoreType.DMA((ENC_COPIES,)),
            pltpu.SemaphoreType.DMA((WEIGHT_COPIES,)),
            pltpu.SemaphoreType.DMA((3,)),
        ),
    )

    vis_all = lax.all_gather(vis_kv, FAR, axis=0, tiled=True)
    live_same = lax.dynamic_index_in_dim(
        live.reshape(-1, near, lax.axis_size("core"), row_block),
        lax.axis_index(NEAR),
        axis=1,
        keepdims=False,
    )
    parts = call(
        visible_kernel,
        shape_of((near, kept_dev + STAT_ROWS, DEC_INNER), BF16),
        vis_all,
        live_same.reshape(1, -1),
        asking,
        kept_state,
    )
    parts = lax.all_to_all(parts, NEAR, 0, 0, tiled=True)
    dec_out = call(
        finish_kernel,
        shape_of((kept_dev, DEC_WIDTH), BF16),
        parts,
        kept_in,
        dec_out_weight,
    )
    return (enc_out, dec_out)


def solution(mesh):
    grid = (mesh.shape["clip"], mesh.shape["seq"] // (2 * NEAR_CHIPS), NEAR_CHIPS, 2)
    finer = Mesh(mesh.devices.reshape(grid), CLIP_SEQ)
    return jax.shard_map(
        body,
        mesh=finer,
        in_specs=(
            P(CLIP_SEQ, None),
            P("clip"),
            P("clip"),
            P("clip"),
            P(CLIP_SEQ),
            P(SEQ, None),
            P(),
            P(),
            P(),
            P(),
            P(),
            P(),
        ),
        out_specs=(P(CLIP_SEQ, None), P(CLIP_SEQ, None)),
        check_vma=False,
    )
```

```python
import math

import jax
import jax.numpy as jnp
import numpy as np
from jax import lax
from jax.experimental import pallas as pl
from jax.experimental.pallas import tpu as pltpu
from jax.sharding import Mesh
from jax.sharding import PartitionSpec as P

HEAD_SIZE = 88
ENC_HEADS = 8
ENC_INNER = ENC_HEADS * HEAD_SIZE
DEC_WIDTH = 512
DEC_HEAD_SIZE = 64
DEC_HEADS = 4
DEC_INNER = DEC_HEADS * DEC_HEAD_SIZE
ROW_BLOCK = 64
WEIGHT_ROWS = 24
STAT_ROWS = 24
ENC_CHUNKS = 2
ENC_COPIES = 16
WEIGHT_COPIES = 8
LANES = 128
SEQ = ("far", "chip", "core")
NEAR = "chip"
FAR = ("far", "core")
CLIP_SEQ = ("clip", "far", "chip", "core")
NEAR_CHIPS = 4
ENC_WINDOW = 768
ENC_SHIFT = ENC_WINDOW - ENC_INNER
HEAD_PAIRS = ENC_HEADS // 2
PAIR_SIZE = 2 * HEAD_SIZE

LOG2_E = math.log2(math.e)
NEG_FILL = -1e30
LN_EPS = 1e-06
F32 = jnp.float32
BF16 = jnp.bfloat16


def shifted(shard, axis, by):
    devices = lax.axis_size(axis)
    pairs = [(i, i + by) for i in range(devices) if 0 <= i + by < devices]
    return lax.ppermute(shard, axis, pairs)


def layer_norm(rows_in, gain_row):
    widened = rows_in.astype(F32)
    centred = widened - jnp.mean(widened, axis=-1, keepdims=True)
    spread = jnp.mean(centred * centred, axis=-1, keepdims=True)
    return centred * lax.rsqrt(spread + LN_EPS) * gain_row


def frequencies():
    half = np.arange(DEC_WIDTH // 2)
    return jnp.asarray(np.power(10000.0, -half * 2.0 / DEC_WIDTH).astype(np.float32))


def sinusoid(positions):
    angles = positions.astype(F32)[:, None] * frequencies()[None, :]
    return jnp.stack([jnp.sin(angles), jnp.cos(angles)], axis=-1).reshape(
        positions.shape[0], DEC_WIDTH
    )


def split_sinusoid(positions):
    angles = positions[:, None] * frequencies()[None, :]
    return jnp.concatenate([jnp.sin(angles), jnp.cos(angles)], axis=-1)


def halves_first(rows):
    apart = rows.reshape(rows.shape[0] // 2, 2, *rows.shape[1:])
    return jnp.concatenate([apart[:, 0], apart[:, 1]], axis=0)


def balance_table(vis_count, row_block):
    left_count = jnp.concatenate([vis_count[:1] * 0, vis_count[:-1]], axis=0)
    return jnp.where(vis_count > 0, jnp.minimum(vis_count, row_block), left_count - row_block)


def nt_dot(left, right):
    return lax.dot_general(left, right, (((1,), (1,)), ((), ())), preferred_element_type=F32)


def head_column(shape, head, size, offset):
    column = lax.broadcasted_iota(jnp.int32, shape, 1) - offset
    return (column >= head * size) & (column < (head + 1) * size)


def lane_window(start, size):
    first = start // LANES * LANES
    return first, -(-(start + size - first) // LANES) * LANES


def encoder_kernel(
    live_ref,
    packets_hbm,
    query_ref,
    mask_ref,
    residual_ref,
    norm_gain_ref,
    bridge_hbm,
    pe_ref,
    dec_gain_ref,
    dec_weight_hbm,
    enc_out_hbm,
    vis_ref,
    kv_ref,
    weight_ref,
    bridge_ref,
    dec_weight_ref,
    spread_ref,
    attn_ref,
    enc_out_ref,
    kv_sems,
    weight_sems,
    other_sems,
):
    devices = packets_hbm.shape[0]
    per_chunk = devices // ENC_CHUNKS
    kv_copies = []
    for k in range(ENC_COPIES):
        part = pl.ds(k * (devices // ENC_COPIES), devices // ENC_COPIES)
        kv_copies.append(
            pltpu.make_async_copy(
                packets_hbm.at[part, pl.ds(0, ROW_BLOCK)], kv_ref.at[part], kv_sems.at[k]
            )
        )
    weight_copies = []
    for k in range(WEIGHT_COPIES):
        part = pl.ds(k * (devices // WEIGHT_COPIES), devices // WEIGHT_COPIES)
        weight_copies.append(
            pltpu.make_async_copy(
                packets_hbm.at[part, pl.ds(ROW_BLOCK, WEIGHT_ROWS)],
                weight_ref.at[part],
                weight_sems.at[k],
            )
        )
    bridge_copy = pltpu.make_async_copy(bridge_hbm, bridge_ref, other_sems.at[0])
    dec_copy = pltpu.make_async_copy(dec_weight_hbm, dec_weight_ref, other_sems.at[1])
    for copy in kv_copies + weight_copies + [bridge_copy, dec_copy]:
        copy.start()
    source = lax.broadcasted_iota(jnp.int32, spread_ref.shape, 0) - ENC_SHIFT
    place = lax.broadcasted_iota(jnp.int32, spread_ref.shape, 1)
    block = (place * 2731) >> 16
    inside = place - block * WEIGHT_ROWS
    used = ENC_INNER // devices
    spread = jnp.where((source == block * used + inside) & (inside < used), 1.0, 0.0)
    spread_ref[...] = spread.astype(BF16)
    scale = LOG2_E / math.sqrt(HEAD_SIZE)
    value_base = 2 * ENC_INNER - ENC_WINDOW
    queries = []
    for pair in range(HEAD_PAIRS):
        first, width = lane_window(pair * PAIR_SIZE, PAIR_SIZE)
        part = query_ref[:, first : first + width]
        copies = [
            jnp.where(
                head_column(part.shape, 2 * pair + k, HEAD_SIZE, -first), part, jnp.zeros_like(part)
            )
            for k in range(2)
        ]
        queries.append(jnp.concatenate(copies, axis=0))
    length = per_chunk * ROW_BLOCK
    peaks = [None] * HEAD_PAIRS
    sums = [0.0] * HEAD_PAIRS
    mixes = [0.0] * HEAD_PAIRS
    for chunk in range(ENC_CHUNKS):
        each = ENC_COPIES // ENC_CHUNKS
        for copy in kv_copies[chunk * each : (chunk + 1) * each]:
            copy.wait()
        those = slice(chunk * per_chunk, (chunk + 1) * per_chunk)
        usable = mask_ref[:, chunk * length : (chunk + 1) * length] > 0.0
        for pair in range(HEAD_PAIRS):
            first, width = lane_window(pair * PAIR_SIZE, PAIR_SIZE)
            keys = kv_ref[those, :, first : first + width].reshape(length, width)
            scores = nt_dot(queries[pair], keys)
            scores = jnp.where(usable, scores, NEG_FILL)
            peak = jnp.max(scores, axis=-1, keepdims=True)
            if chunk > 0:
                peak = jnp.maximum(peaks[pair], peak)
                fade = jnp.exp2((peaks[pair] - peak) * scale)
                sums[pair] *= fade
                mixes[pair] *= fade
            peaks[pair] = peak
            weights = jnp.exp2((scores - peak) * scale)
            sums[pair] += jnp.sum(weights, axis=-1, keepdims=True)
            first, width = lane_window(ENC_SHIFT + pair * PAIR_SIZE, PAIR_SIZE)
            first += value_base
            values = kv_ref[those, :, first : first + width].reshape(length, width)
            mixes[pair] += jnp.dot(weights.astype(BF16), values, preferred_element_type=F32)
    attn_ref[...] = jnp.zeros_like(attn_ref)
    for pair in range(HEAD_PAIRS):
        first, width = lane_window(ENC_SHIFT + pair * PAIR_SIZE, PAIR_SIZE)
        mixed = mixes[pair] / sums[pair]
        part = attn_ref[:, first : first + width]
        for k in range(2):
            mine = head_column(part.shape, 2 * pair + k, HEAD_SIZE, ENC_SHIFT - first)
            part = jnp.where(mine, mixed[k * ROW_BLOCK : (k + 1) * ROW_BLOCK], part)
        attn_ref[:, first : first + width] = part
    attn = attn_ref[...].astype(BF16)
    attn = jnp.dot(attn, spread_ref[...], preferred_element_type=F32).astype(BF16)
    for copy in weight_copies:
        copy.wait()
    weight = weight_ref[...].reshape(-1, weight_ref.shape[-1])
    projected = jnp.dot(attn, weight, preferred_element_type=F32)
    computed = (residual_ref[...].astype(F32) + projected).astype(BF16)
    slot = lax.broadcasted_iota(jnp.int32, computed.shape, 0)
    enc_out_ref[...] = jnp.where(slot < live_ref[0], computed, jnp.zeros_like(computed))
    out_copy = pltpu.make_async_copy(enc_out_ref, enc_out_hbm, other_sems.at[2])
    out_copy.start()
    normed = layer_norm(computed, norm_gain_ref[...]).astype(BF16)
    bridge_copy.wait()
    bridged = jnp.dot(normed, bridge_ref[...], preferred_element_type=F32) + pe_ref[...]
    dec_normed = layer_norm(bridged.astype(BF16), dec_gain_ref[...]).astype(BF16)
    dec_copy.wait()
    pairs = jnp.dot(dec_normed, dec_weight_ref[...], preferred_element_type=F32)
    vis_ref[...] = pairs.astype(BF16)
    out_copy.wait()


def head_stats(stats, head, peak, summed):
    lane = lax.broadcasted_iota(jnp.int32, stats.shape, 1)
    stats = jnp.where(lane == head, peak, stats)
    return jnp.where(lane == DEC_HEADS + head, summed, stats)


def unit_rows(count, width):
    row = lax.broadcasted_iota(jnp.int32, (count, width), 0)
    column = lax.broadcasted_iota(jnp.int32, (count, width), 1)
    return jnp.where(row == column, 1.0, 0.0).astype(BF16)


def three_parts(numbers):
    high = numbers.astype(BF16).astype(F32)
    middle = (numbers - high).astype(BF16).astype(F32)
    return high, middle, numbers - high - middle


def coded_stats(stats):
    group = 2 * DEC_HEADS
    high, middle, low = three_parts(stats)
    lanes = high + pltpu.roll(middle, group, 1) + pltpu.roll(low, 2 * group, 1)
    return nt_dot(unit_rows(STAT_ROWS, LANES), lanes.astype(BF16)).astype(BF16)


def decoded_stats(coded):
    group = 2 * DEC_HEADS
    widened = coded.astype(F32)
    return widened[:group] + (widened[group : 2 * group] + widened[2 * group :])


def kept_kernel(kept_ref, gain_ref, weight_ref, query_ref, state_ref):
    scale = LOG2_E / math.sqrt(DEC_HEAD_SIZE)
    normed = layer_norm(kept_ref[...], gain_ref[...]).astype(BF16)
    pairs = jnp.dot(normed, weight_ref[...], preferred_element_type=F32).astype(BF16)
    queries = query_ref[...]
    total = jnp.zeros(queries.shape, F32)
    stats = jnp.zeros((queries.shape[0], LANES), F32)
    for h in range(DEC_HEADS):
        mine = head_column(queries.shape, h, DEC_HEAD_SIZE, 0)
        scores = nt_dot(jnp.where(mine, queries, jnp.zeros_like(queries)), pairs[:, :DEC_INNER])
        peak = jnp.max(scores, axis=-1, keepdims=True)
        weights = jnp.exp2((scores - peak) * scale)
        stats = head_stats(stats, h, peak, jnp.sum(weights, axis=-1, keepdims=True))
        mixed = jnp.dot(weights.astype(BF16), pairs[:, DEC_INNER:], preferred_element_type=F32)
        total = jnp.where(mine, mixed, total)
    state_ref[:, :DEC_INNER] = total
    state_ref[:, DEC_INNER:] = stats


def visible_kernel(vis_ref, mask_ref, query_ref, state_ref, out_ref):
    scale = LOG2_E / math.sqrt(DEC_HEAD_SIZE)
    usable = mask_ref[...] > 0.0
    queries = query_ref[...]
    total = jnp.zeros(queries.shape, F32)
    stats = jnp.zeros((queries.shape[0], LANES), F32)
    for h in range(DEC_HEADS):
        place = DEC_INNER + h
        kept_peak = state_ref[:, place : place + 1]
        kept_sum = state_ref[:, place + DEC_HEADS : place + DEC_HEADS + 1]
        mine = head_column(queries.shape, h, DEC_HEAD_SIZE, 0)
        scores = nt_dot(jnp.where(mine, queries, jnp.zeros_like(queries)), vis_ref[:, :DEC_INNER])
        scores = jnp.where(usable, scores, NEG_FILL)
        peak = jnp.maximum(kept_peak, jnp.max(scores, axis=-1, keepdims=True))
        weights = jnp.exp2((scores - peak) * scale)
        fade = jnp.exp2((kept_peak - peak) * scale)
        summed = kept_sum * fade + jnp.sum(weights, axis=-1, keepdims=True)
        stats = head_stats(stats, h, peak, summed)
        mixed = jnp.dot(weights.astype(BF16), vis_ref[:, DEC_INNER:], preferred_element_type=F32)
        total = jnp.where(mine, mixed + fade * state_ref[:, :DEC_INNER], total)
    near = out_ref.shape[0]
    rows = out_ref.shape[1] - STAT_ROWS
    for k in range(near):
        those = slice(k * rows, (k + 1) * rows)
        out_ref[k, :rows] = total[those].astype(BF16)
        out_ref[k, rows:] = jnp.zeros((STAT_ROWS, DEC_INNER), BF16)
        out_ref[k, rows:, :rows] = coded_stats(stats[those])


def finish_kernel(parts_ref, kept_ref, weight_ref, out_ref):
    scale = LOG2_E / math.sqrt(DEC_HEAD_SIZE)
    near = parts_ref.shape[0]
    rows = parts_ref.shape[1] - STAT_ROWS
    stats = [decoded_stats(parts_ref[k, rows:, :rows]) for k in range(near)]
    peak = stats[0]
    for k in range(1, near):
        peak = jnp.maximum(peak, stats[k])
    fades = [jnp.exp2((stats[k] - peak) * scale) for k in range(near)]
    summed = 0.0
    for k in range(near):
        summed += pltpu.roll(fades[k], DEC_HEADS, 0) * stats[k]
    summed = pltpu.roll(summed, DEC_HEADS, 0)
    group = 2 * DEC_HEADS
    row = lax.broadcasted_iota(jnp.int32, (STAT_ROWS, DEC_INNER), 0)
    column = lax.broadcasted_iota(jnp.int32, (STAT_ROWS, DEC_INNER), 1)
    within = row - row // group * group
    over_heads = jnp.where(within == column // DEC_HEAD_SIZE, 1.0, 0.0).astype(BF16)
    turn = unit_rows(rows, rows)
    is_head = lax.broadcasted_iota(jnp.int32, summed.shape, 0) < DEC_HEADS
    total = jnp.zeros((rows, DEC_INNER), F32)
    for k in range(near):
        factor = jnp.where(is_head, fades[k] / summed, 0.0)
        factor = jnp.concatenate(three_parts(factor), axis=0).astype(BF16)
        factor = nt_dot(turn, factor).astype(BF16)
        factor = jnp.dot(factor, over_heads, preferred_element_type=F32)
        total += parts_ref[k, :rows].astype(F32) * factor
    attn = total.astype(BF16)
    projected = jnp.dot(attn, weight_ref[...], preferred_element_type=F32)
    out_ref[...] = (kept_ref[...].astype(F32) + projected).astype(BF16)


def call(kernel, out_shape, *operands, scalars=0, in_hbm=(), out_hbm=(), scratch=()):
    in_vmem = pl.BlockSpec(memory_space=pltpu.VMEM)
    specs = [in_vmem] * len(operands)
    for k in range(scalars):
        specs[k] = pl.BlockSpec(memory_space=pltpu.SMEM)
    for k in in_hbm:
        specs[k] = pl.BlockSpec(memory_space=pl.ANY)
    out_specs = jax.tree.map(lambda _: in_vmem, out_shape)
    for k in out_hbm:
        out_specs = out_specs[:k] + (pl.BlockSpec(memory_space=pl.ANY),) + out_specs[k + 1 :]
    return pl.pallas_call(
        kernel,
        out_shape=out_shape,
        in_specs=specs,
        out_specs=out_specs,
        scratch_shapes=list(scratch),
        compiler_params=pltpu.CompilerParams(vmem_limit_bytes=56 * 1024 * 1024),
    )(*operands)


def body(
    enc_rows,
    vis_count,
    vis_dest,
    vis_pos,
    kept_pos,
    out_weight,
    norm_gain,
    bridge_weight,
    mask_token,
    dec_gain,
    dec_qkv_weight,
    dec_out_weight,
):
    row_block = ROW_BLOCK
    shape_of = jax.ShapeDtypeStruct
    myself = lax.axis_index(SEQ)
    near = lax.axis_size(NEAR)
    far = lax.axis_size(FAR)
    bal_counts = balance_table(vis_count, row_block)
    has_own = vis_count[myself] > 0

    pair_rows = enc_rows[:, ENC_INNER : 3 * ENC_INNER]
    overflow, enc_rows = lax.optimization_barrier((pair_rows[row_block:], enc_rows))
    own_rows = enc_rows[:row_block, ENC_INNER : 3 * ENC_INNER]
    key_value = jnp.where(has_own, own_rows, shifted(overflow, SEQ, 1))
    seq_devices = lax.axis_size(SEQ)
    weight_rows = out_weight.shape[0]
    padded_weight = jnp.pad(out_weight, ((0, WEIGHT_ROWS - weight_rows), (0, 0)))
    packet = jnp.concatenate([key_value, padded_weight], axis=0)
    packets = lax.all_gather(packet, SEQ, axis=0, tiled=True).reshape(seq_devices, -1, packet.shape[1])
    enc_late, kept_pos, _ = lax.optimization_barrier((enc_rows, kept_pos, key_value))

    kept_dev = kept_pos.shape[0]
    kept_all = lax.all_to_all(
        jnp.broadcast_to(kept_pos[None, :], (far, kept_dev)), FAR, 0, 0, tiled=True
    )
    kept_all = kept_all.reshape(-1).astype(F32)

    rest = jnp.concatenate([enc_late[:, :ENC_INNER], enc_late[:, 3 * ENC_INNER :]], axis=1)
    rest = jnp.where(has_own, rest[:row_block], shifted(rest[row_block:], SEQ, 1))
    queries = jnp.pad(rest[:, :ENC_INNER], ((0, 0), (0, ENC_SHIFT)))
    residual = rest[:, ENC_INNER:]

    kept_in = (mask_token.astype(F32)[None, :] + sinusoid(kept_pos)).astype(BF16)
    own_normed = layer_norm(kept_in, dec_gain[None, :]).astype(BF16)
    asking = jnp.dot(
        own_normed, dec_qkv_weight[:, :DEC_INNER], preferred_element_type=F32
    ).astype(BF16)
    asking = lax.all_gather(asking, NEAR, axis=0, tiled=True)
    mask_split = halves_first(mask_token)
    kept_split = (mask_split.astype(F32)[None, :] + split_sinusoid(kept_all)).astype(BF16)
    asked = asking.shape[0]
    kept_state = call(
        kept_kernel,
        shape_of((asked, DEC_INNER + LANES), F32),
        kept_split,
        halves_first(dec_gain)[None, :],
        halves_first(dec_qkv_weight[:, DEC_INNER:]),
        asking,
    )

    packets, kept_state = lax.optimization_barrier((packets, kept_state))

    first_row = jnp.where(has_own, myself * 2 * row_block, (myself - 1) * 2 * row_block + row_block)
    bal_pos = lax.dynamic_slice_in_dim(vis_pos, first_row, row_block)
    within = jnp.arange(row_block, dtype=jnp.int32)
    live = (within[None, :] < bal_counts[:, None]).astype(F32)
    pair_width = 2 * DEC_INNER
    model_width = residual.shape[1]
    enc_out, vis_kv = call(
        encoder_kernel,
        (
            shape_of((row_block, model_width), BF16),
            shape_of((row_block, pair_width), BF16),
        ),
        bal_counts[myself][None],
        packets,
        queries,
        live.reshape(1, -1),
        residual,
        norm_gain[None, :],
        bridge_weight,
        sinusoid(bal_pos),
        dec_gain[None, :],
        dec_qkv_weight[:, DEC_INNER:],
        scalars=1,
        in_hbm=(1, 6, 9),
        out_hbm=(0,),
        scratch=(
            pltpu.VMEM((seq_devices, row_block, 2 * ENC_INNER), BF16),
            pltpu.VMEM((seq_devices, WEIGHT_ROWS, model_width), BF16),
            pltpu.VMEM(bridge_weight.shape, BF16),
            pltpu.VMEM((DEC_WIDTH, pair_width), BF16),
            pltpu.VMEM((ENC_WINDOW, seq_devices * WEIGHT_ROWS), BF16),
            pltpu.VMEM((row_block, ENC_WINDOW), F32),
            pltpu.VMEM((row_block, model_width), BF16),
            pltpu.SemaphoreType.DMA((ENC_COPIES,)),
            pltpu.SemaphoreType.DMA((WEIGHT_COPIES,)),
            pltpu.SemaphoreType.DMA((3,)),
        ),
    )

    vis_all = lax.all_gather(vis_kv, FAR, axis=0, tiled=True)
    live_same = lax.dynamic_index_in_dim(
        live.reshape(-1, near, lax.axis_size("core"), row_block),
        lax.axis_index(NEAR),
        axis=1,
        keepdims=False,
    )
    parts = call(
        visible_kernel,
        shape_of((near, kept_dev + STAT_ROWS, DEC_INNER), BF16),
        vis_all,
        live_same.reshape(1, -1),
        asking,
        kept_state,
    )
    parts = lax.all_to_all(parts, NEAR, 0, 0, tiled=True)
    dec_out = call(
        finish_kernel,
        shape_of((kept_dev, DEC_WIDTH), BF16),
        parts,
        kept_in,
        dec_out_weight,
    )
    return (enc_out, dec_out)


def solution(mesh):
    grid = (mesh.shape["clip"], mesh.shape["seq"] // (2 * NEAR_CHIPS), NEAR_CHIPS, 2)
    finer = Mesh(mesh.devices.reshape(grid), CLIP_SEQ)
    return jax.shard_map(
        body,
        mesh=finer,
        in_specs=(
            P(CLIP_SEQ, None),
            P("clip"),
            P("clip"),
            P("clip"),
            P(CLIP_SEQ),
            P(SEQ, None),
            P(),
            P(),
            P(),
            P(),
            P(),
            P(),
        ),
        out_specs=(P(CLIP_SEQ, None), P(CLIP_SEQ, None)),
        check_vma=False,
    )
```
